32 devices in a mesh: grp: 2 (over y), shard: 16 (over z, x, core).
Axes of the slice: x: 2, y: 2, z: 4, core: 2. Of those that a mesh axis runs over, the one named last changes fastest.
Arguments:
- projections: bfloat16 [3, 4096, 512], P(None, ('grp', 'shard')), may hold values from -6 to 6
- short_taps: float32 [3, 7, 512], replicated, may hold values from -2 to 2
- long_filter: float32 [4096, 512], P(('grp', 'shard')), may hold values from -0.09375 to 0.09375
- skip_gain: float32 [512], replicated, may hold values from 0.5 to 1.5
Outputs:
- output: bfloat16 [4096, 512], P(('grp', 'shard'))
The draws below stay inside these ranges and needn't reach their ends.
All inputs are finite; a program needn't handle non-finite values.
Results may differ from the reference program's by a relative error of at most 0.001.
Values may be sent and summed in bfloat16 or wider, within the bound.
A program may use at most 64 MiB of HBM per device.

```python
import jax
import jax.numpy as jnp
from jax import lax

CH = 512
WIDTH = 7
SEQ = 4096


def block_scale(key, dims, shards, smallest, top_value):
    level = 1.0
    for position, parts in shards:
        heights = jax.random.uniform(jax.random.fold_in(jax.random.fold_in(key, 6), position), (parts,), jnp.float32, smallest / len(shards), top_value / len(shards))
        level = level * jnp.repeat(jnp.exp(heights), dims[position] // parts).reshape((-1,) + (1,) * (len(dims) - 1 - position))
    return level


def bell_draw(rng, shape, scale, limit, split=(), held_as=jnp.bfloat16):
    gain = block_scale(rng, shape, split, -0.22, 0.18) if split else 1.0
    drawn = jax.random.normal(rng, shape, jnp.float32) * scale * gain
    return jnp.minimum(jnp.maximum(drawn, -limit), limit).astype(held_as)


def setup_inputs(seed: int = 0) -> dict:
    streams_of = jax.random.split(jax.random.key(seed), 5)
    projections = bell_draw(streams_of[0], (3, SEQ, CH), 1.0, 6.0, ((1, 32),))
    short_taps = bell_draw(streams_of[1], (3, WIDTH, CH), WIDTH ** -0.5, 2.0, (), jnp.float32)
    long_filter = bell_draw(streams_of[2], (SEQ, CH), SEQ ** -0.5, 0.09375, ((0, 32),), jnp.float32)
    skip_gain = jnp.clip(jax.random.uniform(streams_of[3], (CH,), jnp.float32, 0.5, 1.5), 0.5, 1.5)
    return {"projections": projections, "short_taps": short_taps, "long_filter": long_filter, "skip_gain": skip_gain}


def reference(projections, short_taps, long_filter, skip_gain):
    widened = projections.astype(jnp.float32)
    padded = jnp.pad(widened, ((0, 0), (WIDTH - 1, 0), (0, 0)))
    shortened = short_taps[:, 0, None, :] * padded[:, WIDTH - 1:WIDTH - 1 + SEQ, :]
    for tap_index in range(1, WIDTH):
        shortened = shortened + short_taps[:, tap_index, None, :] * padded[:, WIDTH - 1 - tap_index:WIDTH - 1 - tap_index + SEQ, :]
    query = shortened[0]
    mixed = shortened[1] * shortened[2]
    band_width = min(CH, 64)

    def one_band(pair):
        mixed_band, filt_band = pair
        zeros_band = jnp.zeros_like(mixed_band)
        mixed_spec = jnp.fft.fft(jnp.concatenate([mixed_band, zeros_band], axis=0), axis=0)
        filt_spec = jnp.fft.fft(jnp.concatenate([filt_band, zeros_band], axis=0), axis=0)
        back = jnp.fft.ifft(mixed_spec * filt_spec, axis=0)
        return jnp.real(back)[:SEQ].astype(mixed_band.dtype)

    mixed_bands = mixed.reshape(SEQ, CH // band_width, band_width).transpose(1, 0, 2)
    filt_bands = long_filter.reshape(SEQ, CH // band_width, band_width).transpose(1, 0, 2)
    conv = lax.map(one_band, (mixed_bands, filt_bands)).transpose(1, 0, 2).reshape(SEQ, CH)
    return (query * (conv + skip_gain * mixed)).astype(jnp.bfloat16)
```

```python
import functools
import math

import jax
import jax.numpy as jnp
import numpy as np
from jax import lax
from jax.experimental import pallas as pl
from jax.experimental.pallas import tpu as pltpu
from jax.sharding import PartitionSpec as P

precise = lax.Precision.HIGHEST


def from_behind(block, axis, distance):
    devices = range(lax.axis_size(axis))
    route = [(i - distance, i) for i in devices if i - distance in devices]
    return lax.ppermute(block, axis, route)


def angles_of(first, second, modulus):
    return (first * second % modulus).astype(jnp.float32) * (2.0 * math.pi / modulus)


def per_device(projections, short_taps, long_filter, skip_gain):
    positions = projections.shape[1]
    channels = projections.shape[2]
    taps_count = short_taps.shape[1]
    groups = lax.axis_size("grp")
    shards = lax.axis_size("shard")
    devices = groups * shards
    span_len = 2 * devices
    length = span_len * positions
    slice_len = positions * channels // devices
    device_id = lax.axis_index("grp") * shards + lax.axis_index("shard")
    rim_rows = from_behind(projections[:, positions - (taps_count - 1) :, :], ("grp", "shard"), 1)
    extended = jnp.concatenate([rim_rows, projections], axis=1)
    shortened = short_taps[:, 0, None, :] * extended[
        :, taps_count - 1 : taps_count - 1 + positions, :
    ].astype(jnp.float32)
    for tap_index in range(1, taps_count):
        shortened = shortened + short_taps[:, tap_index, None, :] * extended[
            :, taps_count - 1 - tap_index : taps_count - 1 - tap_index + positions, :
        ].astype(jnp.float32)
    query = shortened[0]
    mixed = shortened[1] * shortened[2]
    mixed_rows = mixed.reshape(groups, shards, slice_len)
    filt_rows = long_filter.reshape(groups, shards, slice_len)
    got_mixed, got_filt = (
        lax.all_to_all(
            lax.all_to_all(mixed_rows, "grp", split_axis=0, concat_axis=0, tiled=True),
            "shard",
            split_axis=1,
            concat_axis=1,
            tiled=True,
        ),
        lax.all_to_all(
            lax.all_to_all(filt_rows, "grp", split_axis=0, concat_axis=0, tiled=True),
            "shard",
            split_axis=1,
            concat_axis=1,
            tiled=True,
        ),
    )
    dev_ids = jnp.arange(devices, dtype=jnp.int32)
    freq_ids = jnp.arange(span_len, dtype=jnp.int32)
    outer = angles_of(freq_ids[:, None], dev_ids[None, :], span_len)
    outer_cos, outer_sin = (jnp.cos(outer), jnp.sin(outer))
    flat_ids = device_id * slice_len + jnp.arange(slice_len, dtype=jnp.int32)
    row_of = flat_ids // channels
    twist = angles_of(freq_ids[:, None], row_of[None, :], length)
    twist_cos, twist_sin = (jnp.cos(twist), jnp.sin(twist))

    def forward_outer(values):
        flat_values = values.reshape(devices, slice_len)
        real = jnp.dot(outer_cos, flat_values, precision=precise)
        imag = -jnp.dot(outer_sin, flat_values, precision=precise)
        turned_re = real * twist_cos + imag * twist_sin
        turned_im = imag * twist_cos - real * twist_sin
        return (
            turned_re.reshape(2, groups, shards, slice_len),
            turned_im.reshape(2, groups, shards, slice_len),
        )

    mixed_re, mixed_im = forward_outer(got_mixed)
    filt_re, filt_im = forward_outer(got_filt)
    mixed_re, mixed_im, filt_re, filt_im = (
        lax.all_to_all(
            lax.all_to_all(mixed_re, "grp", split_axis=1, concat_axis=1, tiled=True),
            "shard",
            split_axis=2,
            concat_axis=2,
            tiled=True,
        ),
        lax.all_to_all(
            lax.all_to_all(mixed_im, "grp", split_axis=1, concat_axis=1, tiled=True),
            "shard",
            split_axis=2,
            concat_axis=2,
            tiled=True,
        ),
        lax.all_to_all(
            lax.all_to_all(filt_re, "grp", split_axis=1, concat_axis=1, tiled=True),
            "shard",
            split_axis=2,
            concat_axis=2,
            tiled=True,
        ),
        lax.all_to_all(
            lax.all_to_all(filt_im, "grp", split_axis=1, concat_axis=1, tiled=True),
            "shard",
            split_axis=2,
            concat_axis=2,
            tiled=True,
        ),
    )
    row_ids = jnp.arange(positions, dtype=jnp.int32)
    inner = angles_of(row_ids[:, None], row_ids[None, :], positions)
    inner_cos, inner_sin = (jnp.cos(inner), jnp.sin(inner))

    def forward_inner(real, imag):
        real = real.reshape(2, positions, channels)
        imag = imag.reshape(2, positions, channels)
        out_re = jnp.einsum("kp,rpc->rkc", inner_cos, real, precision=precise) + jnp.einsum(
            "kp,rpc->rkc", inner_sin, imag, precision=precise
        )
        out_im = jnp.einsum("kp,rpc->rkc", inner_cos, imag, precision=precise) - jnp.einsum(
            "kp,rpc->rkc", inner_sin, real, precision=precise
        )
        return (out_re, out_im)

    spec_mixed_re, spec_mixed_im = forward_inner(mixed_re, mixed_im)
    spec_filt_re, spec_filt_im = forward_inner(filt_re, filt_im)
    prod_re = spec_mixed_re * spec_filt_re - spec_mixed_im * spec_filt_im
    prod_im = spec_mixed_re * spec_filt_im + spec_mixed_im * spec_filt_re
    back_re = jnp.einsum("kp,rkc->rpc", inner_cos, prod_re, precision=precise) - jnp.einsum(
        "kp,rkc->rpc", inner_sin, prod_im, precision=precise
    )
    back_im = jnp.einsum("kp,rkc->rpc", inner_cos, prod_im, precision=precise) + jnp.einsum(
        "kp,rkc->rpc", inner_sin, prod_re, precision=precise
    )
    own_freqs = jnp.arange(2, dtype=jnp.int32) * devices + device_id
    back_twist = angles_of(own_freqs[:, None], row_ids[None, :], length)
    back_cos, back_sin = (jnp.cos(back_twist)[:, :, None], jnp.sin(back_twist)[:, :, None])
    rot_re = (back_re * back_cos - back_im * back_sin).reshape(2, groups, shards, slice_len)
    rot_im = (back_re * back_sin + back_im * back_cos).reshape(2, groups, shards, slice_len)
    rot_re, rot_im = (
        lax.all_to_all(
            lax.all_to_all(rot_re, "grp", split_axis=1, concat_axis=1, tiled=True),
            "shard",
            split_axis=2,
            concat_axis=2,
            tiled=True,
        ),
        lax.all_to_all(
            lax.all_to_all(rot_im, "grp", split_axis=1, concat_axis=1, tiled=True),
            "shard",
            split_axis=2,
            concat_axis=2,
            tiled=True,
        ),
    )
    rot_re = rot_re.reshape(span_len, slice_len)
    rot_im = rot_im.reshape(span_len, slice_len)
    values = (
        jnp.einsum("kd,kf->df", outer_cos, rot_re, precision=precise)
        - jnp.einsum("kd,kf->df", outer_sin, rot_im, precision=precise)
    ) / length
    values = values.reshape(groups, shards, slice_len)
    conv_rows = lax.all_to_all(
        lax.all_to_all(values, "grp", split_axis=0, concat_axis=0, tiled=True),
        "shard",
        split_axis=1,
        concat_axis=1,
        tiled=True,
    )
    conv = conv_rows.reshape(positions, channels)
    return (query * (conv + skip_gain * mixed)).astype(jnp.bfloat16)


MESH = pl.DeviceIdType.MESH
LANES = 128
SUB = 8
HALO = 16
TOGETHER = 4


def turned(value, numerator, denominator):
    numerator %= denominator
    real, imag = value
    eighths, rest = divmod(8 * numerator, denominator)
    if rest == 0:
        half = math.sqrt(0.5)
        if eighths == 0:
            return (real, imag)
        if eighths == 2:
            return (-imag, real)
        if eighths == 4:
            return (-real, -imag)
        if eighths == 6:
            return (imag, -real)
        if eighths == 1:
            return ((real - imag) * half, (real + imag) * half)
        if eighths == 3:
            return ((real + imag) * -half, (real - imag) * half)
        if eighths == 5:
            return ((imag - real) * half, (real + imag) * -half)
        return ((real + imag) * half, (imag - real) * half)
    angle = 2.0 * math.pi * numerator / denominator
    cos, sin = (math.cos(angle), math.sin(angle))
    return (real * cos - imag * sin, real * sin + imag * cos)


def fft(loads, sign):
    count = len(loads)
    if count == 1:
        return [loads[0]()]
    even, odd = (fft(loads[::2], sign), fft(loads[1::2], sign))
    low, high = ([], [])
    for k in range(count // 2):
        moved = turned(odd[k], sign * k, count)
        low.append((even[k][0] + moved[0], even[k][1] + moved[1]))
        high.append((even[k][0] - moved[0], even[k][1] - moved[1]))
    return low + high


def dot3(values, table_hi, table_lo):
    hi = values.astype(jnp.bfloat16)
    lo = (values - hi.astype(jnp.float32)).astype(jnp.bfloat16)
    dot = functools.partial(jnp.dot, preferred_element_type=jnp.float32)
    return dot(hi, table_hi[...]) + (dot(lo, table_hi[...]) + dot(hi, table_lo[...]))


def owner_kernel(
    sizes,
    proj_ref_far,
    taps_ref_far,
    filt_ref_far,
    gain_ref_far,
    fwd_hi_far,
    fwd_lo_far,
    inv_hi_far,
    inv_lo_far,
    twist_cos_far,
    twist_sin_far,
    out_ref,
    proj_ref,
    taps_ref,
    filt_ref,
    gain_ref,
    fwd_hi,
    fwd_lo,
    inv_hi,
    inv_lo,
    twist_cos,
    twist_sin,
    rim,
    ext,
    query,
    direct,
    filt_out,
    pair_out,
    filt_in,
    pair_in,
    mix_in,
    tap_rows,
    tap_columns,
    conv_out,
    conv_in,
    spec_a,
    spec_held,
    spec_g,
    load_sems,
    rim_sems,
    send_sems,
    recv_sems,
):
    groups, shards, positions, channels, taps = sizes
    devices = groups * shards
    owned = channels // devices
    halves = owned // SUB
    per_chunk = LANES // owned
    chunks = channels // LANES
    my_group, my_shard = (lax.axis_index("grp"), lax.axis_index("shard"))
    me = my_group * shards + my_shard

    def partners(act):
        for apart in range(devices - 1, 0, -1):
            group = jnp.bitwise_xor(my_group, apart // shards)
            shard = jnp.bitwise_xor(my_shard, apart % shards)
            act((group, shard), group * shards + shard)

    def place(target):
        return (target // shards, target % shards)

    barrier = pltpu.get_barrier_semaphore()
    partners(
        lambda there, target: pl.semaphore_signal(
            barrier, inc=1, device_id=there, device_id_type=MESH
        )
    )

    def scatter_rows(chunk, turned_block, store):
        for part in range(per_chunk):
            for half in range(halves):
                first = part * owned + half * SUB
                store[half, chunk * per_chunk + part] = turned_block[first : first + SUB, :]

    far = (proj_ref_far, filt_ref_far, taps_ref_far, gain_ref_far, fwd_hi_far, fwd_lo_far)
    far += (inv_hi_far, inv_lo_far, twist_cos_far, twist_sin_far)
    near = (proj_ref, filt_ref, taps_ref, gain_ref, fwd_hi, fwd_lo)
    near += (inv_hi, inv_lo, twist_cos, twist_sin)
    loads = [
        pltpu.make_async_copy(source_ref, here_ref, load_sems.at[which])
        for which, (source_ref, here_ref) in enumerate(zip(far, near))
    ]
    for load in loads:
        load.start()
    for load in loads[:3]:
        load.wait()

    for chunk in range(chunks):
        lanes = slice(chunk * LANES, (chunk + 1) * LANES)
        scatter_rows(chunk, filt_ref[:, lanes].T, filt_out)
        for which in range(3):
            ext[which, chunk, HALO:, :] = proj_ref[which, :, lanes].astype(jnp.float32)
        tap_rows[...] = jnp.zeros_like(tap_rows)
        for pair in range(2):
            block = ext[pair + 1, chunk, HALO:, :].T.astype(jnp.bfloat16)
            for part in range(per_chunk):
                rows = slice(part * owned, (part + 1) * owned)
                pair_out[pair, chunk * per_chunk + part] = block[rows, :]
            tap_rows[pair * HALO : pair * HALO + taps, :] = taps_ref[pair + 1, :, lanes]
        block = tap_rows[...].T
        for part in range(per_chunk):
            tap_columns[chunk * per_chunk + part] = block[part * owned : (part + 1) * owned, :]
    for pair in range(2):
        pair_in[pair, 0] = jnp.zeros((owned, LANES), jnp.bfloat16)

    for load in loads[3:]:
        load.wait()
    pl.semaphore_wait(barrier, devices - 1)

    rim_copy = pltpu.make_async_remote_copy(
        src_ref=proj_ref.at[:, positions - HALO :, :],
        dst_ref=rim,
        send_sem=rim_sems.at[0],
        recv_sem=rim_sems.at[1],
        device_id=place(lax.rem(me + 1, devices)),
        device_id_type=MESH,
    )

    def send_all(source, landing, kind, half, shift=0):
        def send(there, target):
            pltpu.make_async_remote_copy(
                src_ref=source.at[half, target],
                dst_ref=landing.at[half, me + shift],
                send_sem=send_sems.at[kind, half],
                recv_sem=recv_sems.at[kind, half],
                device_id=there,
                device_id_type=MESH,
            ).start()

        partners(send)
        landing[half, me + shift] = source[half, me]

    def wait_all(landing, sems, kind, half):
        others = landing.at[half, pl.ds(0, devices - 1)]
        pltpu.make_async_copy(others, others, sems.at[kind, half]).wait()

    for pair in range(2):
        send_all(pair_out, pair_in, 0, pair, 1)
    for half in range(halves):
        send_all(filt_out, filt_in, 1, half)

    rim_copy.start()

    def transform(landing, half):
        def load(block):
            def get():
                value = landing[half, block]
                angle = 2.0 * math.pi * block / (4 * devices)
                return (value * math.cos(angle), value * math.sin(angle))

            return get

        for k, (real, imag) in enumerate(fft([load(b) for b in range(devices)], 1)):
            cos, sin = (twist_cos[k : k + 1, :], twist_sin[k : k + 1, :])
            rows = slice(k * SUB, (k + 1) * SUB)
            spec_a[rows, :LANES] = real * cos - imag * sin
            spec_a[rows, LANES:] = real * sin + imag * cos
        return dot3(spec_a[...], fwd_hi, fwd_lo)

    for pair in range(2):
        wait_all(pair_in, recv_sems, 0, pair)
    own_taps = tap_columns[me]

    @pl.loop(0, devices // TOGETHER)
    def _(step):
        lane = lax.broadcasted_iota(jnp.int32, (TOGETHER, owned, LANES), 2)

        def convolved(pair):
            before = pair_in[pair, pl.ds(step * TOGETHER, TOGETHER)].astype(jnp.float32)
            block = pair_in[pair, pl.ds(step * TOGETHER + 1, TOGETHER)].astype(jnp.float32)
            total = None
            for tap in range(taps):
                moved = block
                if tap:
                    moved = pltpu.roll(jnp.where(lane >= LANES - tap, before, block), tap, 2)
                column = pair * HALO + tap
                term = own_taps[:, column : column + 1][None] * moved
                total = term if total is None else total + term
            return total

        mixed = convolved(0) * convolved(1)
        for half in range(halves):
            rows = slice(half * SUB, (half + 1) * SUB)
            mix_in[half, pl.ds(step * TOGETHER, TOGETHER)] = mixed[:, rows, :]

    for half in range(halves):
        spec_held[half] = transform(mix_in, half)

    for half in range(halves):
        wait_all(filt_in, recv_sems, 1, half)
        far_spec = transform(filt_in, half)
        far_re, far_im = (far_spec[:, :LANES], far_spec[:, LANES:])
        held_re, held_im = (spec_held[half, :, :LANES], spec_held[half, :, LANES:])
        spec_a[:, :LANES] = far_re * held_re - far_im * held_im
        spec_a[:, LANES:] = far_re * held_im + far_im * held_re
        spec_g[...] = dot3(spec_a[...], inv_hi, inv_lo)

        def load(k):
            def get():
                rows = slice(k * SUB, (k + 1) * SUB)
                real, imag = (spec_g[rows, :LANES], spec_g[rows, LANES:])
                cos, sin = (twist_cos[k : k + 1, :], twist_sin[k : k + 1, :])
                return (real * cos + imag * sin, imag * cos - real * sin)

            return get

        for block, (real, imag) in enumerate(fft([load(k) for k in range(devices)], -1)):
            angle = 2.0 * math.pi * block / (4 * devices)
            conv_out[half, block] = real * math.cos(angle) + imag * math.sin(angle)
        send_all(conv_out, conv_in, 2, half)

    rim_copy.wait()
    keep = jnp.where(me > 0, 1.0, 0.0).astype(jnp.float32)
    for chunk in range(chunks):
        lanes = slice(chunk * LANES, (chunk + 1) * LANES)
        for which in range(3):
            ext[which, chunk, :HALO, :] = rim[which, :, lanes].astype(jnp.float32) * keep

    def shortened(which, chunk):
        lanes = slice(chunk * LANES, (chunk + 1) * LANES)
        total = None
        for tap in range(taps):
            term = taps_ref[which, tap : tap + 1, lanes] * ext[
                which, chunk, HALO - tap : HALO - tap + positions, :
            ]
            total = term if total is None else total + term
        return total

    for chunk in range(chunks):
        lanes = slice(chunk * LANES, (chunk + 1) * LANES)
        query[chunk] = shortened(0, chunk)
        direct[chunk] = shortened(1, chunk) * shortened(2, chunk) * gain_ref[:, lanes]

    for half in range(halves):
        wait_all(conv_in, recv_sems, 2, half)
    for chunk in range(chunks):
        lanes = slice(chunk * LANES, (chunk + 1) * LANES)
        pieces = [
            conv_in[half, chunk * per_chunk + part]
            for part in range(per_chunk)
            for half in range(halves)
        ]
        conv = jnp.concatenate(pieces, axis=0).T
        out_ref[:, lanes] = (query[chunk] * (conv + direct[chunk])).astype(out_ref.dtype)
    for pair in range(2):
        wait_all(pair_in, send_sems, 0, pair)
    for half in range(halves):
        wait_all(filt_out, send_sems, 1, half)
        wait_all(conv_out, send_sems, 2, half)


def split_table(table):
    hi = table.astype(jnp.bfloat16)
    lo = (table - hi.astype(np.float64)).astype(jnp.bfloat16)
    return hi, lo


def tables(devices, positions):
    p = np.arange(positions, dtype=np.float64)
    angle = 2.0 * np.pi * ((p[:, None] * p[None, :]) % positions) / positions
    cos, sin = (np.cos(angle), np.sin(angle))
    forward = np.block([[cos, sin], [-sin, cos]])
    backward = np.block([[cos, -sin], [sin, cos]]) / (devices * positions)
    k = np.arange(devices, dtype=np.float64)
    twist = 2.0 * np.pi * (k[:, None] + 0.25) * p[None, :] / (devices * positions)
    return (
        *split_table(forward),
        *split_table(backward),
        np.cos(twist).astype(np.float32),
        np.sin(twist).astype(np.float32),
    )


def owned_channels(consts, groups, shards, projections, short_taps, long_filter, skip_gain):
    _, positions, channels = projections.shape
    devices = groups * shards
    owned = channels // devices
    halves = owned // SUB
    chunks = channels // LANES
    sizes = (groups, shards, positions, channels, short_taps.shape[1])
    f32, bf16 = (jnp.float32, jnp.bfloat16)
    operands = (projections, short_taps, long_filter, skip_gain.reshape(1, channels), *consts)
    slabs = pltpu.VMEM((halves, devices, SUB, LANES), f32)
    vmem = pl.BlockSpec(memory_space=pltpu.VMEM)
    return pl.pallas_call(
        functools.partial(owner_kernel, sizes),
        out_shape=jax.ShapeDtypeStruct((positions, channels), bf16),
        in_specs=[pl.BlockSpec(memory_space=pl.ANY)] * (4 + len(consts)),
        out_specs=vmem,
        scratch_shapes=[
            *(pltpu.VMEM(operand.shape, operand.dtype) for operand in operands),
            pltpu.VMEM((3, HALO, channels), bf16),
            pltpu.VMEM((3, chunks, HALO + positions, LANES), f32),
            pltpu.VMEM((chunks, positions, LANES), f32),
            pltpu.VMEM((chunks, positions, LANES), f32),
            slabs,
            pltpu.VMEM((2, devices, owned, LANES), bf16),
            slabs,
            pltpu.VMEM((2, devices + 1, owned, LANES), bf16),
            slabs,
            pltpu.VMEM((LANES, LANES), f32),
            pltpu.VMEM((devices, owned, LANES), f32),
            slabs,
            slabs,
            pltpu.VMEM((devices * SUB, 2 * LANES), f32),
            pltpu.VMEM((halves, devices * SUB, 2 * LANES), f32),
            pltpu.VMEM((devices * SUB, 2 * LANES), f32),
            pltpu.SemaphoreType.DMA((len(operands),)),
            pltpu.SemaphoreType.DMA((2,)),
            pltpu.SemaphoreType.DMA((3, max(halves, 2))),
            pltpu.SemaphoreType.DMA((3, max(halves, 2))),
        ],
        compiler_params=pltpu.CompilerParams(collective_id=0, has_side_effects=True, vmem_limit_bytes=16*1024*1024),
    )(*(pltpu.with_memory_space_constraint(o, pltpu.HBM) for o in operands))


def on_device(groups, shards, projections, short_taps, long_filter, skip_gain):
    _, positions, channels = projections.shape
    devices = groups * shards
    fits = (
        positions == LANES
        and channels % LANES == 0
        and channels % (SUB * devices) == 0
        and LANES % (channels // devices) == 0
        and devices & (devices - 1) == 0
        and (channels // devices) % 16 == 0
        and devices % TOGETHER == 0
        and short_taps.shape[1] <= HALO
    )
    if not fits:
        return per_device(projections, short_taps, long_filter, skip_gain)
    consts = tables(devices, positions)
    return owned_channels(consts, groups, shards, projections, short_taps, long_filter, skip_gain)


def solution(mesh):
    placed = (P(None, ("grp", "shard"), None), P(), P(("grp", "shard"), None), P())
    body = functools.partial(on_device, mesh.shape["grp"], mesh.shape["shard"])
    return jax.shard_map(
        body, mesh=mesh, in_specs=placed, out_specs=P(("grp", "shard"), None), check_vma=False
    )
```

```python
import functools
import math

import jax
import jax.numpy as jnp
import numpy as np
from jax import lax
from jax.experimental import pallas as pl
from jax.experimental.pallas import tpu as pltpu
from jax.sharding import PartitionSpec as P

precise = lax.Precision.HIGHEST


def from_behind(block, axis, distance):
    devices = range(lax.axis_size(axis))
    route = [(i - distance, i) for i in devices if i - distance in devices]
    return lax.ppermute(block, axis, route)


def angles_of(first, second, modulus):
    return (first * second % modulus).astype(jnp.float32) * (2.0 * math.pi / modulus)


def per_device(projections, short_taps, long_filter, skip_gain):
    positions = projections.shape[1]
    channels = projections.shape[2]
    taps_count = short_taps.shape[1]
    groups = lax.axis_size("grp")
    shards = lax.axis_size("shard")
    devices = groups * shards
    span_len = 2 * devices
    length = span_len * positions
    slice_len = positions * channels // devices
    device_id = lax.axis_index("grp") * shards + lax.axis_index("shard")
    rim_rows = from_behind(projections[:, positions - (taps_count - 1) :, :], ("grp", "shard"), 1)
    extended = jnp.concatenate([rim_rows, projections], axis=1)
    shortened = short_taps[:, 0, None, :] * extended[
        :, taps_count - 1 : taps_count - 1 + positions, :
    ].astype(jnp.float32)
    for tap_index in range(1, taps_count):
        shortened = shortened + short_taps[:, tap_index, None, :] * extended[
            :, taps_count - 1 - tap_index : taps_count - 1 - tap_index + positions, :
        ].astype(jnp.float32)
    query = shortened[0]
    mixed = shortened[1] * shortened[2]
    mixed_rows = mixed.reshape(groups, shards, slice_len)
    filt_rows = long_filter.reshape(groups, shards, slice_len)
    got_mixed, got_filt = (
        lax.all_to_all(
            lax.all_to_all(mixed_rows, "grp", split_axis=0, concat_axis=0, tiled=True),
            "shard",
            split_axis=1,
            concat_axis=1,
            tiled=True,
        ),
        lax.all_to_all(
            lax.all_to_all(filt_rows, "grp", split_axis=0, concat_axis=0, tiled=True),
            "shard",
            split_axis=1,
            concat_axis=1,
            tiled=True,
        ),
    )
    dev_ids = jnp.arange(devices, dtype=jnp.int32)
    freq_ids = jnp.arange(span_len, dtype=jnp.int32)
    outer = angles_of(freq_ids[:, None], dev_ids[None, :], span_len)
    outer_cos, outer_sin = (jnp.cos(outer), jnp.sin(outer))
    flat_ids = device_id * slice_len + jnp.arange(slice_len, dtype=jnp.int32)
    row_of = flat_ids // channels
    twist = angles_of(freq_ids[:, None], row_of[None, :], length)
    twist_cos, twist_sin = (jnp.cos(twist), jnp.sin(twist))

    def forward_outer(values):
        flat_values = values.reshape(devices, slice_len)
        real = jnp.dot(outer_cos, flat_values, precision=precise)
        imag = -jnp.dot(outer_sin, flat_values, precision=precise)
        turned_re = real * twist_cos + imag * twist_sin
        turned_im = imag * twist_cos - real * twist_sin
        return (
            turned_re.reshape(2, groups, shards, slice_len),
            turned_im.reshape(2, groups, shards, slice_len),
        )

    mixed_re, mixed_im = forward_outer(got_mixed)
    filt_re, filt_im = forward_outer(got_filt)
    mixed_re, mixed_im, filt_re, filt_im = (
        lax.all_to_all(
            lax.all_to_all(mixed_re, "grp", split_axis=1, concat_axis=1, tiled=True),
            "shard",
            split_axis=2,
            concat_axis=2,
            tiled=True,
        ),
        lax.all_to_all(
            lax.all_to_all(mixed_im, "grp", split_axis=1, concat_axis=1, tiled=True),
            "shard",
            split_axis=2,
            concat_axis=2,
            tiled=True,
        ),
        lax.all_to_all(
            lax.all_to_all(filt_re, "grp", split_axis=1, concat_axis=1, tiled=True),
            "shard",
            split_axis=2,
            concat_axis=2,
            tiled=True,
        ),
        lax.all_to_all(
            lax.all_to_all(filt_im, "grp", split_axis=1, concat_axis=1, tiled=True),
            "shard",
            split_axis=2,
            concat_axis=2,
            tiled=True,
        ),
    )
    row_ids = jnp.arange(positions, dtype=jnp.int32)
    inner = angles_of(row_ids[:, None], row_ids[None, :], positions)
    inner_cos, inner_sin = (jnp.cos(inner), jnp.sin(inner))

    def forward_inner(real, imag):
        real = real.reshape(2, positions, channels)
        imag = imag.reshape(2, positions, channels)
        out_re = jnp.einsum("kp,rpc->rkc", inner_cos, real, precision=precise) + jnp.einsum(
            "kp,rpc->rkc", inner_sin, imag, precision=precise
        )
        out_im = jnp.einsum("kp,rpc->rkc", inner_cos, imag, precision=precise) - jnp.einsum(
            "kp,rpc->rkc", inner_sin, real, precision=precise
        )
        return (out_re, out_im)

    spec_mixed_re, spec_mixed_im = forward_inner(mixed_re, mixed_im)
    spec_filt_re, spec_filt_im = forward_inner(filt_re, filt_im)
    prod_re = spec_mixed_re * spec_filt_re - spec_mixed_im * spec_filt_im
    prod_im = spec_mixed_re * spec_filt_im + spec_mixed_im * spec_filt_re
    back_re = jnp.einsum("kp,rkc->rpc", inner_cos, prod_re, precision=precise) - jnp.einsum(
        "kp,rkc->rpc", inner_sin, prod_im, precision=precise
    )
    back_im = jnp.einsum("kp,rkc->rpc", inner_cos, prod_im, precision=precise) + jnp.einsum(
        "kp,rkc->rpc", inner_sin, prod_re, precision=precise
    )
    own_freqs = jnp.arange(2, dtype=jnp.int32) * devices + device_id
    back_twist = angles_of(own_freqs[:, None], row_ids[None, :], length)
    back_cos, back_sin = (jnp.cos(back_twist)[:, :, None], jnp.sin(back_twist)[:, :, None])
    rot_re = (back_re * back_cos - back_im * back_sin).reshape(2, groups, shards, slice_len)
    rot_im = (back_re * back_sin + back_im * back_cos).reshape(2, groups, shards, slice_len)
    rot_re, rot_im = (
        lax.all_to_all(
            lax.all_to_all(rot_re, "grp", split_axis=1, concat_axis=1, tiled=True),
            "shard",
            split_axis=2,
            concat_axis=2,
            tiled=True,
        ),
        lax.all_to_all(
            lax.all_to_all(rot_im, "grp", split_axis=1, concat_axis=1, tiled=True),
            "shard",
            split_axis=2,
            concat_axis=2,
            tiled=True,
        ),
    )
    rot_re = rot_re.reshape(span_len, slice_len)
    rot_im = rot_im.reshape(span_len, slice_len)
    values = (
        jnp.einsum("kd,kf->df", outer_cos, rot_re, precision=precise)
        - jnp.einsum("kd,kf->df", outer_sin, rot_im, precision=precise)
    ) / length
    values = values.reshape(groups, shards, slice_len)
    conv_rows = lax.all_to_all(
        lax.all_to_all(values, "grp", split_axis=0, concat_axis=0, tiled=True),
        "shard",
        split_axis=1,
        concat_axis=1,
        tiled=True,
    )
    conv = conv_rows.reshape(positions, channels)
    return (query * (conv + skip_gain * mixed)).astype(jnp.bfloat16)


MESH = pl.DeviceIdType.MESH
LANES = 128
SUB = 8
HALO = 8
REACH = 250.0
FAINT = 1e-30
RIMS = ((1, 2), (0, 0))


def turned(value, numerator, denominator):
    numerator %= denominator
    real, imag = value
    eighths, rest = divmod(8 * numerator, denominator)
    if rest == 0:
        half = math.sqrt(0.5)
        if eighths == 0:
            return (real, imag)
        if eighths == 2:
            return (-imag, real)
        if eighths == 4:
            return (-real, -imag)
        if eighths == 6:
            return (imag, -real)
        if eighths == 1:
            return ((real - imag) * half, (real + imag) * half)
        if eighths == 3:
            return ((real + imag) * -half, (real - imag) * half)
        if eighths == 5:
            return ((imag - real) * half, (real + imag) * -half)
        return ((real + imag) * half, (imag - real) * half)
    angle = 2.0 * math.pi * numerator / denominator
    cos, sin = (math.cos(angle), math.sin(angle))
    return (real * cos - imag * sin, real * sin + imag * cos)


def fft(loads, sign):
    count = len(loads)
    if count == 1:
        return [loads[0]()]
    even, odd = (fft(loads[::2], sign), fft(loads[1::2], sign))
    low, high = ([], [])
    for k in range(count // 2):
        moved = turned(odd[k], sign * k, count)
        low.append((even[k][0] + moved[0], even[k][1] + moved[1]))
        high.append((even[k][0] - moved[0], even[k][1] - moved[1]))
    return low + high


def dot3(values, table_hi, table_lo):
    hi = values.astype(jnp.bfloat16)
    lo = (values - hi.astype(jnp.float32)).astype(jnp.bfloat16)
    dot = functools.partial(jnp.dot, preferred_element_type=jnp.float32)
    return dot(hi, table_hi[...]) + (dot(lo, table_hi[...]) + dot(hi, table_lo[...]))


def encoded(scaled):
    magnitude = jnp.exp2(jnp.abs(scaled) - REACH / 2)
    return jnp.where(scaled < 0, -magnitude, magnitude)


def decoded(code):
    wide = code.astype(jnp.float32)
    magnitude = jnp.log2(jnp.abs(wide)) + REACH / 2
    return jnp.where(wide < 0, -magnitude, magnitude)


def owner_kernel(
    sizes,
    proj_ref_far,
    taps_ref_far,
    filt_ref_far,
    gain_ref_far,
    fwd_hi_far,
    fwd_lo_far,
    inv_hi_far,
    inv_lo_far,
    twist_cos_far,
    twist_sin_far,
    out_ref,
    proj_ref,
    taps_ref,
    filt_ref,
    gain_ref,
    fwd_hi,
    fwd_lo,
    inv_hi,
    inv_lo,
    twist_cos,
    twist_sin,
    rim_out,
    rim_in,
    ext,
    query,
    mixed,
    filt_out,
    mix_out,
    conv_out,
    filt_in,
    mix_in,
    conv_in,
    mix_top,
    mix_tops,
    conv_top,
    conv_tops,
    columns,
    blocks,
    spec_a,
    spec_held,
    spec_g,
    load_sems,
    rim_sems,
    send_sems,
    recv_sems,
):
    groups, shards, positions, channels, taps = sizes
    devices = groups * shards
    owned = channels // devices
    halves = owned // SUB
    per_chunk = LANES // owned
    chunks = channels // LANES
    bound = 6.0 / math.sqrt(devices * positions)
    my_group, my_shard = (lax.axis_index("grp"), lax.axis_index("shard"))
    me = my_group * shards + my_shard
    first_lane = lax.rem(me, per_chunk) * owned

    def partners(act):
        for apart in range(devices - 1, 0, -1):
            group = jnp.bitwise_xor(my_group, apart // shards)
            shard = jnp.bitwise_xor(my_shard, apart % shards)
            act((group, shard), group * shards + shard)

    def place(target):
        return (target // shards, target % shards)

    barrier = pltpu.get_barrier_semaphore()
    partners(
        lambda there, target: pl.semaphore_signal(
            barrier, inc=1, device_id=there, device_id_type=MESH
        )
    )

    far = (filt_ref_far, proj_ref_far, taps_ref_far, gain_ref_far, fwd_hi_far, fwd_lo_far)
    far += (inv_hi_far, inv_lo_far, twist_cos_far, twist_sin_far)
    near = (filt_ref, proj_ref, taps_ref, gain_ref, fwd_hi, fwd_lo)
    near += (inv_hi, inv_lo, twist_cos, twist_sin)
    loads = [
        pltpu.make_async_copy(source_ref, here_ref, load_sems.at[which])
        for which, (source_ref, here_ref) in enumerate(zip(far, near))
    ]
    for load in loads:
        load.start()

    def spread(chunk, block, store):
        turned_block = block.T.astype(jnp.bfloat16)
        for part in range(per_chunk):
            store[chunk * per_chunk + part] = turned_block[part * owned : (part + 1) * owned, :]

    loads[0].wait()
    for chunk in range(chunks):
        lanes = slice(chunk * LANES, (chunk + 1) * LANES)
        spread(chunk, encoded(filt_ref[:, lanes] * (REACH / bound)), filt_out)
    loads[1].wait()
    last = slice(positions - 16, positions)
    for pair in range(2):
        tails = [
            proj_ref[which, last, :].astype(jnp.float32)[8:]
            for which in RIMS[pair]
        ]
        rim_out[pair] = jnp.concatenate(tails, axis=0).astype(jnp.bfloat16)
    pl.semaphore_wait(barrier, devices - 1)

    rim_copies = [
        pltpu.make_async_remote_copy(
            src_ref=rim_out.at[pair],
            dst_ref=rim_in.at[pair],
            send_sem=rim_sems.at[0, pair],
            recv_sem=rim_sems.at[1, pair],
            device_id=place(lax.rem(me + 1, devices)),
            device_id_type=MESH,
        )
        for pair in range(2)
    ]

    def send_all(kind, source, landing, index=lambda target: target):
        def send(there, target):
            pltpu.make_async_remote_copy(
                src_ref=source.at[index(target)],
                dst_ref=landing.at[me],
                send_sem=send_sems.at[kind],
                recv_sem=recv_sems.at[kind],
                device_id=there,
                device_id_type=MESH,
            ).start()

        partners(send)
        landing[me] = source[index(me)]

    def wait_all(kind, landing, sems):
        others = landing.at[pl.ds(0, devices - 1)]
        pltpu.make_async_copy(others, others, sems.at[kind]).wait()

    for rim_copy in rim_copies:
        rim_copy.start()
    send_all(0, filt_out, filt_in)

    for load in loads[2:]:
        load.wait()

    def shortened(which, chunk, begin, end):
        lanes = slice(chunk * LANES, (chunk + 1) * LANES)
        total = None
        for tap in range(taps):
            term = taps_ref[which, tap : tap + 1, lanes] * ext[
                which, chunk, HALO + begin - tap : HALO + end - tap, :
            ]
            total = term if total is None else total + term
        return total

    for chunk in range(chunks):
        lanes = slice(chunk * LANES, (chunk + 1) * LANES)
        for which in range(3):
            ext[which, chunk, HALO:, :] = proj_ref[which, :, lanes].astype(jnp.float32)
        mixed[chunk, HALO:, :] = shortened(1, chunk, HALO, positions) * shortened(
            2, chunk, HALO, positions
        )
    for rim_copy in rim_copies:
        rim_copy.wait()
    keep = jnp.where(me > 0, 1.0, 0.0).astype(jnp.float32)
    for chunk in range(chunks):
        lanes = slice(chunk * LANES, (chunk + 1) * LANES)
        for which in range(3):
            pair = 0 if which in RIMS[0] else 1
            part = RIMS[pair].index(which)
            tail = rim_in[pair, :, lanes].astype(jnp.float32)[part * 8 : part * 8 + 8]
            ext[which, chunk, HALO - 8 : HALO, :] = tail * keep
        mixed[chunk, :HALO, :] = shortened(1, chunk, 0, HALO) * shortened(2, chunk, 0, HALO)
        block = mixed[chunk]
        top = jnp.maximum(jnp.max(jnp.abs(block), axis=0, keepdims=True), FAINT)
        mix_top[chunk] = top * (1.0 / REACH)
        spread(chunk, encoded(block * (REACH / top)), mix_out)
    send_all(1, mix_top, mix_tops, lambda target: target // per_chunk)
    send_all(2, mix_out, mix_in)

    for chunk in range(chunks):
        lanes = slice(chunk * LANES, (chunk + 1) * LANES)
        query[chunk] = shortened(0, chunk, 0, positions)
        mixed[chunk] = mixed[chunk] * gain_ref[:, lanes]

    def transform(half, level):
        def load(block):
            def get():
                value = blocks[half, block]
                angle = 2.0 * math.pi * block / (4 * devices)
                return (value * (level * math.cos(angle)), value * (level * math.sin(angle)))

            return get

        for k, (real, imag) in enumerate(fft([load(b) for b in range(devices)], 1)):
            cos, sin = (twist_cos[k : k + 1, :], twist_sin[k : k + 1, :])
            rows = slice(k * SUB, (k + 1) * SUB)
            spec_a[rows, :LANES] = real * cos - imag * sin
            spec_a[rows, LANES:] = real * sin + imag * cos
        return dot3(spec_a[...], fwd_hi, fwd_lo)

    wait_all(0, filt_in, recv_sems)
    for block in range(devices):
        value = decoded(filt_in[block])
        for half in range(halves):
            blocks[half, block] = value[half * SUB : (half + 1) * SUB, :]
    for half in range(halves):
        spec_held[half] = transform(half, bound / REACH)

    wait_all(1, mix_tops, recv_sems)
    columns[...] = jnp.zeros_like(columns)
    columns[:devices, :] = mix_tops[:, 0, :]
    columns[...] = columns[...].T
    own_tops = columns[pl.ds(pl.multiple_of(first_lane, owned), owned), :]
    wait_all(2, mix_in, recv_sems)
    for block in range(devices):
        value = decoded(mix_in[block]) * own_tops[:, block : block + 1]
        for half in range(halves):
            blocks[half, block] = value[half * SUB : (half + 1) * SUB, :]

    tops = []
    for half in range(halves):
        far_spec = transform(half, 1.0)
        far_re, far_im = (far_spec[:, :LANES], far_spec[:, LANES:])
        held_re, held_im = (spec_held[half, :, :LANES], spec_held[half, :, LANES:])
        spec_a[:, :LANES] = far_re * held_re - far_im * held_im
        spec_a[:, LANES:] = far_re * held_im + far_im * held_re
        spec_g[...] = dot3(spec_a[...], inv_hi, inv_lo)

        def load(k):
            def get():
                rows = slice(k * SUB, (k + 1) * SUB)
                real, imag = (spec_g[rows, :LANES], spec_g[rows, LANES:])
                cos, sin = (twist_cos[k : k + 1, :], twist_sin[k : k + 1, :])
                return (real * cos + imag * sin, imag * cos - real * sin)

            return get

        top = None
        for block, (real, imag) in enumerate(fft([load(k) for k in range(devices)], -1)):
            angle = 2.0 * math.pi * block / (4 * devices)
            value = real * math.cos(angle) + imag * math.sin(angle)
            blocks[half, block] = value
            top = jnp.abs(value) if top is None else jnp.maximum(top, jnp.abs(value))
        tops.append(jnp.maximum(jnp.max(top, axis=1, keepdims=True), FAINT))
    ratios = [REACH / top for top in tops]
    for block in range(devices):
        value = jnp.concatenate([blocks[half, block] * ratios[half] for half in range(halves)], axis=0)
        conv_out[block] = encoded(value).astype(jnp.bfloat16)
    row = lax.broadcasted_iota(jnp.int32, (owned, LANES), 0) + first_lane
    lane = lax.broadcasted_iota(jnp.int32, (owned, LANES), 1)
    top = jnp.concatenate(tops, axis=0) * (1.0 / REACH)
    conv_top[0] = jnp.sum(jnp.where(row == lane, top, 0.0), axis=0, keepdims=True)
    send_all(3, conv_out, conv_in)
    send_all(4, conv_top, conv_tops, lambda target: 0)

    wait_all(4, conv_tops, recv_sems)
    wait_all(3, conv_in, recv_sems)
    for chunk in range(chunks):
        lanes = slice(chunk * LANES, (chunk + 1) * LANES)
        owners = slice(chunk * per_chunk, (chunk + 1) * per_chunk)
        top = jnp.sum(conv_tops[owners, 0, :], axis=0, keepdims=True)
        conv = decoded(conv_in[owners].reshape(LANES, LANES)).T * top
        out_ref[:, lanes] = (query[chunk] * (conv + mixed[chunk])).astype(out_ref.dtype)
    wait_all(0, filt_out, send_sems)
    wait_all(1, mix_tops, send_sems)
    wait_all(2, mix_out, send_sems)
    wait_all(3, conv_out, send_sems)
    wait_all(4, conv_tops, send_sems)


def split_table(table):
    hi = table.astype(jnp.bfloat16)
    lo = (table - hi.astype(np.float64)).astype(jnp.bfloat16)
    return hi, lo


def tables(devices, positions):
    p = np.arange(positions, dtype=np.float64)
    angle = 2.0 * np.pi * ((p[:, None] * p[None, :]) % positions) / positions
    cos, sin = (np.cos(angle), np.sin(angle))
    forward = np.block([[cos, sin], [-sin, cos]])
    backward = np.block([[cos, -sin], [sin, cos]]) / (devices * positions)
    k = np.arange(devices, dtype=np.float64)
    twist = 2.0 * np.pi * (k[:, None] + 0.25) * p[None, :] / (devices * positions)
    return (
        *split_table(forward),
        *split_table(backward),
        np.cos(twist).astype(np.float32),
        np.sin(twist).astype(np.float32),
    )


def owned_channels(consts, groups, shards, projections, short_taps, long_filter, skip_gain):
    _, positions, channels = projections.shape
    devices = groups * shards
    owned = channels // devices
    halves = owned // SUB
    chunks = channels // LANES
    sizes = (groups, shards, positions, channels, short_taps.shape[1])
    f32, bf16 = (jnp.float32, jnp.bfloat16)
    operands = (projections, short_taps, long_filter, skip_gain.reshape(1, channels), *consts)
    slabs = pltpu.VMEM((devices, owned, LANES), bf16)
    vmem = pl.BlockSpec(memory_space=pltpu.VMEM)
    return pl.pallas_call(
        functools.partial(owner_kernel, sizes),
        out_shape=jax.ShapeDtypeStruct((positions, channels), bf16),
        in_specs=[pl.BlockSpec(memory_space=pl.ANY)] * (4 + len(consts)),
        out_specs=vmem,
        scratch_shapes=[
            *(pltpu.VMEM(operand.shape, operand.dtype) for operand in operands),
            pltpu.VMEM((2, 16, channels), bf16),
            pltpu.VMEM((2, 16, channels), bf16),
            pltpu.VMEM((3, chunks, HALO + positions, LANES), f32),
            pltpu.VMEM((chunks, positions, LANES), f32),
            pltpu.VMEM((chunks, positions, LANES), f32),
            *(slabs for _ in range(6)),
            pltpu.VMEM((chunks, 1, LANES), f32),
            pltpu.VMEM((devices, 1, LANES), f32),
            pltpu.VMEM((1, 1, LANES), f32),
            pltpu.VMEM((devices, 1, LANES), f32),
            pltpu.VMEM((LANES, LANES), f32),
            pltpu.VMEM((halves, devices, SUB, LANES), f32),
            pltpu.VMEM((devices * SUB, 2 * LANES), f32),
            pltpu.VMEM((halves, devices * SUB, 2 * LANES), f32),
            pltpu.VMEM((devices * SUB, 2 * LANES), f32),
            pltpu.SemaphoreType.DMA((len(operands),)),
            pltpu.SemaphoreType.DMA((2, 2)),
            pltpu.SemaphoreType.DMA((5,)),
            pltpu.SemaphoreType.DMA((5,)),
        ],
        compiler_params=pltpu.CompilerParams(collective_id=0, has_side_effects=True, vmem_limit_bytes=16*1024*1024),
    )(*(pltpu.with_memory_space_constraint(o, pltpu.HBM) for o in operands))


def on_device(groups, shards, projections, short_taps, long_filter, skip_gain):
    _, positions, channels = projections.shape
    devices = groups * shards
    fits = (
        positions == LANES
        and channels % LANES == 0
        and channels % (SUB * devices) == 0
        and LANES % (channels // devices) == 0
        and devices & (devices - 1) == 0
        and (channels // devices) % 16 == 0
        and devices <= LANES
        and short_taps.shape[1] <= HALO + 1
    )
    if not fits:
        return per_device(projections, short_taps, long_filter, skip_gain)
    consts = tables(devices, positions)
    return owned_channels(consts, groups, shards, projections, short_taps, long_filter, skip_gain)


def solution(mesh):
    placed = (P(None, ("grp", "shard"), None), P(), P(("grp", "shard"), None), P())
    body = functools.partial(on_device, mesh.shape["grp"], mesh.shape["shard"])
    return jax.shard_map(
        body, mesh=mesh, in_specs=placed, out_specs=P(("grp", "shard"), None), check_vma=False
    )
```

```python
import functools
import math

import jax
import jax.numpy as jnp
import numpy as np
from jax import lax
from jax.experimental import pallas as pl
from jax.experimental.pallas import tpu as pltpu
from jax.sharding import PartitionSpec as P

precise = lax.Precision.HIGHEST


def from_behind(block, axis, distance):
    devices = range(lax.axis_size(axis))
    route = [(i - distance, i) for i in devices if i - distance in devices]
    return lax.ppermute(block, axis, route)


def angles_of(first, second, modulus):
    return (first * second % modulus).astype(jnp.float32) * (2.0 * math.pi / modulus)


def per_device(projections, short_taps, long_filter, skip_gain):
    positions = projections.shape[1]
    channels = projections.shape[2]
    taps_count = short_taps.shape[1]
    groups = lax.axis_size("grp")
    shards = lax.axis_size("shard")
    devices = groups * shards
    span_len = 2 * devices
    length = span_len * positions
    slice_len = positions * channels // devices
    device_id = lax.axis_index("grp") * shards + lax.axis_index("shard")
    rim_rows = from_behind(projections[:, positions - (taps_count - 1) :, :], ("grp", "shard"), 1)
    extended = jnp.concatenate([rim_rows, projections], axis=1)
    shortened = short_taps[:, 0, None, :] * extended[
        :, taps_count - 1 : taps_count - 1 + positions, :
    ].astype(jnp.float32)
    for tap_index in range(1, taps_count):
        shortened = shortened + short_taps[:, tap_index, None, :] * extended[
            :, taps_count - 1 - tap_index : taps_count - 1 - tap_index + positions, :
        ].astype(jnp.float32)
    query = shortened[0]
    mixed = shortened[1] * shortened[2]
    mixed_rows = mixed.reshape(groups, shards, slice_len)
    filt_rows = long_filter.reshape(groups, shards, slice_len)
    got_mixed, got_filt = (
        lax.all_to_all(
            lax.all_to_all(mixed_rows, "grp", split_axis=0, concat_axis=0, tiled=True),
            "shard",
            split_axis=1,
            concat_axis=1,
            tiled=True,
        ),
        lax.all_to_all(
            lax.all_to_all(filt_rows, "grp", split_axis=0, concat_axis=0, tiled=True),
            "shard",
            split_axis=1,
            concat_axis=1,
            tiled=True,
        ),
    )
    dev_ids = jnp.arange(devices, dtype=jnp.int32)
    freq_ids = jnp.arange(span_len, dtype=jnp.int32)
    outer = angles_of(freq_ids[:, None], dev_ids[None, :], span_len)
    outer_cos, outer_sin = (jnp.cos(outer), jnp.sin(outer))
    flat_ids = device_id * slice_len + jnp.arange(slice_len, dtype=jnp.int32)
    row_of = flat_ids // channels
    twist = angles_of(freq_ids[:, None], row_of[None, :], length)
    twist_cos, twist_sin = (jnp.cos(twist), jnp.sin(twist))

    def forward_outer(values):
        flat_values = values.reshape(devices, slice_len)
        real = jnp.dot(outer_cos, flat_values, precision=precise)
        imag = -jnp.dot(outer_sin, flat_values, precision=precise)
        turned_re = real * twist_cos + imag * twist_sin
        turned_im = imag * twist_cos - real * twist_sin
        return (
            turned_re.reshape(2, groups, shards, slice_len),
            turned_im.reshape(2, groups, shards, slice_len),
        )

    mixed_re, mixed_im = forward_outer(got_mixed)
    filt_re, filt_im = forward_outer(got_filt)
    mixed_re, mixed_im, filt_re, filt_im = (
        lax.all_to_all(
            lax.all_to_all(mixed_re, "grp", split_axis=1, concat_axis=1, tiled=True),
            "shard",
            split_axis=2,
            concat_axis=2,
            tiled=True,
        ),
        lax.all_to_all(
            lax.all_to_all(mixed_im, "grp", split_axis=1, concat_axis=1, tiled=True),
            "shard",
            split_axis=2,
            concat_axis=2,
            tiled=True,
        ),
        lax.all_to_all(
            lax.all_to_all(filt_re, "grp", split_axis=1, concat_axis=1, tiled=True),
            "shard",
            split_axis=2,
            concat_axis=2,
            tiled=True,
        ),
        lax.all_to_all(
            lax.all_to_all(filt_im, "grp", split_axis=1, concat_axis=1, tiled=True),
            "shard",
            split_axis=2,
            concat_axis=2,
            tiled=True,
        ),
    )
    row_ids = jnp.arange(positions, dtype=jnp.int32)
    inner = angles_of(row_ids[:, None], row_ids[None, :], positions)
    inner_cos, inner_sin = (jnp.cos(inner), jnp.sin(inner))

    def forward_inner(real, imag):
        real = real.reshape(2, positions, channels)
        imag = imag.reshape(2, positions, channels)
        out_re = jnp.einsum("kp,rpc->rkc", inner_cos, real, precision=precise) + jnp.einsum(
            "kp,rpc->rkc", inner_sin, imag, precision=precise
        )
        out_im = jnp.einsum("kp,rpc->rkc", inner_cos, imag, precision=precise) - jnp.einsum(
            "kp,rpc->rkc", inner_sin, real, precision=precise
        )
        return (out_re, out_im)

    spec_mixed_re, spec_mixed_im = forward_inner(mixed_re, mixed_im)
    spec_filt_re, spec_filt_im = forward_inner(filt_re, filt_im)
    prod_re = spec_mixed_re * spec_filt_re - spec_mixed_im * spec_filt_im
    prod_im = spec_mixed_re * spec_filt_im + spec_mixed_im * spec_filt_re
    back_re = jnp.einsum("kp,rkc->rpc", inner_cos, prod_re, precision=precise) - jnp.einsum(
        "kp,rkc->rpc", inner_sin, prod_im, precision=precise
    )
    back_im = jnp.einsum("kp,rkc->rpc", inner_cos, prod_im, precision=precise) + jnp.einsum(
        "kp,rkc->rpc", inner_sin, prod_re, precision=precise
    )
    own_freqs = jnp.arange(2, dtype=jnp.int32) * devices + device_id
    back_twist = angles_of(own_freqs[:, None], row_ids[None, :], length)
    back_cos, back_sin = (jnp.cos(back_twist)[:, :, None], jnp.sin(back_twist)[:, :, None])
    rot_re = (back_re * back_cos - back_im * back_sin).reshape(2, groups, shards, slice_len)
    rot_im = (back_re * back_sin + back_im * back_cos).reshape(2, groups, shards, slice_len)
    rot_re, rot_im = (
        lax.all_to_all(
            lax.all_to_all(rot_re, "grp", split_axis=1, concat_axis=1, tiled=True),
            "shard",
            split_axis=2,
            concat_axis=2,
            tiled=True,
        ),
        lax.all_to_all(
            lax.all_to_all(rot_im, "grp", split_axis=1, concat_axis=1, tiled=True),
            "shard",
            split_axis=2,
            concat_axis=2,
            tiled=True,
        ),
    )
    rot_re = rot_re.reshape(span_len, slice_len)
    rot_im = rot_im.reshape(span_len, slice_len)
    values = (
        jnp.einsum("kd,kf->df", outer_cos, rot_re, precision=precise)
        - jnp.einsum("kd,kf->df", outer_sin, rot_im, precision=precise)
    ) / length
    values = values.reshape(groups, shards, slice_len)
    conv_rows = lax.all_to_all(
        lax.all_to_all(values, "grp", split_axis=0, concat_axis=0, tiled=True),
        "shard",
        split_axis=1,
        concat_axis=1,
        tiled=True,
    )
    conv = conv_rows.reshape(positions, channels)
    return (query * (conv + skip_gain * mixed)).astype(jnp.bfloat16)


MESH = pl.DeviceIdType.MESH
LANES = 128
SUB = 8
HALO = 8
REACH = 250.0
FAINT = 1e-30
MIX = 3
RIMS = ((1, 2), (0, 0))


def turned(value, numerator, denominator):
    numerator %= denominator
    real, imag = value
    eighths, rest = divmod(8 * numerator, denominator)
    if rest == 0:
        half = math.sqrt(0.5)
        if eighths == 0:
            return (real, imag)
        if eighths == 2:
            return (-imag, real)
        if eighths == 4:
            return (-real, -imag)
        if eighths == 6:
            return (imag, -real)
        if eighths == 1:
            return ((real - imag) * half, (real + imag) * half)
        if eighths == 3:
            return ((real + imag) * -half, (real - imag) * half)
        if eighths == 5:
            return ((imag - real) * half, (real + imag) * -half)
        return ((real + imag) * half, (imag - real) * half)
    angle = 2.0 * math.pi * numerator / denominator
    cos, sin = (math.cos(angle), math.sin(angle))
    return (real * cos - imag * sin, real * sin + imag * cos)


def fft(loads, sign):
    count = len(loads)
    if count == 1:
        return [loads[0]()]
    even, odd = (fft(loads[::2], sign), fft(loads[1::2], sign))
    low, high = ([], [])
    for k in range(count // 2):
        moved = turned(odd[k], sign * k, count)
        low.append((even[k][0] + moved[0], even[k][1] + moved[1]))
        high.append((even[k][0] - moved[0], even[k][1] - moved[1]))
    return low + high


def dot3(values, table_hi, table_lo):
    hi = values.astype(jnp.bfloat16)
    lo = (values - hi.astype(jnp.float32)).astype(jnp.bfloat16)
    dot = functools.partial(jnp.dot, preferred_element_type=jnp.float32)
    return dot(hi, table_hi[...]) + (dot(lo, table_hi[...]) + dot(hi, table_lo[...]))


def encoded(scaled):
    magnitude = jnp.exp2(jnp.abs(scaled) - REACH / 2)
    return jnp.where(scaled < 0, -magnitude, magnitude)


def decoded(code):
    wide = code.astype(jnp.float32)
    magnitude = jnp.log2(jnp.abs(wide)) + REACH / 2
    return jnp.where(wide < 0, -magnitude, magnitude)


def owner_kernel(
    sizes,
    proj_ref_far,
    taps_ref_far,
    filt_ref_far,
    gain_ref_far,
    fwd_hi_far,
    fwd_lo_far,
    inv_hi_far,
    inv_lo_far,
    twist_cos_far,
    twist_sin_far,
    out_ref,
    proj_ref,
    taps_ref,
    filt_ref,
    gain_ref,
    fwd_hi,
    fwd_lo,
    inv_hi,
    inv_lo,
    twist_cos,
    twist_sin,
    rim_out,
    rim_in,
    ext,
    query,
    mixed,
    filt_out,
    mix_out,
    conv_out,
    filt_in,
    mix_in,
    conv_in,
    mix_top,
    mix_tops,
    conv_top,
    conv_tops,
    columns,
    blocks,
    spec_a,
    spec_held,
    spec_g,
    load_sems,
    rim_sems,
    send_sems,
    recv_sems,
):
    groups, shards, positions, channels, taps = sizes
    devices = groups * shards
    owned = channels // devices
    halves = owned // SUB
    per_chunk = LANES // owned
    chunks = channels // LANES
    bound = 6.0 / math.sqrt(devices * positions)
    my_group, my_shard = (lax.axis_index("grp"), lax.axis_index("shard"))
    me = my_group * shards + my_shard
    first_lane = lax.rem(me, per_chunk) * owned

    def partners(act):
        for apart in range(devices - 1, 0, -1):
            group = jnp.bitwise_xor(my_group, apart // shards)
            shard = jnp.bitwise_xor(my_shard, apart % shards)
            act((group, shard), group * shards + shard)

    def place(target):
        return (target // shards, target % shards)

    barrier = pltpu.get_barrier_semaphore()
    partners(
        lambda there, target: pl.semaphore_signal(
            barrier, inc=1, device_id=there, device_id_type=MESH
        )
    )

    far = (filt_ref_far, proj_ref_far, taps_ref_far, gain_ref_far, fwd_hi_far, fwd_lo_far)
    far += (inv_hi_far, inv_lo_far, twist_cos_far, twist_sin_far)
    near = (filt_ref, proj_ref, taps_ref, gain_ref, fwd_hi, fwd_lo)
    near += (inv_hi, inv_lo, twist_cos, twist_sin)
    loads = [
        pltpu.make_async_copy(source_ref, here_ref, load_sems.at[which])
        for which, (source_ref, here_ref) in enumerate(zip(far, near))
    ]
    for load in loads:
        load.start()

    def spread(chunk, block, stores):
        turned_block = block.T
        rows = owned // len(stores)
        for part in range(per_chunk):
            for which, store in enumerate(stores):
                first = part * owned + which * rows
                piece = turned_block[first : first + rows, :]
                store[chunk * per_chunk + part] = piece.astype(jnp.bfloat16)

    loads[0].wait()
    for chunk in range(chunks):
        lanes = slice(chunk * LANES, (chunk + 1) * LANES)
        spread(chunk, encoded(filt_ref[:, lanes] * (REACH / bound)), [filt_out])
    loads[1].wait()
    last = slice(positions - 16, positions)
    for pair in range(2):
        tails = [
            proj_ref[which, last, :].astype(jnp.float32)[8:]
            for which in RIMS[pair]
        ]
        rim_out[pair] = jnp.concatenate(tails, axis=0).astype(jnp.bfloat16)
    pl.semaphore_wait(barrier, devices - 1)

    rim_copies = [
        pltpu.make_async_remote_copy(
            src_ref=rim_out.at[pair],
            dst_ref=rim_in.at[pair],
            send_sem=rim_sems.at[0, pair],
            recv_sem=rim_sems.at[1, pair],
            device_id=place(lax.rem(me + 1, devices)),
            device_id_type=MESH,
        )
        for pair in range(2)
    ]

    def send_all(kind, source, landing, index=lambda target: target):
        def send(there, target):
            pltpu.make_async_remote_copy(
                src_ref=source.at[index(target)],
                dst_ref=landing.at[me],
                send_sem=send_sems.at[kind],
                recv_sem=recv_sems.at[kind],
                device_id=there,
                device_id_type=MESH,
            ).start()

        partners(send)
        landing[me] = source[index(me)]

    def wait_all(kind, landing, sems):
        others = landing.at[pl.ds(0, devices - 1)]
        pltpu.make_async_copy(others, others, sems.at[kind]).wait()

    for rim_copy in rim_copies:
        rim_copy.start()
    send_all(0, filt_out, filt_in)

    for load in loads[2:]:
        load.wait()

    def shortened(which, chunk, begin, end):
        lanes = slice(chunk * LANES, (chunk + 1) * LANES)
        total = None
        for tap in range(taps):
            term = taps_ref[which, tap : tap + 1, lanes] * ext[
                which, chunk, HALO + begin - tap : HALO + end - tap, :
            ]
            total = term if total is None else total + term
        return total

    for chunk in range(chunks):
        lanes = slice(chunk * LANES, (chunk + 1) * LANES)
        for which in range(3):
            ext[which, chunk, HALO:, :] = proj_ref[which, :, lanes].astype(jnp.float32)
        mixed[chunk, HALO:, :] = shortened(1, chunk, HALO, positions) * shortened(
            2, chunk, HALO, positions
        )
    for rim_copy in rim_copies:
        rim_copy.wait()
    keep = jnp.where(me > 0, 1.0, 0.0).astype(jnp.float32)
    for chunk in range(chunks):
        lanes = slice(chunk * LANES, (chunk + 1) * LANES)
        for which in range(3):
            pair = 0 if which in RIMS[0] else 1
            part = RIMS[pair].index(which)
            tail = rim_in[pair, :, lanes].astype(jnp.float32)[part * 8 : part * 8 + 8]
            ext[which, chunk, HALO - 8 : HALO, :] = tail * keep
        mixed[chunk, :HALO, :] = shortened(1, chunk, 0, HALO) * shortened(2, chunk, 0, HALO)
        block = mixed[chunk]
        top = jnp.maximum(jnp.max(jnp.abs(block), axis=0, keepdims=True), FAINT)
        mix_top[chunk] = top * (1.0 / REACH)
        spread(chunk, encoded(block * (REACH / top)), [mix_out.at[half] for half in range(halves)])
    send_all(1, mix_top, mix_tops, lambda target: target // per_chunk)
    for half in range(halves):
        send_all(MIX + half, mix_out.at[half], mix_in.at[half])

    for chunk in range(chunks):
        lanes = slice(chunk * LANES, (chunk + 1) * LANES)
        query[chunk] = shortened(0, chunk, 0, positions)
        mixed[chunk] = mixed[chunk] * gain_ref[:, lanes]

    def transform(half, level):
        def load(block):
            def get():
                value = blocks[half, block]
                angle = 2.0 * math.pi * block / (4 * devices)
                return (value * (level * math.cos(angle)), value * (level * math.sin(angle)))

            return get

        for k, (real, imag) in enumerate(fft([load(b) for b in range(devices)], 1)):
            cos, sin = (twist_cos[k : k + 1, :], twist_sin[k : k + 1, :])
            rows = slice(k * SUB, (k + 1) * SUB)
            spec_a[rows, :LANES] = real * cos - imag * sin
            spec_a[rows, LANES:] = real * sin + imag * cos
        return dot3(spec_a[...], fwd_hi, fwd_lo)

    wait_all(0, filt_in, recv_sems)
    for block in range(devices):
        value = decoded(filt_in[block])
        for half in range(halves):
            blocks[half, block] = value[half * SUB : (half + 1) * SUB, :]
    for half in range(halves):
        spec_held[half] = transform(half, bound / REACH)

    wait_all(1, mix_tops, recv_sems)
    columns[...] = jnp.zeros_like(columns)
    columns[:devices, :] = mix_tops[:, 0, :]
    columns[...] = columns[...].T
    own_tops = columns[pl.ds(pl.multiple_of(first_lane, owned), owned), :]
    row = lax.broadcasted_iota(jnp.int32, (SUB, LANES), 0) + first_lane
    lane = lax.broadcasted_iota(jnp.int32, (SUB, LANES), 1)
    top_row = None
    for half in range(halves):
        wait_all(MIX + half, mix_in.at[half], recv_sems)
        for block in range(devices):
            top = own_tops[half * SUB : (half + 1) * SUB, block : block + 1]
            blocks[half, block] = decoded(mix_in[half, block]) * top
        far_spec = transform(half, 1.0)
        far_re, far_im = (far_spec[:, :LANES], far_spec[:, LANES:])
        held_re, held_im = (spec_held[half, :, :LANES], spec_held[half, :, LANES:])
        spec_a[:, :LANES] = far_re * held_re - far_im * held_im
        spec_a[:, LANES:] = far_re * held_im + far_im * held_re
        spec_g[...] = dot3(spec_a[...], inv_hi, inv_lo)

        def load(k):
            def get():
                rows = slice(k * SUB, (k + 1) * SUB)
                real, imag = (spec_g[rows, :LANES], spec_g[rows, LANES:])
                cos, sin = (twist_cos[k : k + 1, :], twist_sin[k : k + 1, :])
                return (real * cos + imag * sin, imag * cos - real * sin)

            return get

        top = None
        for block, (real, imag) in enumerate(fft([load(k) for k in range(devices)], -1)):
            angle = 2.0 * math.pi * block / (4 * devices)
            value = real * math.cos(angle) + imag * math.sin(angle)
            blocks[half, block] = value
            top = jnp.abs(value) if top is None else jnp.maximum(top, jnp.abs(value))
        top = jnp.maximum(jnp.max(top, axis=1, keepdims=True), FAINT)
        ratio = REACH / top
        for block in range(devices):
            conv_out[half, block] = encoded(blocks[half, block] * ratio).astype(jnp.bfloat16)
        here = jnp.where(row + half * SUB == lane, top * (1.0 / REACH), 0.0)
        here = jnp.sum(here, axis=0, keepdims=True)
        top_row = here if top_row is None else top_row + here
        if half == halves - 1:
            conv_top[0] = top_row
            send_all(2, conv_top, conv_tops, lambda target: 0)
        send_all(MIX + halves + half, conv_out.at[half], conv_in.at[half])

    wait_all(2, conv_tops, recv_sems)
    for half in range(halves):
        wait_all(MIX + halves + half, conv_in.at[half], recv_sems)
        for block in range(devices):
            blocks[half, block] = decoded(conv_in[half, block])
    for chunk in range(chunks):
        lanes = slice(chunk * LANES, (chunk + 1) * LANES)
        owners = slice(chunk * per_chunk, (chunk + 1) * per_chunk)
        top = jnp.sum(conv_tops[owners, 0, :], axis=0, keepdims=True)
        pieces = [
            blocks[half, chunk * per_chunk + part]
            for part in range(per_chunk)
            for half in range(halves)
        ]
        conv = jnp.concatenate(pieces, axis=0).T * top
        out_ref[:, lanes] = (query[chunk] * (conv + mixed[chunk])).astype(out_ref.dtype)
    wait_all(0, filt_out, send_sems)
    wait_all(1, mix_tops, send_sems)
    wait_all(2, conv_tops, send_sems)
    for half in range(halves):
        wait_all(MIX + half, mix_out.at[half], send_sems)
        wait_all(MIX + halves + half, conv_out.at[half], send_sems)


def split_table(table):
    hi = table.astype(jnp.bfloat16)
    lo = (table - hi.astype(np.float64)).astype(jnp.bfloat16)
    return hi, lo


def tables(devices, positions):
    p = np.arange(positions, dtype=np.float64)
    angle = 2.0 * np.pi * ((p[:, None] * p[None, :]) % positions) / positions
    cos, sin = (np.cos(angle), np.sin(angle))
    forward = np.block([[cos, sin], [-sin, cos]])
    backward = np.block([[cos, -sin], [sin, cos]]) / (devices * positions)
    k = np.arange(devices, dtype=np.float64)
    twist = 2.0 * np.pi * (k[:, None] + 0.25) * p[None, :] / (devices * positions)
    return (
        *split_table(forward),
        *split_table(backward),
        np.cos(twist).astype(np.float32),
        np.sin(twist).astype(np.float32),
    )


def owned_channels(consts, groups, shards, projections, short_taps, long_filter, skip_gain):
    _, positions, channels = projections.shape
    devices = groups * shards
    owned = channels // devices
    halves = owned // SUB
    chunks = channels // LANES
    sizes = (groups, shards, positions, channels, short_taps.shape[1])
    f32, bf16 = (jnp.float32, jnp.bfloat16)
    operands = (projections, short_taps, long_filter, skip_gain.reshape(1, channels), *consts)
    slabs = pltpu.VMEM((devices, owned, LANES), bf16)
    halved = pltpu.VMEM((halves, devices, SUB, LANES), bf16)
    vmem = pl.BlockSpec(memory_space=pltpu.VMEM)
    return pl.pallas_call(
        functools.partial(owner_kernel, sizes),
        out_shape=jax.ShapeDtypeStruct((positions, channels), bf16),
        in_specs=[pl.BlockSpec(memory_space=pl.ANY)] * (4 + len(consts)),
        out_specs=vmem,
        scratch_shapes=[
            *(pltpu.VMEM(operand.shape, operand.dtype) for operand in operands),
            pltpu.VMEM((2, 16, channels), bf16),
            pltpu.VMEM((2, 16, channels), bf16),
            pltpu.VMEM((3, chunks, HALO + positions, LANES), f32),
            pltpu.VMEM((chunks, positions, LANES), f32),
            pltpu.VMEM((chunks, positions, LANES), f32),
            slabs,
            halved,
            halved,
            slabs,
            halved,
            halved,
            pltpu.VMEM((chunks, 1, LANES), f32),
            pltpu.VMEM((devices, 1, LANES), f32),
            pltpu.VMEM((1, 1, LANES), f32),
            pltpu.VMEM((devices, 1, LANES), f32),
            pltpu.VMEM((LANES, LANES), f32),
            pltpu.VMEM((halves, devices, SUB, LANES), f32),
            pltpu.VMEM((devices * SUB, 2 * LANES), f32),
            pltpu.VMEM((halves, devices * SUB, 2 * LANES), f32),
            pltpu.VMEM((devices * SUB, 2 * LANES), f32),
            pltpu.SemaphoreType.DMA((len(operands),)),
            pltpu.SemaphoreType.DMA((2, 2)),
            pltpu.SemaphoreType.DMA((MIX + 2 * halves,)),
            pltpu.SemaphoreType.DMA((MIX + 2 * halves,)),
        ],
        compiler_params=pltpu.CompilerParams(collective_id=0, has_side_effects=True, vmem_limit_bytes=16*1024*1024),
    )(*(pltpu.with_memory_space_constraint(o, pltpu.HBM) for o in operands))


def on_device(groups, shards, projections, short_taps, long_filter, skip_gain):
    _, positions, channels = projections.shape
    devices = groups * shards
    fits = (
        positions == LANES
        and channels % LANES == 0
        and channels % (SUB * devices) == 0
        and LANES % (channels // devices) == 0
        and devices & (devices - 1) == 0
        and (channels // devices) % 16 == 0
        and devices <= LANES
        and short_taps.shape[1] <= HALO + 1
    )
    if not fits:
        return per_device(projections, short_taps, long_filter, skip_gain)
    consts = tables(devices, positions)
    return owned_channels(consts, groups, shards, projections, short_taps, long_filter, skip_gain)


def solution(mesh):
    placed = (P(None, ("grp", "shard"), None), P(), P(("grp", "shard"), None), P())
    body = functools.partial(on_device, mesh.shape["grp"], mesh.shape["shard"])
    return jax.shard_map(
        body, mesh=mesh, in_specs=placed, out_specs=P(("grp", "shard"), None), check_vma=False
    )
```

```python
import functools
import math

import jax
import jax.numpy as jnp
import numpy as np
from jax import lax
from jax.experimental import pallas as pl
from jax.experimental.pallas import tpu as pltpu
from jax.sharding import PartitionSpec as P

precise = lax.Precision.HIGHEST


def from_behind(block, axis, distance):
    devices = range(lax.axis_size(axis))
    route = [(i - distance, i) for i in devices if i - distance in devices]
    return lax.ppermute(block, axis, route)


def angles_of(first, second, modulus):
    return (first * second % modulus).astype(jnp.float32) * (2.0 * math.pi / modulus)


def per_device(projections, short_taps, long_filter, skip_gain):
    positions = projections.shape[1]
    channels = projections.shape[2]
    taps_count = short_taps.shape[1]
    groups = lax.axis_size("grp")
    shards = lax.axis_size("shard")
    devices = groups * shards
    span_len = 2 * devices
    length = span_len * positions
    slice_len = positions * channels // devices
    device_id = lax.axis_index("grp") * shards + lax.axis_index("shard")
    rim_rows = from_behind(projections[:, positions - (taps_count - 1) :, :], ("grp", "shard"), 1)
    extended = jnp.concatenate([rim_rows, projections], axis=1)
    shortened = short_taps[:, 0, None, :] * extended[
        :, taps_count - 1 : taps_count - 1 + positions, :
    ].astype(jnp.float32)
    for tap_index in range(1, taps_count):
        shortened = shortened + short_taps[:, tap_index, None, :] * extended[
            :, taps_count - 1 - tap_index : taps_count - 1 - tap_index + positions, :
        ].astype(jnp.float32)
    query = shortened[0]
    mixed = shortened[1] * shortened[2]
    mixed_rows = mixed.reshape(groups, shards, slice_len)
    filt_rows = long_filter.reshape(groups, shards, slice_len)
    got_mixed, got_filt = (
        lax.all_to_all(
            lax.all_to_all(mixed_rows, "grp", split_axis=0, concat_axis=0, tiled=True),
            "shard",
            split_axis=1,
            concat_axis=1,
            tiled=True,
        ),
        lax.all_to_all(
            lax.all_to_all(filt_rows, "grp", split_axis=0, concat_axis=0, tiled=True),
            "shard",
            split_axis=1,
            concat_axis=1,
            tiled=True,
        ),
    )
    dev_ids = jnp.arange(devices, dtype=jnp.int32)
    freq_ids = jnp.arange(span_len, dtype=jnp.int32)
    outer = angles_of(freq_ids[:, None], dev_ids[None, :], span_len)
    outer_cos, outer_sin = (jnp.cos(outer), jnp.sin(outer))
    flat_ids = device_id * slice_len + jnp.arange(slice_len, dtype=jnp.int32)
    row_of = flat_ids // channels
    twist = angles_of(freq_ids[:, None], row_of[None, :], length)
    twist_cos, twist_sin = (jnp.cos(twist), jnp.sin(twist))

    def forward_outer(values):
        flat_values = values.reshape(devices, slice_len)
        real = jnp.dot(outer_cos, flat_values, precision=precise)
        imag = -jnp.dot(outer_sin, flat_values, precision=precise)
        turned_re = real * twist_cos + imag * twist_sin
        turned_im = imag * twist_cos - real * twist_sin
        return (
            turned_re.reshape(2, groups, shards, slice_len),
            turned_im.reshape(2, groups, shards, slice_len),
        )

    mixed_re, mixed_im = forward_outer(got_mixed)
    filt_re, filt_im = forward_outer(got_filt)
    mixed_re, mixed_im, filt_re, filt_im = (
        lax.all_to_all(
            lax.all_to_all(mixed_re, "grp", split_axis=1, concat_axis=1, tiled=True),
            "shard",
            split_axis=2,
            concat_axis=2,
            tiled=True,
        ),
        lax.all_to_all(
            lax.all_to_all(mixed_im, "grp", split_axis=1, concat_axis=1, tiled=True),
            "shard",
            split_axis=2,
            concat_axis=2,
            tiled=True,
        ),
        lax.all_to_all(
            lax.all_to_all(filt_re, "grp", split_axis=1, concat_axis=1, tiled=True),
            "shard",
            split_axis=2,
            concat_axis=2,
            tiled=True,
        ),
        lax.all_to_all(
            lax.all_to_all(filt_im, "grp", split_axis=1, concat_axis=1, tiled=True),
            "shard",
            split_axis=2,
            concat_axis=2,
            tiled=True,
        ),
    )
    row_ids = jnp.arange(positions, dtype=jnp.int32)
    inner = angles_of(row_ids[:, None], row_ids[None, :], positions)
    inner_cos, inner_sin = (jnp.cos(inner), jnp.sin(inner))

    def forward_inner(real, imag):
        real = real.reshape(2, positions, channels)
        imag = imag.reshape(2, positions, channels)
        out_re = jnp.einsum("kp,rpc->rkc", inner_cos, real, precision=precise) + jnp.einsum(
            "kp,rpc->rkc", inner_sin, imag, precision=precise
        )
        out_im = jnp.einsum("kp,rpc->rkc", inner_cos, imag, precision=precise) - jnp.einsum(
            "kp,rpc->rkc", inner_sin, real, precision=precise
        )
        return (out_re, out_im)

    spec_mixed_re, spec_mixed_im = forward_inner(mixed_re, mixed_im)
    spec_filt_re, spec_filt_im = forward_inner(filt_re, filt_im)
    prod_re = spec_mixed_re * spec_filt_re - spec_mixed_im * spec_filt_im
    prod_im = spec_mixed_re * spec_filt_im + spec_mixed_im * spec_filt_re
    back_re = jnp.einsum("kp,rkc->rpc", inner_cos, prod_re, precision=precise) - jnp.einsum(
        "kp,rkc->rpc", inner_sin, prod_im, precision=precise
    )
    back_im = jnp.einsum("kp,rkc->rpc", inner_cos, prod_im, precision=precise) + jnp.einsum(
        "kp,rkc->rpc", inner_sin, prod_re, precision=precise
    )
    own_freqs = jnp.arange(2, dtype=jnp.int32) * devices + device_id
    back_twist = angles_of(own_freqs[:, None], row_ids[None, :], length)
    back_cos, back_sin = (jnp.cos(back_twist)[:, :, None], jnp.sin(back_twist)[:, :, None])
    rot_re = (back_re * back_cos - back_im * back_sin).reshape(2, groups, shards, slice_len)
    rot_im = (back_re * back_sin + back_im * back_cos).reshape(2, groups, shards, slice_len)
    rot_re, rot_im = (
        lax.all_to_all(
            lax.all_to_all(rot_re, "grp", split_axis=1, concat_axis=1, tiled=True),
            "shard",
            split_axis=2,
            concat_axis=2,
            tiled=True,
        ),
        lax.all_to_all(
            lax.all_to_all(rot_im, "grp", split_axis=1, concat_axis=1, tiled=True),
            "shard",
            split_axis=2,
            concat_axis=2,
            tiled=True,
        ),
    )
    rot_re = rot_re.reshape(span_len, slice_len)
    rot_im = rot_im.reshape(span_len, slice_len)
    values = (
        jnp.einsum("kd,kf->df", outer_cos, rot_re, precision=precise)
        - jnp.einsum("kd,kf->df", outer_sin, rot_im, precision=precise)
    ) / length
    values = values.reshape(groups, shards, slice_len)
    conv_rows = lax.all_to_all(
        lax.all_to_all(values, "grp", split_axis=0, concat_axis=0, tiled=True),
        "shard",
        split_axis=1,
        concat_axis=1,
        tiled=True,
    )
    conv = conv_rows.reshape(positions, channels)
    return (query * (conv + skip_gain * mixed)).astype(jnp.bfloat16)


MESH = pl.DeviceIdType.MESH
LANES = 128
SUB = 8
HALO = 8
REACH = 250.0
FAINT = 1e-30
MIX = 3
EARLY = 2
RIMS = ((1, 2), (0, 0))


def turned(value, numerator, denominator):
    numerator %= denominator
    real, imag = value
    eighths, rest = divmod(8 * numerator, denominator)
    if rest == 0:
        half = math.sqrt(0.5)
        if eighths == 0:
            return (real, imag)
        if eighths == 2:
            return (-imag, real)
        if eighths == 4:
            return (-real, -imag)
        if eighths == 6:
            return (imag, -real)
        if eighths == 1:
            return ((real - imag) * half, (real + imag) * half)
        if eighths == 3:
            return ((real + imag) * -half, (real - imag) * half)
        if eighths == 5:
            return ((imag - real) * half, (real + imag) * -half)
        return ((real + imag) * half, (imag - real) * half)
    angle = 2.0 * math.pi * numerator / denominator
    cos, sin = (math.cos(angle), math.sin(angle))
    return (real * cos - imag * sin, real * sin + imag * cos)


def fft(loads, sign):
    count = len(loads)
    if count == 1:
        return [loads[0]()]
    even, odd = (fft(loads[::2], sign), fft(loads[1::2], sign))
    low, high = ([], [])
    for k in range(count // 2):
        moved = turned(odd[k], sign * k, count)
        low.append((even[k][0] + moved[0], even[k][1] + moved[1]))
        high.append((even[k][0] - moved[0], even[k][1] - moved[1]))
    return low + high


def dot3(values, table_hi, table_lo):
    hi = values.astype(jnp.bfloat16)
    lo = (values - hi.astype(jnp.float32)).astype(jnp.bfloat16)
    dot = functools.partial(jnp.dot, preferred_element_type=jnp.float32)
    return dot(hi, table_hi[...]) + (dot(lo, table_hi[...]) + dot(hi, table_lo[...]))


def encoded(scaled):
    magnitude = jnp.exp2(jnp.abs(scaled) - REACH / 2)
    return jnp.where(scaled < 0, -magnitude, magnitude)


def decoded(code):
    wide = code.astype(jnp.float32)
    magnitude = jnp.log2(jnp.abs(wide)) + REACH / 2
    return jnp.where(wide < 0, -magnitude, magnitude)


def owner_kernel(
    sizes,
    proj_ref_far,
    taps_ref_far,
    filt_ref_far,
    gain_ref_far,
    fwd_hi_far,
    fwd_lo_far,
    inv_hi_far,
    inv_lo_far,
    twist_cos_far,
    twist_sin_far,
    out_ref,
    proj_ref,
    taps_ref,
    filt_ref,
    gain_ref,
    fwd_hi,
    fwd_lo,
    inv_hi,
    inv_lo,
    twist_cos,
    twist_sin,
    rim_out,
    rim_in,
    ext,
    query,
    mixed,
    filt_out,
    mix_out,
    conv_out,
    filt_in,
    mix_in,
    conv_in,
    mix_top,
    mix_tops,
    conv_top,
    conv_tops,
    columns,
    blocks,
    spec_a,
    spec_held,
    spec_g,
    own_filt,
    own_mix,
    first_filt,
    first_mix,
    load_sems,
    rim_sems,
    send_sems,
    recv_sems,
    first_sems,
):
    groups, shards, positions, channels, taps = sizes
    devices = groups * shards
    owned = channels // devices
    halves = owned // SUB
    per_chunk = LANES // owned
    chunks = channels // LANES
    bound = 6.0 / math.sqrt(devices * positions)
    my_group, my_shard = (lax.axis_index("grp"), lax.axis_index("shard"))
    me = my_group * shards + my_shard
    first_lane = lax.rem(me, per_chunk) * owned

    def partners(act):
        for apart in range(devices - 1, 0, -1):
            group = jnp.bitwise_xor(my_group, apart // shards)
            shard = jnp.bitwise_xor(my_shard, apart % shards)
            act((group, shard), group * shards + shard)

    def place(target):
        return (target // shards, target % shards)

    barrier = pltpu.get_barrier_semaphore()
    partners(
        lambda there, target: pl.semaphore_signal(
            barrier, inc=1, device_id=there, device_id_type=MESH
        )
    )

    far = (filt_ref_far, proj_ref_far, taps_ref_far, gain_ref_far, fwd_hi_far, fwd_lo_far)
    far += (inv_hi_far, inv_lo_far, twist_cos_far, twist_sin_far)
    near = (filt_ref, proj_ref, taps_ref, gain_ref, fwd_hi, fwd_lo)
    near += (inv_hi, inv_lo, twist_cos, twist_sin)
    loads = [
        pltpu.make_async_copy(source_ref, here_ref, load_sems.at[which])
        for which, (source_ref, here_ref) in enumerate(zip(far, near))
    ]
    for load in loads:
        load.start()

    def spread(chunk, block, stores):
        turned_block = block.T
        rows = owned // len(stores)
        for part in range(per_chunk):
            for which, store in enumerate(stores):
                first = part * owned + which * rows
                piece = turned_block[first : first + rows, :]
                store[chunk * per_chunk + part] = piece.astype(jnp.bfloat16)

    loads[0].wait()
    for chunk in range(chunks):
        lanes = slice(chunk * LANES, (chunk + 1) * LANES)
        spread(chunk, encoded(filt_ref[:, lanes] * (REACH / bound)), [filt_out])
    loads[1].wait()
    last = slice(positions - 16, positions)
    for pair in range(2):
        tails = [
            proj_ref[which, last, :].astype(jnp.float32)[8:]
            for which in RIMS[pair]
        ]
        rim_out[pair] = jnp.concatenate(tails, axis=0).astype(jnp.bfloat16)
    pl.semaphore_wait(barrier, devices - 1)

    rim_copies = [
        pltpu.make_async_remote_copy(
            src_ref=rim_out.at[pair],
            dst_ref=rim_in.at[pair],
            send_sem=rim_sems.at[0, pair],
            recv_sem=rim_sems.at[1, pair],
            device_id=place(lax.rem(me + 1, devices)),
            device_id_type=MESH,
        )
        for pair in range(2)
    ]

    def send_all(kind, source, landing, index=lambda target: target, first=0):
        def send(there, target):
            copy = pltpu.make_async_remote_copy(
                src_ref=source.at[index(target)],
                dst_ref=landing.at[me],
                send_sem=send_sems.at[kind],
                recv_sem=recv_sems.at[kind],
                device_id=there,
                device_id_type=MESH,
            )
            if first:
                pl.when(target >= first)(copy.start)
            else:
                copy.start()

        partners(send)
        landing[me] = source[index(me)]

    def wait_all(kind, landing, sems, count=devices - 1):
        others = landing.at[pl.ds(0, count)]
        pltpu.make_async_copy(others, others, sems.at[kind]).wait()

    for rim_copy in rim_copies:
        rim_copy.start()
    send_all(0, filt_out, filt_in)

    for load in loads[2:]:
        load.wait()

    def shortened(which, chunk, begin, end):
        lanes = slice(chunk * LANES, (chunk + 1) * LANES)
        total = None
        for tap in range(taps):
            term = taps_ref[which, tap : tap + 1, lanes] * ext[
                which, chunk, HALO + begin - tap : HALO + end - tap, :
            ]
            total = term if total is None else total + term
        return total

    for chunk in range(chunks):
        lanes = slice(chunk * LANES, (chunk + 1) * LANES)
        for which in range(3):
            ext[which, chunk, HALO:, :] = proj_ref[which, :, lanes].astype(jnp.float32)
        mixed[chunk, HALO:, :] = shortened(1, chunk, HALO, positions) * shortened(
            2, chunk, HALO, positions
        )
    for rim_copy in rim_copies:
        rim_copy.wait()
    keep = jnp.where(me > 0, 1.0, 0.0).astype(jnp.float32)
    for chunk in range(chunks):
        lanes = slice(chunk * LANES, (chunk + 1) * LANES)
        for which in range(3):
            pair = 0 if which in RIMS[0] else 1
            part = RIMS[pair].index(which)
            tail = rim_in[pair, :, lanes].astype(jnp.float32)[part * 8 : part * 8 + 8]
            ext[which, chunk, HALO - 8 : HALO, :] = tail * keep
        mixed[chunk, :HALO, :] = shortened(1, chunk, 0, HALO) * shortened(2, chunk, 0, HALO)
        block = mixed[chunk]
        top = jnp.maximum(jnp.max(jnp.abs(block), axis=0, keepdims=True), FAINT)
        mix_top[chunk] = top * (1.0 / REACH)
        spread(chunk, encoded(block * (REACH / top)), [mix_out.at[half] for half in range(halves)])
    send_all(1, mix_top, mix_tops, lambda target: target // per_chunk)
    for half in range(halves):
        send_all(MIX + half, mix_out.at[half], mix_in.at[half])

    for chunk in range(chunks):
        query[chunk] = shortened(0, chunk, 0, positions)

    @pl.when(me < EARLY)
    def _():
        for chunk in range(chunks):
            lanes = slice(chunk * LANES, (chunk + 1) * LANES)
            own_filt[lanes, :] = filt_ref[:, lanes].T
            own_mix[lanes, :] = mixed[chunk].T

    first_copies = [
        pltpu.make_async_remote_copy(
            src_ref=source,
            dst_ref=landing,
            send_sem=first_sems.at[0, which],
            recv_sem=first_sems.at[1, which],
            device_id=place(jnp.bitwise_xor(me, 1)),
            device_id_type=MESH,
        )
        for which, (source, landing) in enumerate(((own_filt, first_filt), (own_mix, first_mix)))
    ]

    @pl.when(me == 0)
    def _():
        for copy in first_copies:
            copy.start()

    for chunk in range(chunks):
        lanes = slice(chunk * LANES, (chunk + 1) * LANES)
        mixed[chunk] = mixed[chunk] * gain_ref[:, lanes]

    def transform(half, level):
        def load(block):
            def get():
                value = blocks[half, block]
                angle = 2.0 * math.pi * block / (4 * devices)
                return (value * (level * math.cos(angle)), value * (level * math.sin(angle)))

            return get

        for k, (real, imag) in enumerate(fft([load(b) for b in range(devices)], 1)):
            cos, sin = (twist_cos[k : k + 1, :], twist_sin[k : k + 1, :])
            rows = slice(k * SUB, (k + 1) * SUB)
            spec_a[rows, :LANES] = real * cos - imag * sin
            spec_a[rows, LANES:] = real * sin + imag * cos
        return dot3(spec_a[...], fwd_hi, fwd_lo)

    wait_all(0, filt_in, recv_sems)
    for block in range(devices):
        value = decoded(filt_in[block])
        for half in range(halves):
            blocks[half, block] = value[half * SUB : (half + 1) * SUB, :]
    for half in range(halves):
        spec_held[half] = transform(half, bound / REACH)

    wait_all(1, mix_tops, recv_sems)
    columns[...] = jnp.zeros_like(columns)
    columns[:devices, :] = mix_tops[:, 0, :]
    columns[...] = columns[...].T
    own_tops = columns[pl.ds(pl.multiple_of(first_lane, owned), owned), :]
    row = lax.broadcasted_iota(jnp.int32, (SUB, LANES), 0) + first_lane
    lane = lax.broadcasted_iota(jnp.int32, (SUB, LANES), 1)
    top_row = None
    for half in range(halves):
        wait_all(MIX + half, mix_in.at[half], recv_sems)
        for block in range(devices):
            top = own_tops[half * SUB : (half + 1) * SUB, block : block + 1]
            blocks[half, block] = decoded(mix_in[half, block]) * top
        far_spec = transform(half, 1.0)
        far_re, far_im = (far_spec[:, :LANES], far_spec[:, LANES:])
        held_re, held_im = (spec_held[half, :, :LANES], spec_held[half, :, LANES:])
        spec_a[:, :LANES] = far_re * held_re - far_im * held_im
        spec_a[:, LANES:] = far_re * held_im + far_im * held_re
        spec_g[...] = dot3(spec_a[...], inv_hi, inv_lo)

        def load(k):
            def get():
                rows = slice(k * SUB, (k + 1) * SUB)
                real, imag = (spec_g[rows, :LANES], spec_g[rows, LANES:])
                cos, sin = (twist_cos[k : k + 1, :], twist_sin[k : k + 1, :])
                return (real * cos + imag * sin, imag * cos - real * sin)

            return get

        top = None
        for block, (real, imag) in enumerate(fft([load(k) for k in range(devices)], -1)):
            angle = 2.0 * math.pi * block / (4 * devices)
            value = real * math.cos(angle) + imag * math.sin(angle)
            blocks[half, block] = value
            top = jnp.abs(value) if top is None else jnp.maximum(top, jnp.abs(value))
        top = jnp.maximum(jnp.max(top, axis=1, keepdims=True), FAINT)
        ratio = REACH / top
        for block in range(devices):
            conv_out[half, block] = encoded(blocks[half, block] * ratio).astype(jnp.bfloat16)
        here = jnp.where(row + half * SUB == lane, top * (1.0 / REACH), 0.0)
        here = jnp.sum(here, axis=0, keepdims=True)
        top_row = here if top_row is None else top_row + here
        if half == halves - 1:
            conv_top[0] = top_row
            send_all(2, conv_top, conv_tops, lambda target: 0, EARLY)
        send_all(MIX + halves + half, conv_out.at[half], conv_in.at[half], first=EARLY)

    def store(chunk, conv):
        lanes = slice(chunk * LANES, (chunk + 1) * LANES)
        out_ref[:, lanes] = (query[chunk] * (conv + mixed[chunk])).astype(out_ref.dtype)

    @pl.when(me >= EARLY)
    def _():
        wait_all(2, conv_tops, recv_sems)
        for half in range(halves):
            wait_all(MIX + halves + half, conv_in.at[half], recv_sems)
            for block in range(devices):
                blocks[half, block] = decoded(conv_in[half, block])
        for chunk in range(chunks):
            owners = slice(chunk * per_chunk, (chunk + 1) * per_chunk)
            top = jnp.sum(conv_tops[owners, 0, :], axis=0, keepdims=True)
            pieces = [
                blocks[half, chunk * per_chunk + part]
                for part in range(per_chunk)
                for half in range(halves)
            ]
            store(chunk, jnp.concatenate(pieces, axis=0).T * top)
        wait_all(2, conv_tops, send_sems, devices - 1 - EARLY)
        for half in range(halves):
            wait_all(MIX + halves + half, conv_in.at[half], send_sems, devices - 1 - EARLY)

    @pl.when(me == 0)
    def _():
        for copy in first_copies:
            copy.wait_send()
        first_filt[...] = own_filt[...]
        first_mix[...] = jnp.zeros_like(first_mix)

    @pl.when(me == 1)
    def _():
        for copy in first_copies:
            copy.wait_recv()

    @pl.when(me < EARLY)
    def _():
        cos, sin = (twist_cos[devices : devices + 1, :], twist_sin[devices : devices + 1, :])

        def spectrum(source, rows):
            value = source[rows, :]
            return dot3(jnp.concatenate([value * cos, value * sin], axis=1), fwd_hi, fwd_lo)

        def product(left, right):
            left_re, left_im = (left[:, :LANES], left[:, LANES:])
            right_re, right_im = (right[:, :LANES], right[:, LANES:])
            return (left_re * right_re - left_im * right_im, left_re * right_im + left_im * right_re)

        for chunk in range(chunks):
            rows = slice(chunk * LANES, (chunk + 1) * LANES)
            filt_here, mix_here = (spectrum(own_filt, rows), spectrum(own_mix, rows))
            filt_first, mix_first = (spectrum(first_filt, rows), spectrum(first_mix, rows))
            near_re, near_im = product(mix_here, filt_first)
            cross_re, cross_im = product(mix_first, filt_here)
            over_re, over_im = product(mix_first, filt_first)
            total = jnp.concatenate(
                [near_re + cross_re + over_im, near_im + cross_im - over_re], axis=1
            )
            back = dot3(total, inv_hi, inv_lo) * float(devices)
            store(chunk, (back[:, :LANES] * cos + back[:, LANES:] * sin).T)
        wait_all(2, conv_tops, send_sems, devices - EARLY)
        for half in range(halves):
            wait_all(MIX + halves + half, conv_in.at[half], send_sems, devices - EARLY)

    wait_all(0, filt_out, send_sems)
    wait_all(1, mix_tops, send_sems)
    for half in range(halves):
        wait_all(MIX + half, mix_out.at[half], send_sems)


def split_table(table):
    hi = table.astype(jnp.bfloat16)
    lo = (table - hi.astype(np.float64)).astype(jnp.bfloat16)
    return hi, lo


def tables(devices, positions):
    p = np.arange(positions, dtype=np.float64)
    angle = 2.0 * np.pi * ((p[:, None] * p[None, :]) % positions) / positions
    cos, sin = (np.cos(angle), np.sin(angle))
    forward = np.block([[cos, sin], [-sin, cos]])
    backward = np.block([[cos, -sin], [sin, cos]]) / (devices * positions)
    k = np.arange(devices, dtype=np.float64)
    turns = np.append(k + 0.25, 0.25 * devices)
    twist = 2.0 * np.pi * turns[:, None] * p[None, :] / (devices * positions)
    return (
        *split_table(forward),
        *split_table(backward),
        np.cos(twist).astype(np.float32),
        np.sin(twist).astype(np.float32),
    )


def owned_channels(consts, groups, shards, projections, short_taps, long_filter, skip_gain):
    _, positions, channels = projections.shape
    devices = groups * shards
    owned = channels // devices
    halves = owned // SUB
    chunks = channels // LANES
    sizes = (groups, shards, positions, channels, short_taps.shape[1])
    f32, bf16 = (jnp.float32, jnp.bfloat16)
    operands = (projections, short_taps, long_filter, skip_gain.reshape(1, channels), *consts)
    slabs = pltpu.VMEM((devices, owned, LANES), bf16)
    halved = pltpu.VMEM((halves, devices, SUB, LANES), bf16)
    vmem = pl.BlockSpec(memory_space=pltpu.VMEM)
    return pl.pallas_call(
        functools.partial(owner_kernel, sizes),
        out_shape=jax.ShapeDtypeStruct((positions, channels), bf16),
        in_specs=[pl.BlockSpec(memory_space=pl.ANY)] * (4 + len(consts)),
        out_specs=vmem,
        scratch_shapes=[
            *(pltpu.VMEM(operand.shape, operand.dtype) for operand in operands),
            pltpu.VMEM((2, 16, channels), bf16),
            pltpu.VMEM((2, 16, channels), bf16),
            pltpu.VMEM((3, chunks, HALO + positions, LANES), f32),
            pltpu.VMEM((chunks, positions, LANES), f32),
            pltpu.VMEM((chunks, positions, LANES), f32),
            slabs,
            halved,
            halved,
            slabs,
            halved,
            halved,
            pltpu.VMEM((chunks, 1, LANES), f32),
            pltpu.VMEM((devices, 1, LANES), f32),
            pltpu.VMEM((1, 1, LANES), f32),
            pltpu.VMEM((devices, 1, LANES), f32),
            pltpu.VMEM((LANES, LANES), f32),
            pltpu.VMEM((halves, devices, SUB, LANES), f32),
            pltpu.VMEM((devices * SUB, 2 * LANES), f32),
            pltpu.VMEM((halves, devices * SUB, 2 * LANES), f32),
            pltpu.VMEM((devices * SUB, 2 * LANES), f32),
            *(pltpu.VMEM((channels, LANES), f32) for _ in range(4)),
            pltpu.SemaphoreType.DMA((len(operands),)),
            pltpu.SemaphoreType.DMA((2, 2)),
            pltpu.SemaphoreType.DMA((MIX + 2 * halves,)),
            pltpu.SemaphoreType.DMA((MIX + 2 * halves,)),
            pltpu.SemaphoreType.DMA((2, 2)),
        ],
        compiler_params=pltpu.CompilerParams(collective_id=0, has_side_effects=True, vmem_limit_bytes=16*1024*1024),
    )(*(pltpu.with_memory_space_constraint(o, pltpu.HBM) for o in operands))


def on_device(groups, shards, projections, short_taps, long_filter, skip_gain):
    _, positions, channels = projections.shape
    devices = groups * shards
    fits = (
        positions == LANES
        and channels % LANES == 0
        and channels % (SUB * devices) == 0
        and LANES % (channels // devices) == 0
        and devices & (devices - 1) == 0
        and (channels // devices) % 16 == 0
        and EARLY < devices <= LANES
        and short_taps.shape[1] <= HALO + 1
    )
    if not fits:
        return per_device(projections, short_taps, long_filter, skip_gain)
    consts = tables(devices, positions)
    return owned_channels(consts, groups, shards, projections, short_taps, long_filter, skip_gain)


def solution(mesh):
    placed = (P(None, ("grp", "shard"), None), P(), P(("grp", "shard"), None), P())
    body = functools.partial(on_device, mesh.shape["grp"], mesh.shape["shard"])
    return jax.shard_map(
        body, mesh=mesh, in_specs=placed, out_specs=P(("grp", "shard"), None), check_vma=False
    )
```

```python
import functools
import math

import jax
import jax.numpy as jnp
import numpy as np
from jax import lax
from jax.experimental import pallas as pl
from jax.experimental.pallas import tpu as pltpu
from jax.sharding import PartitionSpec as P

precise = lax.Precision.HIGHEST


def from_behind(block, axis, distance):
    devices = range(lax.axis_size(axis))
    route = [(i - distance, i) for i in devices if i - distance in devices]
    return lax.ppermute(block, axis, route)


def angles_of(first, second, modulus):
    return (first * second % modulus).astype(jnp.float32) * (2.0 * math.pi / modulus)


def per_device(projections, short_taps, long_filter, skip_gain):
    positions = projections.shape[1]
    channels = projections.shape[2]
    taps_count = short_taps.shape[1]
    groups = lax.axis_size("grp")
    shards = lax.axis_size("shard")
    devices = groups * shards
    span_len = 2 * devices
    length = span_len * positions
    slice_len = positions * channels // devices
    device_id = lax.axis_index("grp") * shards + lax.axis_index("shard")
    rim_rows = from_behind(projections[:, positions - (taps_count - 1) :, :], ("grp", "shard"), 1)
    extended = jnp.concatenate([rim_rows, projections], axis=1)
    shortened = short_taps[:, 0, None, :] * extended[
        :, taps_count - 1 : taps_count - 1 + positions, :
    ].astype(jnp.float32)
    for tap_index in range(1, taps_count):
        shortened = shortened + short_taps[:, tap_index, None, :] * extended[
            :, taps_count - 1 - tap_index : taps_count - 1 - tap_index + positions, :
        ].astype(jnp.float32)
    query = shortened[0]
    mixed = shortened[1] * shortened[2]
    mixed_rows = mixed.reshape(groups, shards, slice_len)
    filt_rows = long_filter.reshape(groups, shards, slice_len)
    got_mixed, got_filt = (
        lax.all_to_all(
            lax.all_to_all(mixed_rows, "grp", split_axis=0, concat_axis=0, tiled=True),
            "shard",
            split_axis=1,
            concat_axis=1,
            tiled=True,
        ),
        lax.all_to_all(
            lax.all_to_all(filt_rows, "grp", split_axis=0, concat_axis=0, tiled=True),
            "shard",
            split_axis=1,
            concat_axis=1,
            tiled=True,
        ),
    )
    dev_ids = jnp.arange(devices, dtype=jnp.int32)
    freq_ids = jnp.arange(span_len, dtype=jnp.int32)
    outer = angles_of(freq_ids[:, None], dev_ids[None, :], span_len)
    outer_cos, outer_sin = (jnp.cos(outer), jnp.sin(outer))
    flat_ids = device_id * slice_len + jnp.arange(slice_len, dtype=jnp.int32)
    row_of = flat_ids // channels
    twist = angles_of(freq_ids[:, None], row_of[None, :], length)
    twist_cos, twist_sin = (jnp.cos(twist), jnp.sin(twist))

    def forward_outer(values):
        flat_values = values.reshape(devices, slice_len)
        real = jnp.dot(outer_cos, flat_values, precision=precise)
        imag = -jnp.dot(outer_sin, flat_values, precision=precise)
        turned_re = real * twist_cos + imag * twist_sin
        turned_im = imag * twist_cos - real * twist_sin
        return (
            turned_re.reshape(2, groups, shards, slice_len),
            turned_im.reshape(2, groups, shards, slice_len),
        )

    mixed_re, mixed_im = forward_outer(got_mixed)
    filt_re, filt_im = forward_outer(got_filt)
    mixed_re, mixed_im, filt_re, filt_im = (
        lax.all_to_all(
            lax.all_to_all(mixed_re, "grp", split_axis=1, concat_axis=1, tiled=True),
            "shard",
            split_axis=2,
            concat_axis=2,
            tiled=True,
        ),
        lax.all_to_all(
            lax.all_to_all(mixed_im, "grp", split_axis=1, concat_axis=1, tiled=True),
            "shard",
            split_axis=2,
            concat_axis=2,
            tiled=True,
        ),
        lax.all_to_all(
            lax.all_to_all(filt_re, "grp", split_axis=1, concat_axis=1, tiled=True),
            "shard",
            split_axis=2,
            concat_axis=2,
            tiled=True,
        ),
        lax.all_to_all(
            lax.all_to_all(filt_im, "grp", split_axis=1, concat_axis=1, tiled=True),
            "shard",
            split_axis=2,
            concat_axis=2,
            tiled=True,
        ),
    )
    row_ids = jnp.arange(positions, dtype=jnp.int32)
    inner = angles_of(row_ids[:, None], row_ids[None, :], positions)
    inner_cos, inner_sin = (jnp.cos(inner), jnp.sin(inner))

    def forward_inner(real, imag):
        real = real.reshape(2, positions, channels)
        imag = imag.reshape(2, positions, channels)
        out_re = jnp.einsum("kp,rpc->rkc", inner_cos, real, precision=precise) + jnp.einsum(
            "kp,rpc->rkc", inner_sin, imag, precision=precise
        )
        out_im = jnp.einsum("kp,rpc->rkc", inner_cos, imag, precision=precise) - jnp.einsum(
            "kp,rpc->rkc", inner_sin, real, precision=precise
        )
        return (out_re, out_im)

    spec_mixed_re, spec_mixed_im = forward_inner(mixed_re, mixed_im)
    spec_filt_re, spec_filt_im = forward_inner(filt_re, filt_im)
    prod_re = spec_mixed_re * spec_filt_re - spec_mixed_im * spec_filt_im
    prod_im = spec_mixed_re * spec_filt_im + spec_mixed_im * spec_filt_re
    back_re = jnp.einsum("kp,rkc->rpc", inner_cos, prod_re, precision=precise) - jnp.einsum(
        "kp,rkc->rpc", inner_sin, prod_im, precision=precise
    )
    back_im = jnp.einsum("kp,rkc->rpc", inner_cos, prod_im, precision=precise) + jnp.einsum(
        "kp,rkc->rpc", inner_sin, prod_re, precision=precise
    )
    own_freqs = jnp.arange(2, dtype=jnp.int32) * devices + device_id
    back_twist = angles_of(own_freqs[:, None], row_ids[None, :], length)
    back_cos, back_sin = (jnp.cos(back_twist)[:, :, None], jnp.sin(back_twist)[:, :, None])
    rot_re = (back_re * back_cos - back_im * back_sin).reshape(2, groups, shards, slice_len)
    rot_im = (back_re * back_sin + back_im * back_cos).reshape(2, groups, shards, slice_len)
    rot_re, rot_im = (
        lax.all_to_all(
            lax.all_to_all(rot_re, "grp", split_axis=1, concat_axis=1, tiled=True),
            "shard",
            split_axis=2,
            concat_axis=2,
            tiled=True,
        ),
        lax.all_to_all(
            lax.all_to_all(rot_im, "grp", split_axis=1, concat_axis=1, tiled=True),
            "shard",
            split_axis=2,
            concat_axis=2,
            tiled=True,
        ),
    )
    rot_re = rot_re.reshape(span_len, slice_len)
    rot_im = rot_im.reshape(span_len, slice_len)
    values = (
        jnp.einsum("kd,kf->df", outer_cos, rot_re, precision=precise)
        - jnp.einsum("kd,kf->df", outer_sin, rot_im, precision=precise)
    ) / length
    values = values.reshape(groups, shards, slice_len)
    conv_rows = lax.all_to_all(
        lax.all_to_all(values, "grp", split_axis=0, concat_axis=0, tiled=True),
        "shard",
        split_axis=1,
        concat_axis=1,
        tiled=True,
    )
    conv = conv_rows.reshape(positions, channels)
    return (query * (conv + skip_gain * mixed)).astype(jnp.bfloat16)


MESH = pl.DeviceIdType.MESH
LANES = 128
SUB = 8
HALO = 8
REACH = 250.0
FAINT = 1e-30
MIX = 3
EARLY = 2
RIMS = ((1, 2), (0, 0))


def turned(value, numerator, denominator):
    numerator %= denominator
    real, imag = value
    eighths, rest = divmod(8 * numerator, denominator)
    if rest == 0:
        half = math.sqrt(0.5)
        if eighths == 0:
            return (real, imag)
        if eighths == 2:
            return (-imag, real)
        if eighths == 4:
            return (-real, -imag)
        if eighths == 6:
            return (imag, -real)
        if eighths == 1:
            return ((real - imag) * half, (real + imag) * half)
        if eighths == 3:
            return ((real + imag) * -half, (real - imag) * half)
        if eighths == 5:
            return ((imag - real) * half, (real + imag) * -half)
        return ((real + imag) * half, (imag - real) * half)
    angle = 2.0 * math.pi * numerator / denominator
    cos, sin = (math.cos(angle), math.sin(angle))
    return (real * cos - imag * sin, real * sin + imag * cos)


def fft(loads, sign):
    count = len(loads)
    if count == 1:
        return [loads[0]()]
    even, odd = (fft(loads[::2], sign), fft(loads[1::2], sign))
    low, high = ([], [])
    for k in range(count // 2):
        moved = turned(odd[k], sign * k, count)
        low.append((even[k][0] + moved[0], even[k][1] + moved[1]))
        high.append((even[k][0] - moved[0], even[k][1] - moved[1]))
    return low + high


def dot3(values, table_hi, table_lo):
    hi = values.astype(jnp.bfloat16)
    lo = (values - hi.astype(jnp.float32)).astype(jnp.bfloat16)
    dot = functools.partial(jnp.dot, preferred_element_type=jnp.float32)
    return dot(hi, table_hi[...]) + (dot(lo, table_hi[...]) + dot(hi, table_lo[...]))


def encoded(scaled):
    magnitude = jnp.exp2(jnp.abs(scaled) - REACH / 2)
    return jnp.where(scaled < 0, -magnitude, magnitude)


def decoded(code):
    wide = code.astype(jnp.float32)
    magnitude = jnp.log2(jnp.abs(wide)) + REACH / 2
    return jnp.where(wide < 0, -magnitude, magnitude)


def owner_kernel(
    sizes,
    proj_ref_far,
    taps_ref_far,
    filt_ref_far,
    gain_ref_far,
    fwd_hi_far,
    fwd_lo_far,
    inv_hi_far,
    inv_lo_far,
    twist_cos_far,
    twist_sin_far,
    out_ref,
    proj_ref,
    taps_ref,
    filt_ref,
    gain_ref,
    fwd_hi,
    fwd_lo,
    inv_hi,
    inv_lo,
    twist_cos,
    twist_sin,
    rim_out,
    rim_in,
    ext,
    query,
    mixed,
    filt_out,
    mix_out,
    conv_out,
    filt_in,
    mix_in,
    conv_in,
    mix_top,
    mix_tops,
    conv_top,
    conv_tops,
    columns,
    blocks,
    spec_a,
    spec_held,
    spec_g,
    own_filt,
    own_mix,
    first_filt,
    first_mix,
    load_sems,
    rim_sems,
    send_sems,
    recv_sems,
    first_sems,
):
    groups, shards, positions, channels, taps = sizes
    devices = groups * shards
    owned = channels // devices
    halves = owned // SUB
    per_chunk = LANES // owned
    chunks = channels // LANES
    bound = 6.0 / math.sqrt(devices * positions)
    my_group, my_shard = (lax.axis_index("grp"), lax.axis_index("shard"))
    me = my_group * shards + my_shard
    first_lane = lax.rem(me, per_chunk) * owned

    def partners(act):
        for apart in range(devices - 1, 0, -1):
            group = jnp.bitwise_xor(my_group, apart // shards)
            shard = jnp.bitwise_xor(my_shard, apart % shards)
            act((group, shard), group * shards + shard)

    def outward(act):
        layer = shards // 4
        for step in range(4):
            for low in range(2 * layer - 1, -1, -1):
                group = jnp.bitwise_xor(my_group, low // layer)
                shard = step * layer + jnp.bitwise_xor(lax.rem(my_shard, layer), low % layer)
                target = group * shards + shard
                yield_to = functools.partial(act, (group, shard), target)
                if low:
                    yield_to()
                else:
                    pl.when(target != me)(yield_to)

    def place(target):
        return (target // shards, target % shards)

    barrier = pltpu.get_barrier_semaphore()
    partners(
        lambda there, target: pl.semaphore_signal(
            barrier, inc=1, device_id=there, device_id_type=MESH
        )
    )

    far = (filt_ref_far, proj_ref_far, taps_ref_far, gain_ref_far, fwd_hi_far, fwd_lo_far)
    far += (inv_hi_far, inv_lo_far, twist_cos_far, twist_sin_far)
    near = (filt_ref, proj_ref, taps_ref, gain_ref, fwd_hi, fwd_lo)
    near += (inv_hi, inv_lo, twist_cos, twist_sin)
    loads = [
        pltpu.make_async_copy(source_ref, here_ref, load_sems.at[which])
        for which, (source_ref, here_ref) in enumerate(zip(far, near))
    ]
    for load in loads:
        load.start()

    def spread(chunk, block, stores):
        turned_block = block.T
        rows = owned // len(stores)
        for part in range(per_chunk):
            for which, store in enumerate(stores):
                first = part * owned + which * rows
                piece = turned_block[first : first + rows, :]
                store[chunk * per_chunk + part] = piece.astype(jnp.bfloat16)

    loads[0].wait()
    for chunk in range(chunks):
        lanes = slice(chunk * LANES, (chunk + 1) * LANES)
        spread(chunk, encoded(filt_ref[:, lanes] * (REACH / bound)), [filt_out])
    loads[1].wait()
    last = slice(positions - 16, positions)
    for pair in range(2):
        tails = [
            proj_ref[which, last, :].astype(jnp.float32)[8:]
            for which in RIMS[pair]
        ]
        rim_out[pair] = jnp.concatenate(tails, axis=0).astype(jnp.bfloat16)
    pl.semaphore_wait(barrier, devices - 1)

    rim_copies = [
        pltpu.make_async_remote_copy(
            src_ref=rim_out.at[pair],
            dst_ref=rim_in.at[pair],
            send_sem=rim_sems.at[0, pair],
            recv_sem=rim_sems.at[1, pair],
            device_id=place(lax.rem(me + 1, devices)),
            device_id_type=MESH,
        )
        for pair in range(2)
    ]

    def send_all(kind, source, landing, index=lambda target: target, first=0, last=False):
        def send(there, target):
            copy = pltpu.make_async_remote_copy(
                src_ref=source.at[index(target)],
                dst_ref=landing.at[me],
                send_sem=send_sems.at[kind],
                recv_sem=recv_sems.at[kind],
                device_id=there,
                device_id_type=MESH,
            )
            if first:
                @pl.when(target >= first)
                def _():
                    copy.start()
                    if last:
                        pltpu.make_async_remote_copy(
                            src_ref=conv_top.at[0],
                            dst_ref=conv_tops.at[me],
                            send_sem=send_sems.at[2],
                            recv_sem=recv_sems.at[2],
                            device_id=there,
                            device_id_type=MESH,
                        ).start()
            else:
                copy.start()

        (outward if first else partners)(send)
        landing[me] = source[index(me)]

    def wait_all(kind, landing, sems, count=devices - 1):
        others = landing.at[pl.ds(0, count)]
        pltpu.make_async_copy(others, others, sems.at[kind]).wait()

    rim_copies[0].start()
    send_all(0, filt_out, filt_in)

    for load in loads[2:]:
        load.wait()

    def shortened(which, chunk, begin, end):
        lanes = slice(chunk * LANES, (chunk + 1) * LANES)
        total = None
        for tap in range(taps):
            term = taps_ref[which, tap : tap + 1, lanes] * ext[
                which, chunk, HALO + begin - tap : HALO + end - tap, :
            ]
            total = term if total is None else total + term
        return total

    for chunk in range(chunks):
        lanes = slice(chunk * LANES, (chunk + 1) * LANES)
        for which in range(3):
            ext[which, chunk, HALO:, :] = proj_ref[which, :, lanes].astype(jnp.float32)
        mixed[chunk, HALO:, :] = shortened(1, chunk, HALO, positions) * shortened(
            2, chunk, HALO, positions
        )
    rim_copies[0].wait()
    keep = jnp.where(me > 0, 1.0, 0.0).astype(jnp.float32)
    for chunk in range(chunks):
        lanes = slice(chunk * LANES, (chunk + 1) * LANES)
        for part, which in enumerate(RIMS[0]):
            tail = rim_in[0, :, lanes].astype(jnp.float32)[part * 8 : part * 8 + 8]
            ext[which, chunk, HALO - 8 : HALO, :] = tail * keep
        mixed[chunk, :HALO, :] = shortened(1, chunk, 0, HALO) * shortened(2, chunk, 0, HALO)
        block = mixed[chunk]
        top = jnp.maximum(jnp.max(jnp.abs(block), axis=0, keepdims=True), FAINT)
        mix_top[chunk] = top * (1.0 / REACH)
        spread(chunk, encoded(block * (REACH / top)), [mix_out.at[half] for half in range(halves)])
    send_all(1, mix_top, mix_tops, lambda target: target // per_chunk)
    for half in range(halves):
        send_all(MIX + half, mix_out.at[half], mix_in.at[half])

    rim_copies[1].start()

    @pl.when(me < EARLY)
    def _():
        for chunk in range(chunks):
            lanes = slice(chunk * LANES, (chunk + 1) * LANES)
            own_filt[lanes, :] = filt_ref[:, lanes].T
            own_mix[lanes, :] = mixed[chunk].T

    first_copies = [
        pltpu.make_async_remote_copy(
            src_ref=source,
            dst_ref=landing,
            send_sem=first_sems.at[0, which],
            recv_sem=first_sems.at[1, which],
            device_id=place(jnp.bitwise_xor(me, 1)),
            device_id_type=MESH,
        )
        for which, (source, landing) in enumerate(((own_filt, first_filt), (own_mix, first_mix)))
    ]

    @pl.when(me == 0)
    def _():
        for copy in first_copies:
            copy.start()

    for chunk in range(chunks):
        lanes = slice(chunk * LANES, (chunk + 1) * LANES)
        mixed[chunk] = mixed[chunk] * gain_ref[:, lanes]

    def transform(half, level):
        def load(block):
            def get():
                value = blocks[half, block]
                angle = 2.0 * math.pi * block / (4 * devices)
                return (value * (level * math.cos(angle)), value * (level * math.sin(angle)))

            return get

        for k, (real, imag) in enumerate(fft([load(b) for b in range(devices)], 1)):
            cos, sin = (twist_cos[k : k + 1, :], twist_sin[k : k + 1, :])
            rows = slice(k * SUB, (k + 1) * SUB)
            spec_a[rows, :LANES] = real * cos - imag * sin
            spec_a[rows, LANES:] = real * sin + imag * cos
        return dot3(spec_a[...], fwd_hi, fwd_lo)

    wait_all(0, filt_in, recv_sems)
    for block in range(devices):
        value = decoded(filt_in[block])
        for half in range(halves):
            blocks[half, block] = value[half * SUB : (half + 1) * SUB, :]
    for half in range(halves):
        spec_held[half] = transform(half, bound / REACH)

    wait_all(1, mix_tops, recv_sems)
    columns[...] = jnp.zeros_like(columns)
    columns[:devices, :] = mix_tops[:, 0, :]
    columns[...] = columns[...].T
    own_tops = columns[pl.ds(pl.multiple_of(first_lane, owned), owned), :]
    rim_copies[1].wait()
    for chunk in range(chunks):
        lanes = slice(chunk * LANES, (chunk + 1) * LANES)
        ext[0, chunk, :HALO, :] = rim_in[1, :, lanes].astype(jnp.float32)[:HALO] * keep
        query[chunk] = shortened(0, chunk, 0, positions)

    row = lax.broadcasted_iota(jnp.int32, (SUB, LANES), 0) + first_lane
    lane = lax.broadcasted_iota(jnp.int32, (SUB, LANES), 1)
    top_row = None
    for half in range(halves):
        wait_all(MIX + half, mix_in.at[half], recv_sems)
        for block in range(devices):
            top = own_tops[half * SUB : (half + 1) * SUB, block : block + 1]
            blocks[half, block] = decoded(mix_in[half, block]) * top
        far_spec = transform(half, 1.0)
        far_re, far_im = (far_spec[:, :LANES], far_spec[:, LANES:])
        held_re, held_im = (spec_held[half, :, :LANES], spec_held[half, :, LANES:])
        spec_a[:, :LANES] = far_re * held_re - far_im * held_im
        spec_a[:, LANES:] = far_re * held_im + far_im * held_re
        spec_g[...] = dot3(spec_a[...], inv_hi, inv_lo)

        def load(k):
            def get():
                rows = slice(k * SUB, (k + 1) * SUB)
                real, imag = (spec_g[rows, :LANES], spec_g[rows, LANES:])
                cos, sin = (twist_cos[k : k + 1, :], twist_sin[k : k + 1, :])
                return (real * cos + imag * sin, imag * cos - real * sin)

            return get

        top = None
        for block, (real, imag) in enumerate(fft([load(k) for k in range(devices)], -1)):
            angle = 2.0 * math.pi * block / (4 * devices)
            value = real * math.cos(angle) + imag * math.sin(angle)
            blocks[half, block] = value
            top = jnp.abs(value) if top is None else jnp.maximum(top, jnp.abs(value))
        top = jnp.maximum(jnp.max(top, axis=1, keepdims=True), FAINT)
        ratio = REACH / top
        for block in range(devices):
            conv_out[half, block] = encoded(blocks[half, block] * ratio).astype(jnp.bfloat16)
        here = jnp.where(row + half * SUB == lane, top * (1.0 / REACH), 0.0)
        here = jnp.sum(here, axis=0, keepdims=True)
        top_row = here if top_row is None else top_row + here
        if half == halves - 1:
            conv_top[0] = top_row
            conv_tops[me] = top_row
            pass
        send_all(MIX + halves + half, conv_out.at[half], conv_in.at[half], first=EARLY, last=half == halves - 1)

    def store(chunk, conv):
        lanes = slice(chunk * LANES, (chunk + 1) * LANES)
        out_ref[:, lanes] = (query[chunk] * (conv + mixed[chunk])).astype(out_ref.dtype)

    @pl.when(me >= EARLY)
    def _():
        wait_all(2, conv_tops, recv_sems)
        for half in range(halves):
            wait_all(MIX + halves + half, conv_in.at[half], recv_sems)
            for block in range(devices):
                blocks[half, block] = decoded(conv_in[half, block])
        for chunk in range(chunks):
            owners = slice(chunk * per_chunk, (chunk + 1) * per_chunk)
            top = jnp.sum(conv_tops[owners, 0, :], axis=0, keepdims=True)
            pieces = [
                blocks[half, chunk * per_chunk + part]
                for part in range(per_chunk)
                for half in range(halves)
            ]
            store(chunk, jnp.concatenate(pieces, axis=0).T * top)
        wait_all(2, conv_tops, send_sems, devices - 1 - EARLY)
        for half in range(halves):
            wait_all(MIX + halves + half, conv_in.at[half], send_sems, devices - 1 - EARLY)

    @pl.when(me == 0)
    def _():
        for copy in first_copies:
            copy.wait_send()
        first_filt[...] = own_filt[...]
        first_mix[...] = jnp.zeros_like(first_mix)

    @pl.when(me == 1)
    def _():
        for copy in first_copies:
            copy.wait_recv()

    @pl.when(me < EARLY)
    def _():
        cos, sin = (twist_cos[devices : devices + 1, :], twist_sin[devices : devices + 1, :])

        def spectrum(source, rows):
            value = source[rows, :]
            return dot3(jnp.concatenate([value * cos, value * sin], axis=1), fwd_hi, fwd_lo)

        def product(left, right):
            left_re, left_im = (left[:, :LANES], left[:, LANES:])
            right_re, right_im = (right[:, :LANES], right[:, LANES:])
            return (left_re * right_re - left_im * right_im, left_re * right_im + left_im * right_re)

        for chunk in range(chunks):
            rows = slice(chunk * LANES, (chunk + 1) * LANES)
            filt_here, mix_here = (spectrum(own_filt, rows), spectrum(own_mix, rows))
            filt_first, mix_first = (spectrum(first_filt, rows), spectrum(first_mix, rows))
            near_re, near_im = product(mix_here, filt_first)
            cross_re, cross_im = product(mix_first, filt_here)
            over_re, over_im = product(mix_first, filt_first)
            total = jnp.concatenate(
                [near_re + cross_re + over_im, near_im + cross_im - over_re], axis=1
            )
            back = dot3(total, inv_hi, inv_lo) * float(devices)
            store(chunk, (back[:, :LANES] * cos + back[:, LANES:] * sin).T)
        wait_all(2, conv_tops, send_sems, devices - EARLY)
        for half in range(halves):
            wait_all(MIX + halves + half, conv_in.at[half], send_sems, devices - EARLY)

    wait_all(0, filt_out, send_sems)
    wait_all(1, mix_tops, send_sems)
    for half in range(halves):
        wait_all(MIX + half, mix_out.at[half], send_sems)


def split_table(table):
    hi = table.astype(jnp.bfloat16)
    lo = (table - hi.astype(np.float64)).astype(jnp.bfloat16)
    return hi, lo


def tables(devices, positions):
    p = np.arange(positions, dtype=np.float64)
    angle = 2.0 * np.pi * ((p[:, None] * p[None, :]) % positions) / positions
    cos, sin = (np.cos(angle), np.sin(angle))
    forward = np.block([[cos, sin], [-sin, cos]])
    backward = np.block([[cos, -sin], [sin, cos]]) / (devices * positions)
    k = np.arange(devices, dtype=np.float64)
    turns = np.append(k + 0.25, 0.25 * devices)
    twist = 2.0 * np.pi * turns[:, None] * p[None, :] / (devices * positions)
    return (
        *split_table(forward),
        *split_table(backward),
        np.cos(twist).astype(np.float32),
        np.sin(twist).astype(np.float32),
    )


def owned_channels(consts, groups, shards, projections, short_taps, long_filter, skip_gain):
    _, positions, channels = projections.shape
    devices = groups * shards
    owned = channels // devices
    halves = owned // SUB
    chunks = channels // LANES
    sizes = (groups, shards, positions, channels, short_taps.shape[1])
    f32, bf16 = (jnp.float32, jnp.bfloat16)
    operands = (projections, short_taps, long_filter, skip_gain.reshape(1, channels), *consts)
    slabs = pltpu.VMEM((devices, owned, LANES), bf16)
    halved = pltpu.VMEM((halves, devices, SUB, LANES), bf16)
    vmem = pl.BlockSpec(memory_space=pltpu.VMEM)
    return pl.pallas_call(
        functools.partial(owner_kernel, sizes),
        out_shape=jax.ShapeDtypeStruct((positions, channels), bf16),
        in_specs=[pl.BlockSpec(memory_space=pl.ANY)] * (4 + len(consts)),
        out_specs=vmem,
        scratch_shapes=[
            *(pltpu.VMEM(operand.shape, operand.dtype) for operand in operands),
            pltpu.VMEM((2, 16, channels), bf16),
            pltpu.VMEM((2, 16, channels), bf16),
            pltpu.VMEM((3, chunks, HALO + positions, LANES), f32),
            pltpu.VMEM((chunks, positions, LANES), f32),
            pltpu.VMEM((chunks, positions, LANES), f32),
            slabs,
            halved,
            halved,
            slabs,
            halved,
            halved,
            pltpu.VMEM((chunks, 1, LANES), f32),
            pltpu.VMEM((devices, 1, LANES), f32),
            pltpu.VMEM((1, 1, LANES), f32),
            pltpu.VMEM((devices, 1, LANES), f32),
            pltpu.VMEM((LANES, LANES), f32),
            pltpu.VMEM((halves, devices, SUB, LANES), f32),
            pltpu.VMEM((devices * SUB, 2 * LANES), f32),
            pltpu.VMEM((halves, devices * SUB, 2 * LANES), f32),
            pltpu.VMEM((devices * SUB, 2 * LANES), f32),
            *(pltpu.VMEM((channels, LANES), f32) for _ in range(4)),
            pltpu.SemaphoreType.DMA((len(operands),)),
            pltpu.SemaphoreType.DMA((2, 2)),
            pltpu.SemaphoreType.DMA((MIX + 2 * halves,)),
            pltpu.SemaphoreType.DMA((MIX + 2 * halves,)),
            pltpu.SemaphoreType.DMA((2, 2)),
        ],
        compiler_params=pltpu.CompilerParams(collective_id=0, has_side_effects=True, vmem_limit_bytes=12*1024*1024),
    )(*(pltpu.with_memory_space_constraint(o, pltpu.HBM) for o in operands))


def on_device(groups, shards, projections, short_taps, long_filter, skip_gain):
    _, positions, channels = projections.shape
    devices = groups * shards
    fits = (
        positions == LANES
        and channels % LANES == 0
        and channels % (SUB * devices) == 0
        and LANES % (channels // devices) == 0
        and devices & (devices - 1) == 0
        and (channels // devices) % 16 == 0
        and EARLY < devices <= LANES
        and groups == 2
        and shards % 4 == 0
        and short_taps.shape[1] <= HALO + 1
    )
    if not fits:
        return per_device(projections, short_taps, long_filter, skip_gain)
    consts = tables(devices, positions)
    return owned_channels(consts, groups, shards, projections, short_taps, long_filter, skip_gain)


def solution(mesh):
    placed = (P(None, ("grp", "shard"), None), P(), P(("grp", "shard"), None), P())
    body = functools.partial(on_device, mesh.shape["grp"], mesh.shape["shard"])
    return jax.shard_map(
        body, mesh=mesh, in_specs=placed, out_specs=P(("grp", "shard"), None), check_vma=False
    )
```

```python
import functools
import math

import jax
import jax.numpy as jnp
import numpy as np
from jax import lax
from jax.experimental import pallas as pl
from jax.experimental.pallas import tpu as pltpu
from jax.sharding import PartitionSpec as P

precise = lax.Precision.HIGHEST


def from_behind(block, axis, distance):
    devices = range(lax.axis_size(axis))
    route = [(i - distance, i) for i in devices if i - distance in devices]
    return lax.ppermute(block, axis, route)


def angles_of(first, second, modulus):
    return (first * second % modulus).astype(jnp.float32) * (2.0 * math.pi / modulus)


def per_device(projections, short_taps, long_filter, skip_gain):
    positions = projections.shape[1]
    channels = projections.shape[2]
    taps_count = short_taps.shape[1]
    groups = lax.axis_size("grp")
    shards = lax.axis_size("shard")
    devices = groups * shards
    span_len = 2 * devices
    length = span_len * positions
    slice_len = positions * channels // devices
    device_id = lax.axis_index("grp") * shards + lax.axis_index("shard")
    rim_rows = from_behind(projections[:, positions - (taps_count - 1) :, :], ("grp", "shard"), 1)
    extended = jnp.concatenate([rim_rows, projections], axis=1)
    shortened = short_taps[:, 0, None, :] * extended[
        :, taps_count - 1 : taps_count - 1 + positions, :
    ].astype(jnp.float32)
    for tap_index in range(1, taps_count):
        shortened = shortened + short_taps[:, tap_index, None, :] * extended[
            :, taps_count - 1 - tap_index : taps_count - 1 - tap_index + positions, :
        ].astype(jnp.float32)
    query = shortened[0]
    mixed = shortened[1] * shortened[2]
    mixed_rows = mixed.reshape(groups, shards, slice_len)
    filt_rows = long_filter.reshape(groups, shards, slice_len)
    got_mixed, got_filt = (
        lax.all_to_all(
            lax.all_to_all(mixed_rows, "grp", split_axis=0, concat_axis=0, tiled=True),
            "shard",
            split_axis=1,
            concat_axis=1,
            tiled=True,
        ),
        lax.all_to_all(
            lax.all_to_all(filt_rows, "grp", split_axis=0, concat_axis=0, tiled=True),
            "shard",
            split_axis=1,
            concat_axis=1,
            tiled=True,
        ),
    )
    dev_ids = jnp.arange(devices, dtype=jnp.int32)
    freq_ids = jnp.arange(span_len, dtype=jnp.int32)
    outer = angles_of(freq_ids[:, None], dev_ids[None, :], span_len)
    outer_cos, outer_sin = (jnp.cos(outer), jnp.sin(outer))
    flat_ids = device_id * slice_len + jnp.arange(slice_len, dtype=jnp.int32)
    row_of = flat_ids // channels
    twist = angles_of(freq_ids[:, None], row_of[None, :], length)
    twist_cos, twist_sin = (jnp.cos(twist), jnp.sin(twist))

    def forward_outer(values):
        flat_values = values.reshape(devices, slice_len)
        real = jnp.dot(outer_cos, flat_values, precision=precise)
        imag = -jnp.dot(outer_sin, flat_values, precision=precise)
        turned_re = real * twist_cos + imag * twist_sin
        turned_im = imag * twist_cos - real * twist_sin
        return (
            turned_re.reshape(2, groups, shards, slice_len),
            turned_im.reshape(2, groups, shards, slice_len),
        )

    mixed_re, mixed_im = forward_outer(got_mixed)
    filt_re, filt_im = forward_outer(got_filt)
    mixed_re, mixed_im, filt_re, filt_im = (
        lax.all_to_all(
            lax.all_to_all(mixed_re, "grp", split_axis=1, concat_axis=1, tiled=True),
            "shard",
            split_axis=2,
            concat_axis=2,
            tiled=True,
        ),
        lax.all_to_all(
            lax.all_to_all(mixed_im, "grp", split_axis=1, concat_axis=1, tiled=True),
            "shard",
            split_axis=2,
            concat_axis=2,
            tiled=True,
        ),
        lax.all_to_all(
            lax.all_to_all(filt_re, "grp", split_axis=1, concat_axis=1, tiled=True),
            "shard",
            split_axis=2,
            concat_axis=2,
            tiled=True,
        ),
        lax.all_to_all(
            lax.all_to_all(filt_im, "grp", split_axis=1, concat_axis=1, tiled=True),
            "shard",
            split_axis=2,
            concat_axis=2,
            tiled=True,
        ),
    )
    row_ids = jnp.arange(positions, dtype=jnp.int32)
    inner = angles_of(row_ids[:, None], row_ids[None, :], positions)
    inner_cos, inner_sin = (jnp.cos(inner), jnp.sin(inner))

    def forward_inner(real, imag):
        real = real.reshape(2, positions, channels)
        imag = imag.reshape(2, positions, channels)
        out_re = jnp.einsum("kp,rpc->rkc", inner_cos, real, precision=precise) + jnp.einsum(
            "kp,rpc->rkc", inner_sin, imag, precision=precise
        )
        out_im = jnp.einsum("kp,rpc->rkc", inner_cos, imag, precision=precise) - jnp.einsum(
            "kp,rpc->rkc", inner_sin, real, precision=precise
        )
        return (out_re, out_im)

    spec_mixed_re, spec_mixed_im = forward_inner(mixed_re, mixed_im)
    spec_filt_re, spec_filt_im = forward_inner(filt_re, filt_im)
    prod_re = spec_mixed_re * spec_filt_re - spec_mixed_im * spec_filt_im
    prod_im = spec_mixed_re * spec_filt_im + spec_mixed_im * spec_filt_re
    back_re = jnp.einsum("kp,rkc->rpc", inner_cos, prod_re, precision=precise) - jnp.einsum(
        "kp,rkc->rpc", inner_sin, prod_im, precision=precise
    )
    back_im = jnp.einsum("kp,rkc->rpc", inner_cos, prod_im, precision=precise) + jnp.einsum(
        "kp,rkc->rpc", inner_sin, prod_re, precision=precise
    )
    own_freqs = jnp.arange(2, dtype=jnp.int32) * devices + device_id
    back_twist = angles_of(own_freqs[:, None], row_ids[None, :], length)
    back_cos, back_sin = (jnp.cos(back_twist)[:, :, None], jnp.sin(back_twist)[:, :, None])
    rot_re = (back_re * back_cos - back_im * back_sin).reshape(2, groups, shards, slice_len)
    rot_im = (back_re * back_sin + back_im * back_cos).reshape(2, groups, shards, slice_len)
    rot_re, rot_im = (
        lax.all_to_all(
            lax.all_to_all(rot_re, "grp", split_axis=1, concat_axis=1, tiled=True),
            "shard",
            split_axis=2,
            concat_axis=2,
            tiled=True,
        ),
        lax.all_to_all(
            lax.all_to_all(rot_im, "grp", split_axis=1, concat_axis=1, tiled=True),
            "shard",
            split_axis=2,
            concat_axis=2,
            tiled=True,
        ),
    )
    rot_re = rot_re.reshape(span_len, slice_len)
    rot_im = rot_im.reshape(span_len, slice_len)
    values = (
        jnp.einsum("kd,kf->df", outer_cos, rot_re, precision=precise)
        - jnp.einsum("kd,kf->df", outer_sin, rot_im, precision=precise)
    ) / length
    values = values.reshape(groups, shards, slice_len)
    conv_rows = lax.all_to_all(
        lax.all_to_all(values, "grp", split_axis=0, concat_axis=0, tiled=True),
        "shard",
        split_axis=1,
        concat_axis=1,
        tiled=True,
    )
    conv = conv_rows.reshape(positions, channels)
    return (query * (conv + skip_gain * mixed)).astype(jnp.bfloat16)


MESH = pl.DeviceIdType.MESH
LANES = 128
SUB = 8
HALO = 8
REACH = 250.0
FAINT = 1e-30
MIX = 3
EARLY = 2
RIMS = ((1, 2), (0, 0))


def turned(value, numerator, denominator):
    numerator %= denominator
    real, imag = value
    eighths, rest = divmod(8 * numerator, denominator)
    if rest == 0:
        half = math.sqrt(0.5)
        if eighths == 0:
            return (real, imag)
        if eighths == 2:
            return (-imag, real)
        if eighths == 4:
            return (-real, -imag)
        if eighths == 6:
            return (imag, -real)
        if eighths == 1:
            return ((real - imag) * half, (real + imag) * half)
        if eighths == 3:
            return ((real + imag) * -half, (real - imag) * half)
        if eighths == 5:
            return ((imag - real) * half, (real + imag) * -half)
        return ((real + imag) * half, (imag - real) * half)
    angle = 2.0 * math.pi * numerator / denominator
    cos, sin = (math.cos(angle), math.sin(angle))
    return (real * cos - imag * sin, real * sin + imag * cos)


def fft(loads, sign):
    count = len(loads)
    if count == 1:
        return [loads[0]()]
    even, odd = (fft(loads[::2], sign), fft(loads[1::2], sign))
    low, high = ([], [])
    for k in range(count // 2):
        moved = turned(odd[k], sign * k, count)
        low.append((even[k][0] + moved[0], even[k][1] + moved[1]))
        high.append((even[k][0] - moved[0], even[k][1] - moved[1]))
    return low + high


def dot3(values, table_hi, table_lo):
    hi = values.astype(jnp.bfloat16)
    lo = (values - hi.astype(jnp.float32)).astype(jnp.bfloat16)
    dot = functools.partial(jnp.dot, preferred_element_type=jnp.float32)
    return dot(hi, table_hi[...]) + (dot(lo, table_hi[...]) + dot(hi, table_lo[...]))


def encoded(scaled):
    magnitude = jnp.exp2(jnp.abs(scaled) - REACH / 2)
    return jnp.where(scaled < 0, -magnitude, magnitude)


def decoded(code):
    wide = code.astype(jnp.float32)
    magnitude = jnp.log2(jnp.abs(wide)) + REACH / 2
    return jnp.where(wide < 0, -magnitude, magnitude)


def owner_kernel(
    sizes,
    proj_ref_far,
    taps_ref_far,
    filt_ref_far,
    gain_ref_far,
    fwd_hi_far,
    fwd_lo_far,
    inv_hi_far,
    inv_lo_far,
    twist_cos_far,
    twist_sin_far,
    out_ref,
    proj_ref,
    taps_ref,
    filt_ref,
    gain_ref,
    fwd_hi,
    fwd_lo,
    inv_hi,
    inv_lo,
    twist_cos,
    twist_sin,
    rim_out,
    rim_in,
    ext,
    query,
    mixed,
    filt_out,
    mix_out,
    conv_out,
    filt_in,
    mix_in,
    conv_in,
    mix_top,
    mix_tops,
    conv_top,
    conv_tops,
    columns,
    blocks,
    spec_a,
    spec_held,
    spec_g,
    own_filt,
    own_mix,
    first_filt,
    first_mix,
    load_sems,
    rim_sems,
    send_sems,
    recv_sems,
    first_sems,
):
    groups, shards, positions, channels, taps = sizes
    devices = groups * shards
    owned = channels // devices
    halves = owned // SUB
    per_chunk = LANES // owned
    chunks = channels // LANES
    bound = 6.0 / math.sqrt(devices * positions)
    my_group, my_shard = (lax.axis_index("grp"), lax.axis_index("shard"))
    me = my_group * shards + my_shard
    first_lane = lax.rem(me, per_chunk) * owned

    def partners(act, aparts=()):
        for apart in aparts or range(devices - 1, 0, -1):
            group = jnp.bitwise_xor(my_group, apart // shards)
            shard = jnp.bitwise_xor(my_shard, apart % shards)
            act((group, shard), group * shards + shard)

    def place(target):
        return (target // shards, target % shards)

    barrier = pltpu.get_barrier_semaphore()
    partners(
        lambda there, target: pl.semaphore_signal(
            barrier, inc=1, device_id=there, device_id_type=MESH
        )
    )

    far = (filt_ref_far, proj_ref_far, taps_ref_far, gain_ref_far, fwd_hi_far, fwd_lo_far)
    far += (inv_hi_far, inv_lo_far, twist_cos_far, twist_sin_far)
    near = (filt_ref, proj_ref, taps_ref, gain_ref, fwd_hi, fwd_lo)
    near += (inv_hi, inv_lo, twist_cos, twist_sin)
    loads = [
        pltpu.make_async_copy(source_ref, here_ref, load_sems.at[which])
        for which, (source_ref, here_ref) in enumerate(zip(far, near))
    ]
    for load in loads:
        load.start()

    def spread(chunk, block, stores):
        turned_block = block.T
        rows = owned // len(stores)
        for part in range(per_chunk):
            for which, store in enumerate(stores):
                first = part * owned + which * rows
                piece = turned_block[first : first + rows, :]
                store[chunk * per_chunk + part] = piece.astype(jnp.bfloat16)

    loads[0].wait()
    for chunk in range(chunks):
        lanes = slice(chunk * LANES, (chunk + 1) * LANES)
        spread(chunk, encoded(filt_ref[:, lanes] * (REACH / bound)), [filt_out])
    loads[1].wait()
    last = slice(positions - 16, positions)
    for pair in range(2):
        tails = [
            proj_ref[which, last, :].astype(jnp.float32)[8:]
            for which in RIMS[pair]
        ]
        rim_out[pair] = jnp.concatenate(tails, axis=0).astype(jnp.bfloat16)
    pl.semaphore_wait(barrier, devices - 1)

    rim_copies = [
        pltpu.make_async_remote_copy(
            src_ref=rim_out.at[pair],
            dst_ref=rim_in.at[pair],
            send_sem=rim_sems.at[0, pair],
            recv_sem=rim_sems.at[1, pair],
            device_id=place(lax.rem(me + 1, devices)),
            device_id_type=MESH,
        )
        for pair in range(2)
    ]

    def send_all(kind, source, landing, index=lambda target: target, first=0, aparts=()):
        def send(there, target):
            copy = pltpu.make_async_remote_copy(
                src_ref=source.at[index(target)],
                dst_ref=landing.at[me],
                send_sem=send_sems.at[kind],
                recv_sem=recv_sems.at[kind],
                device_id=there,
                device_id_type=MESH,
            )
            if first:
                pl.when(target >= first)(copy.start)
            else:
                copy.start()

        partners(send, aparts)
        landing[me] = source[index(me)]

    def wait_all(kind, landing, sems, count=devices - 1):
        others = landing.at[pl.ds(0, count)]
        pltpu.make_async_copy(others, others, sems.at[kind]).wait()

    for rim_copy in rim_copies:
        rim_copy.start()
    send_all(0, filt_out, filt_in, aparts=[a for a in range(devices - 1, 0, -1) if a & (shards // 2)])

    for load in loads[2:]:
        load.wait()

    def shortened(which, chunk, begin, end):
        lanes = slice(chunk * LANES, (chunk + 1) * LANES)
        total = None
        for tap in range(taps):
            term = taps_ref[which, tap : tap + 1, lanes] * ext[
                which, chunk, HALO + begin - tap : HALO + end - tap, :
            ]
            total = term if total is None else total + term
        return total

    for chunk in range(chunks):
        lanes = slice(chunk * LANES, (chunk + 1) * LANES)
        for which in range(3):
            ext[which, chunk, HALO:, :] = proj_ref[which, :, lanes].astype(jnp.float32)
        mixed[chunk, HALO:, :] = shortened(1, chunk, HALO, positions) * shortened(
            2, chunk, HALO, positions
        )
    for rim_copy in rim_copies:
        rim_copy.wait()
    keep = jnp.where(me > 0, 1.0, 0.0).astype(jnp.float32)
    for chunk in range(chunks):
        lanes = slice(chunk * LANES, (chunk + 1) * LANES)
        for which in range(3):
            pair = 0 if which in RIMS[0] else 1
            part = RIMS[pair].index(which)
            tail = rim_in[pair, :, lanes].astype(jnp.float32)[part * 8 : part * 8 + 8]
            ext[which, chunk, HALO - 8 : HALO, :] = tail * keep
        mixed[chunk, :HALO, :] = shortened(1, chunk, 0, HALO) * shortened(2, chunk, 0, HALO)
        block = mixed[chunk]
        top = jnp.maximum(jnp.max(jnp.abs(block), axis=0, keepdims=True), FAINT)
        mix_top[chunk] = top * (1.0 / REACH)
        spread(chunk, encoded(block * (REACH / top)), [mix_out.at[half] for half in range(halves)])
    send_all(1, mix_top, mix_tops, lambda target: target // per_chunk)
    for half in range(halves):
        send_all(MIX + half, mix_out.at[half], mix_in.at[half])
        if half == 0:
            send_all(0, filt_out, filt_in, aparts=[a for a in range(devices - 1, 0, -1) if not a & (shards // 2)])

    for chunk in range(chunks):
        query[chunk] = shortened(0, chunk, 0, positions)

    @pl.when(me < EARLY)
    def _():
        for chunk in range(chunks):
            lanes = slice(chunk * LANES, (chunk + 1) * LANES)
            own_filt[lanes, :] = filt_ref[:, lanes].T
            own_mix[lanes, :] = mixed[chunk].T

    first_copies = [
        pltpu.make_async_remote_copy(
            src_ref=source,
            dst_ref=landing,
            send_sem=first_sems.at[0, which],
            recv_sem=first_sems.at[1, which],
            device_id=place(jnp.bitwise_xor(me, 1)),
            device_id_type=MESH,
        )
        for which, (source, landing) in enumerate(((own_filt, first_filt), (own_mix, first_mix)))
    ]

    @pl.when(me == 0)
    def _():
        for copy in first_copies:
            copy.start()

    for chunk in range(chunks):
        lanes = slice(chunk * LANES, (chunk + 1) * LANES)
        mixed[chunk] = mixed[chunk] * gain_ref[:, lanes]

    def transform(half, level):
        def load(block):
            def get():
                value = blocks[half, block]
                angle = 2.0 * math.pi * block / (4 * devices)
                return (value * (level * math.cos(angle)), value * (level * math.sin(angle)))

            return get

        for k, (real, imag) in enumerate(fft([load(b) for b in range(devices)], 1)):
            cos, sin = (twist_cos[k : k + 1, :], twist_sin[k : k + 1, :])
            rows = slice(k * SUB, (k + 1) * SUB)
            spec_a[rows, :LANES] = real * cos - imag * sin
            spec_a[rows, LANES:] = real * sin + imag * cos
        return dot3(spec_a[...], fwd_hi, fwd_lo)

    wait_all(0, filt_in, recv_sems)
    for block in range(devices):
        value = decoded(filt_in[block])
        for half in range(halves):
            blocks[half, block] = value[half * SUB : (half + 1) * SUB, :]
    for half in range(halves):
        spec_held[half] = transform(half, bound / REACH)

    wait_all(1, mix_tops, recv_sems)
    columns[...] = jnp.zeros_like(columns)
    columns[:devices, :] = mix_tops[:, 0, :]
    columns[...] = columns[...].T
    own_tops = columns[pl.ds(pl.multiple_of(first_lane, owned), owned), :]
    row = lax.broadcasted_iota(jnp.int32, (SUB, LANES), 0) + first_lane
    lane = lax.broadcasted_iota(jnp.int32, (SUB, LANES), 1)
    top_row = None
    for half in range(halves):
        wait_all(MIX + half, mix_in.at[half], recv_sems)
        for block in range(devices):
            top = own_tops[half * SUB : (half + 1) * SUB, block : block + 1]
            blocks[half, block] = decoded(mix_in[half, block]) * top
        far_spec = transform(half, 1.0)
        far_re, far_im = (far_spec[:, :LANES], far_spec[:, LANES:])
        held_re, held_im = (spec_held[half, :, :LANES], spec_held[half, :, LANES:])
        spec_a[:, :LANES] = far_re * held_re - far_im * held_im
        spec_a[:, LANES:] = far_re * held_im + far_im * held_re
        spec_g[...] = dot3(spec_a[...], inv_hi, inv_lo)

        def load(k):
            def get():
                rows = slice(k * SUB, (k + 1) * SUB)
                real, imag = (spec_g[rows, :LANES], spec_g[rows, LANES:])
                cos, sin = (twist_cos[k : k + 1, :], twist_sin[k : k + 1, :])
                return (real * cos + imag * sin, imag * cos - real * sin)

            return get

        top = None
        for block, (real, imag) in enumerate(fft([load(k) for k in range(devices)], -1)):
            angle = 2.0 * math.pi * block / (4 * devices)
            value = real * math.cos(angle) + imag * math.sin(angle)
            blocks[half, block] = value
            top = jnp.abs(value) if top is None else jnp.maximum(top, jnp.abs(value))
        top = jnp.maximum(jnp.max(top, axis=1, keepdims=True), FAINT)
        ratio = REACH / top
        for block in range(devices):
            conv_out[half, block] = encoded(blocks[half, block] * ratio).astype(jnp.bfloat16)
        here = jnp.where(row + half * SUB == lane, top * (1.0 / REACH), 0.0)
        here = jnp.sum(here, axis=0, keepdims=True)
        top_row = here if top_row is None else top_row + here
        if half == halves - 1:
            conv_top[0] = top_row
            send_all(2, conv_top, conv_tops, lambda target: 0, EARLY)
        send_all(MIX + halves + half, conv_out.at[half], conv_in.at[half], first=EARLY)

    def store(chunk, conv):
        lanes = slice(chunk * LANES, (chunk + 1) * LANES)
        out_ref[:, lanes] = (query[chunk] * (conv + mixed[chunk])).astype(out_ref.dtype)

    @pl.when(me >= EARLY)
    def _():
        wait_all(2, conv_tops, recv_sems)
        for half in range(halves):
            wait_all(MIX + halves + half, conv_in.at[half], recv_sems)
            for block in range(devices):
                blocks[half, block] = decoded(conv_in[half, block])
        for chunk in range(chunks):
            owners = slice(chunk * per_chunk, (chunk + 1) * per_chunk)
            top = jnp.sum(conv_tops[owners, 0, :], axis=0, keepdims=True)
            pieces = [
                blocks[half, chunk * per_chunk + part]
                for part in range(per_chunk)
                for half in range(halves)
            ]
            store(chunk, jnp.concatenate(pieces, axis=0).T * top)
        wait_all(2, conv_tops, send_sems, devices - 1 - EARLY)
        for half in range(halves):
            wait_all(MIX + halves + half, conv_in.at[half], send_sems, devices - 1 - EARLY)

    @pl.when(me == 0)
    def _():
        for copy in first_copies:
            copy.wait_send()
        first_filt[...] = own_filt[...]
        first_mix[...] = jnp.zeros_like(first_mix)

    @pl.when(me == 1)
    def _():
        for copy in first_copies:
            copy.wait_recv()

    @pl.when(me < EARLY)
    def _():
        cos, sin = (twist_cos[devices : devices + 1, :], twist_sin[devices : devices + 1, :])

        def spectrum(source, rows):
            value = source[rows, :]
            return dot3(jnp.concatenate([value * cos, value * sin], axis=1), fwd_hi, fwd_lo)

        def product(left, right):
            left_re, left_im = (left[:, :LANES], left[:, LANES:])
            right_re, right_im = (right[:, :LANES], right[:, LANES:])
            return (left_re * right_re - left_im * right_im, left_re * right_im + left_im * right_re)

        for chunk in range(chunks):
            rows = slice(chunk * LANES, (chunk + 1) * LANES)
            filt_here, mix_here = (spectrum(own_filt, rows), spectrum(own_mix, rows))
            filt_first, mix_first = (spectrum(first_filt, rows), spectrum(first_mix, rows))
            near_re, near_im = product(mix_here, filt_first)
            cross_re, cross_im = product(mix_first, filt_here)
            over_re, over_im = product(mix_first, filt_first)
            total = jnp.concatenate(
                [near_re + cross_re + over_im, near_im + cross_im - over_re], axis=1
            )
            back = dot3(total, inv_hi, inv_lo) * float(devices)
            store(chunk, (back[:, :LANES] * cos + back[:, LANES:] * sin).T)
        wait_all(2, conv_tops, send_sems, devices - EARLY)
        for half in range(halves):
            wait_all(MIX + halves + half, conv_in.at[half], send_sems, devices - EARLY)

    wait_all(0, filt_out, send_sems)
    wait_all(1, mix_tops, send_sems)
    for half in range(halves):
        wait_all(MIX + half, mix_out.at[half], send_sems)


def split_table(table):
    hi = table.astype(jnp.bfloat16)
    lo = (table - hi.astype(np.float64)).astype(jnp.bfloat16)
    return hi, lo


def tables(devices, positions):
    p = np.arange(positions, dtype=np.float64)
    angle = 2.0 * np.pi * ((p[:, None] * p[None, :]) % positions) / positions
    cos, sin = (np.cos(angle), np.sin(angle))
    forward = np.block([[cos, sin], [-sin, cos]])
    backward = np.block([[cos, -sin], [sin, cos]]) / (devices * positions)
    k = np.arange(devices, dtype=np.float64)
    turns = np.append(k + 0.25, 0.25 * devices)
    twist = 2.0 * np.pi * turns[:, None] * p[None, :] / (devices * positions)
    return (
        *split_table(forward),
        *split_table(backward),
        np.cos(twist).astype(np.float32),
        np.sin(twist).astype(np.float32),
    )


def owned_channels(consts, groups, shards, projections, short_taps, long_filter, skip_gain):
    _, positions, channels = projections.shape
    devices = groups * shards
    owned = channels // devices
    halves = owned // SUB
    chunks = channels // LANES
    sizes = (groups, shards, positions, channels, short_taps.shape[1])
    f32, bf16 = (jnp.float32, jnp.bfloat16)
    operands = (projections, short_taps, long_filter, skip_gain.reshape(1, channels), *consts)
    slabs = pltpu.VMEM((devices, owned, LANES), bf16)
    halved = pltpu.VMEM((halves, devices, SUB, LANES), bf16)
    vmem = pl.BlockSpec(memory_space=pltpu.VMEM)
    return pl.pallas_call(
        functools.partial(owner_kernel, sizes),
        out_shape=jax.ShapeDtypeStruct((positions, channels), bf16),
        in_specs=[pl.BlockSpec(memory_space=pl.ANY)] * (4 + len(consts)),
        out_specs=vmem,
        scratch_shapes=[
            *(pltpu.VMEM(operand.shape, operand.dtype) for operand in operands),
            pltpu.VMEM((2, 16, channels), bf16),
            pltpu.VMEM((2, 16, channels), bf16),
            pltpu.VMEM((3, chunks, HALO + positions, LANES), f32),
            pltpu.VMEM((chunks, positions, LANES), f32),
            pltpu.VMEM((chunks, positions, LANES), f32),
            slabs,
            halved,
            halved,
            slabs,
            halved,
            halved,
            pltpu.VMEM((chunks, 1, LANES), f32),
            pltpu.VMEM((devices, 1, LANES), f32),
            pltpu.VMEM((1, 1, LANES), f32),
            pltpu.VMEM((devices, 1, LANES), f32),
            pltpu.VMEM((LANES, LANES), f32),
            pltpu.VMEM((halves, devices, SUB, LANES), f32),
            pltpu.VMEM((devices * SUB, 2 * LANES), f32),
            pltpu.VMEM((halves, devices * SUB, 2 * LANES), f32),
            pltpu.VMEM((devices * SUB, 2 * LANES), f32),
            *(pltpu.VMEM((channels, LANES), f32) for _ in range(4)),
            pltpu.SemaphoreType.DMA((len(operands),)),
            pltpu.SemaphoreType.DMA((2, 2)),
            pltpu.SemaphoreType.DMA((MIX + 2 * halves,)),
            pltpu.SemaphoreType.DMA((MIX + 2 * halves,)),
            pltpu.SemaphoreType.DMA((2, 2)),
        ],
        compiler_params=pltpu.CompilerParams(collective_id=0, has_side_effects=True, vmem_limit_bytes=16*1024*1024),
    )(*(pltpu.with_memory_space_constraint(o, pltpu.HBM) for o in operands))


def on_device(groups, shards, projections, short_taps, long_filter, skip_gain):
    _, positions, channels = projections.shape
    devices = groups * shards
    fits = (
        positions == LANES
        and channels % LANES == 0
        and channels % (SUB * devices) == 0
        and LANES % (channels // devices) == 0
        and devices & (devices - 1) == 0
        and (channels // devices) % 16 == 0
        and EARLY < devices <= LANES
        and short_taps.shape[1] <= HALO + 1
    )
    if not fits:
        return per_device(projections, short_taps, long_filter, skip_gain)
    consts = tables(devices, positions)
    return owned_channels(consts, groups, shards, projections, short_taps, long_filter, skip_gain)


def solution(mesh):
    placed = (P(None, ("grp", "shard"), None), P(), P(("grp", "shard"), None), P())
    body = functools.partial(on_device, mesh.shape["grp"], mesh.shape["shard"])
    return jax.shard_map(
        body, mesh=mesh, in_specs=placed, out_specs=P(("grp", "shard"), None), check_vma=False
    )
```

```python
import functools
import math

import jax
import jax.numpy as jnp
import numpy as np
from jax import lax
from jax.experimental import pallas as pl
from jax.experimental.pallas import tpu as pltpu
from jax.sharding import PartitionSpec as P

precise = lax.Precision.HIGHEST


def from_behind(block, axis, distance):
    devices = range(lax.axis_size(axis))
    route = [(i - distance, i) for i in devices if i - distance in devices]
    return lax.ppermute(block, axis, route)


def angles_of(first, second, modulus):
    return (first * second % modulus).astype(jnp.float32) * (2.0 * math.pi / modulus)


def per_device(projections, short_taps, long_filter, skip_gain):
    positions = projections.shape[1]
    channels = projections.shape[2]
    taps_count = short_taps.shape[1]
    groups = lax.axis_size("grp")
    shards = lax.axis_size("shard")
    devices = groups * shards
    span_len = 2 * devices
    length = span_len * positions
    slice_len = positions * channels // devices
    device_id = lax.axis_index("grp") * shards + lax.axis_index("shard")
    rim_rows = from_behind(projections[:, positions - (taps_count - 1) :, :], ("grp", "shard"), 1)
    extended = jnp.concatenate([rim_rows, projections], axis=1)
    shortened = short_taps[:, 0, None, :] * extended[
        :, taps_count - 1 : taps_count - 1 + positions, :
    ].astype(jnp.float32)
    for tap_index in range(1, taps_count):
        shortened = shortened + short_taps[:, tap_index, None, :] * extended[
            :, taps_count - 1 - tap_index : taps_count - 1 - tap_index + positions, :
        ].astype(jnp.float32)
    query = shortened[0]
    mixed = shortened[1] * shortened[2]
    mixed_rows = mixed.reshape(groups, shards, slice_len)
    filt_rows = long_filter.reshape(groups, shards, slice_len)
    got_mixed, got_filt = (
        lax.all_to_all(
            lax.all_to_all(mixed_rows, "grp", split_axis=0, concat_axis=0, tiled=True),
            "shard",
            split_axis=1,
            concat_axis=1,
            tiled=True,
        ),
        lax.all_to_all(
            lax.all_to_all(filt_rows, "grp", split_axis=0, concat_axis=0, tiled=True),
            "shard",
            split_axis=1,
            concat_axis=1,
            tiled=True,
        ),
    )
    dev_ids = jnp.arange(devices, dtype=jnp.int32)
    freq_ids = jnp.arange(span_len, dtype=jnp.int32)
    outer = angles_of(freq_ids[:, None], dev_ids[None, :], span_len)
    outer_cos, outer_sin = (jnp.cos(outer), jnp.sin(outer))
    flat_ids = device_id * slice_len + jnp.arange(slice_len, dtype=jnp.int32)
    row_of = flat_ids // channels
    twist = angles_of(freq_ids[:, None], row_of[None, :], length)
    twist_cos, twist_sin = (jnp.cos(twist), jnp.sin(twist))

    def forward_outer(values):
        flat_values = values.reshape(devices, slice_len)
        real = jnp.dot(outer_cos, flat_values, precision=precise)
        imag = -jnp.dot(outer_sin, flat_values, precision=precise)
        turned_re = real * twist_cos + imag * twist_sin
        turned_im = imag * twist_cos - real * twist_sin
        return (
            turned_re.reshape(2, groups, shards, slice_len),
            turned_im.reshape(2, groups, shards, slice_len),
        )

    mixed_re, mixed_im = forward_outer(got_mixed)
    filt_re, filt_im = forward_outer(got_filt)
    mixed_re, mixed_im, filt_re, filt_im = (
        lax.all_to_all(
            lax.all_to_all(mixed_re, "grp", split_axis=1, concat_axis=1, tiled=True),
            "shard",
            split_axis=2,
            concat_axis=2,
            tiled=True,
        ),
        lax.all_to_all(
            lax.all_to_all(mixed_im, "grp", split_axis=1, concat_axis=1, tiled=True),
            "shard",
            split_axis=2,
            concat_axis=2,
            tiled=True,
        ),
        lax.all_to_all(
            lax.all_to_all(filt_re, "grp", split_axis=1, concat_axis=1, tiled=True),
            "shard",
            split_axis=2,
            concat_axis=2,
            tiled=True,
        ),
        lax.all_to_all(
            lax.all_to_all(filt_im, "grp", split_axis=1, concat_axis=1, tiled=True),
            "shard",
            split_axis=2,
            concat_axis=2,
            tiled=True,
        ),
    )
    row_ids = jnp.arange(positions, dtype=jnp.int32)
    inner = angles_of(row_ids[:, None], row_ids[None, :], positions)
    inner_cos, inner_sin = (jnp.cos(inner), jnp.sin(inner))

    def forward_inner(real, imag):
        real = real.reshape(2, positions, channels)
        imag = imag.reshape(2, positions, channels)
        out_re = jnp.einsum("kp,rpc->rkc", inner_cos, real, precision=precise) + jnp.einsum(
            "kp,rpc->rkc", inner_sin, imag, precision=precise
        )
        out_im = jnp.einsum("kp,rpc->rkc", inner_cos, imag, precision=precise) - jnp.einsum(
            "kp,rpc->rkc", inner_sin, real, precision=precise
        )
        return (out_re, out_im)

    spec_mixed_re, spec_mixed_im = forward_inner(mixed_re, mixed_im)
    spec_filt_re, spec_filt_im = forward_inner(filt_re, filt_im)
    prod_re = spec_mixed_re * spec_filt_re - spec_mixed_im * spec_filt_im
    prod_im = spec_mixed_re * spec_filt_im + spec_mixed_im * spec_filt_re
    back_re = jnp.einsum("kp,rkc->rpc", inner_cos, prod_re, precision=precise) - jnp.einsum(
        "kp,rkc->rpc", inner_sin, prod_im, precision=precise
    )
    back_im = jnp.einsum("kp,rkc->rpc", inner_cos, prod_im, precision=precise) + jnp.einsum(
        "kp,rkc->rpc", inner_sin, prod_re, precision=precise
    )
    own_freqs = jnp.arange(2, dtype=jnp.int32) * devices + device_id
    back_twist = angles_of(own_freqs[:, None], row_ids[None, :], length)
    back_cos, back_sin = (jnp.cos(back_twist)[:, :, None], jnp.sin(back_twist)[:, :, None])
    rot_re = (back_re * back_cos - back_im * back_sin).reshape(2, groups, shards, slice_len)
    rot_im = (back_re * back_sin + back_im * back_cos).reshape(2, groups, shards, slice_len)
    rot_re, rot_im = (
        lax.all_to_all(
            lax.all_to_all(rot_re, "grp", split_axis=1, concat_axis=1, tiled=True),
            "shard",
            split_axis=2,
            concat_axis=2,
            tiled=True,
        ),
        lax.all_to_all(
            lax.all_to_all(rot_im, "grp", split_axis=1, concat_axis=1, tiled=True),
            "shard",
            split_axis=2,
            concat_axis=2,
            tiled=True,
        ),
    )
    rot_re = rot_re.reshape(span_len, slice_len)
    rot_im = rot_im.reshape(span_len, slice_len)
    values = (
        jnp.einsum("kd,kf->df", outer_cos, rot_re, precision=precise)
        - jnp.einsum("kd,kf->df", outer_sin, rot_im, precision=precise)
    ) / length
    values = values.reshape(groups, shards, slice_len)
    conv_rows = lax.all_to_all(
        lax.all_to_all(values, "grp", split_axis=0, concat_axis=0, tiled=True),
        "shard",
        split_axis=1,
        concat_axis=1,
        tiled=True,
    )
    conv = conv_rows.reshape(positions, channels)
    return (query * (conv + skip_gain * mixed)).astype(jnp.bfloat16)


MESH = pl.DeviceIdType.MESH
LANES = 128
SUB = 8
HALO = 8
REACH = 250.0
FAINT = 1e-30
MIX = 3
EARLY = 2
RIMS = ((1, 2), (0, 0))


def turned(value, numerator, denominator):
    numerator %= denominator
    real, imag = value
    eighths, rest = divmod(8 * numerator, denominator)
    if rest == 0:
        half = math.sqrt(0.5)
        if eighths == 0:
            return (real, imag)
        if eighths == 2:
            return (-imag, real)
        if eighths == 4:
            return (-real, -imag)
        if eighths == 6:
            return (imag, -real)
        if eighths == 1:
            return ((real - imag) * half, (real + imag) * half)
        if eighths == 3:
            return ((real + imag) * -half, (real - imag) * half)
        if eighths == 5:
            return ((imag - real) * half, (real + imag) * -half)
        return ((real + imag) * half, (imag - real) * half)
    angle = 2.0 * math.pi * numerator / denominator
    cos, sin = (math.cos(angle), math.sin(angle))
    return (real * cos - imag * sin, real * sin + imag * cos)


def fft(loads, sign):
    count = len(loads)
    if count == 1:
        return [loads[0]()]
    even, odd = (fft(loads[::2], sign), fft(loads[1::2], sign))
    low, high = ([], [])
    for k in range(count // 2):
        moved = turned(odd[k], sign * k, count)
        low.append((even[k][0] + moved[0], even[k][1] + moved[1]))
        high.append((even[k][0] - moved[0], even[k][1] - moved[1]))
    return low + high


def dot3(values, table_hi, table_lo):
    hi = values.astype(jnp.bfloat16)
    lo = (values - hi.astype(jnp.float32)).astype(jnp.bfloat16)
    dot = functools.partial(jnp.dot, preferred_element_type=jnp.float32)
    return dot(hi, table_hi[...]) + (dot(lo, table_hi[...]) + dot(hi, table_lo[...]))


def encoded(scaled):
    magnitude = jnp.exp2(jnp.abs(scaled) - REACH / 2)
    return jnp.where(scaled < 0, -magnitude, magnitude)


def decoded(code):
    wide = code.astype(jnp.float32)
    magnitude = jnp.log2(jnp.abs(wide)) + REACH / 2
    return jnp.where(wide < 0, -magnitude, magnitude)


def owner_kernel(
    sizes,
    proj_ref_far,
    taps_ref_far,
    filt_ref_far,
    gain_ref_far,
    fwd_hi_far,
    fwd_lo_far,
    inv_hi_far,
    inv_lo_far,
    twist_cos_far,
    twist_sin_far,
    out_ref,
    proj_ref,
    taps_ref,
    filt_ref,
    gain_ref,
    fwd_hi,
    fwd_lo,
    inv_hi,
    inv_lo,
    twist_cos,
    twist_sin,
    rim_out,
    rim_in,
    ext,
    query,
    mixed,
    filt_out,
    mix_out,
    conv_out,
    filt_in,
    mix_in,
    conv_in,
    mix_top,
    mix_tops,
    conv_top,
    conv_tops,
    columns,
    blocks,
    spec_a,
    spec_held,
    spec_g,
    own_filt,
    own_mix,
    first_filt,
    first_mix,
    load_sems,
    rim_sems,
    send_sems,
    recv_sems,
    first_sems,
):
    groups, shards, positions, channels, taps = sizes
    devices = groups * shards
    owned = channels // devices
    halves = owned // SUB
    per_chunk = LANES // owned
    chunks = channels // LANES
    bound = 6.0 / math.sqrt(devices * positions)
    my_group, my_shard = (lax.axis_index("grp"), lax.axis_index("shard"))
    me = my_group * shards + my_shard
    first_lane = lax.rem(me, per_chunk) * owned

    def partners(act, aparts=()):
        for apart in aparts or range(devices - 1, 0, -1):
            group = jnp.bitwise_xor(my_group, apart // shards)
            shard = jnp.bitwise_xor(my_shard, apart % shards)
            act((group, shard), group * shards + shard)

    def place(target):
        return (target // shards, target % shards)

    barrier = pltpu.get_barrier_semaphore()
    partners(
        lambda there, target: pl.semaphore_signal(
            barrier, inc=1, device_id=there, device_id_type=MESH
        )
    )

    far = (filt_ref_far, proj_ref_far, taps_ref_far, gain_ref_far, fwd_hi_far, fwd_lo_far)
    far += (inv_hi_far, inv_lo_far, twist_cos_far, twist_sin_far)
    near = (filt_ref, proj_ref, taps_ref, gain_ref, fwd_hi, fwd_lo)
    near += (inv_hi, inv_lo, twist_cos, twist_sin)
    loads = [
        pltpu.make_async_copy(source_ref, here_ref, load_sems.at[which])
        for which, (source_ref, here_ref) in enumerate(zip(far, near))
    ]
    for load in loads:
        load.start()

    def spread(chunk, block, stores):
        turned_block = block.T
        rows = owned // len(stores)
        for part in range(per_chunk):
            for which, store in enumerate(stores):
                first = part * owned + which * rows
                piece = turned_block[first : first + rows, :]
                store[chunk * per_chunk + part] = piece.astype(jnp.bfloat16)

    loads[0].wait()
    for chunk in range(chunks):
        lanes = slice(chunk * LANES, (chunk + 1) * LANES)
        spread(chunk, encoded(filt_ref[:, lanes] * (REACH / bound)), [filt_out])
    loads[1].wait()
    last = slice(positions - 16, positions)
    for pair in range(2):
        tails = [
            proj_ref[which, last, :].astype(jnp.float32)[8:]
            for which in RIMS[pair]
        ]
        rim_out[pair] = jnp.concatenate(tails, axis=0).astype(jnp.bfloat16)
    pl.semaphore_wait(barrier, devices - 1)

    rim_copies = [
        pltpu.make_async_remote_copy(
            src_ref=rim_out.at[pair],
            dst_ref=rim_in.at[pair],
            send_sem=rim_sems.at[0, pair],
            recv_sem=rim_sems.at[1, pair],
            device_id=place(lax.rem(me + 1, devices)),
            device_id_type=MESH,
        )
        for pair in range(2)
    ]

    def send_all(kind, source, landing, index=lambda target: target, first=0, aparts=()):
        def send(there, target):
            copy = pltpu.make_async_remote_copy(
                src_ref=source.at[index(target)],
                dst_ref=landing.at[me],
                send_sem=send_sems.at[kind],
                recv_sem=recv_sems.at[kind],
                device_id=there,
                device_id_type=MESH,
            )
            if first:
                pl.when(target >= first)(copy.start)
            else:
                copy.start()

        partners(send, aparts)
        landing[me] = source[index(me)]

    def wait_all(kind, landing, sems, count=devices - 1):
        others = landing.at[pl.ds(0, count)]
        pltpu.make_async_copy(others, others, sems.at[kind]).wait()

    for rim_copy in rim_copies:
        rim_copy.start()
    send_all(0, filt_out, filt_in, aparts=[a for a in range(devices - 1, 0, -1) if a & (shards // 2)])

    for load in loads[2:]:
        load.wait()

    def shortened(which, chunk, begin, end):
        lanes = slice(chunk * LANES, (chunk + 1) * LANES)
        total = None
        for tap in range(taps):
            term = taps_ref[which, tap : tap + 1, lanes] * ext[
                which, chunk, HALO + begin - tap : HALO + end - tap, :
            ]
            total = term if total is None else total + term
        return total

    for chunk in range(chunks):
        lanes = slice(chunk * LANES, (chunk + 1) * LANES)
        for which in range(3):
            ext[which, chunk, HALO:, :] = proj_ref[which, :, lanes].astype(jnp.float32)
        mixed[chunk, HALO:, :] = shortened(1, chunk, HALO, positions) * shortened(
            2, chunk, HALO, positions
        )
    for rim_copy in rim_copies:
        rim_copy.wait()
    keep = jnp.where(me > 0, 1.0, 0.0).astype(jnp.float32)
    for chunk in range(chunks):
        lanes = slice(chunk * LANES, (chunk + 1) * LANES)
        for which in range(3):
            pair = 0 if which in RIMS[0] else 1
            part = RIMS[pair].index(which)
            tail = rim_in[pair, :, lanes].astype(jnp.float32)[part * 8 : part * 8 + 8]
            ext[which, chunk, HALO - 8 : HALO, :] = tail * keep
        mixed[chunk, :HALO, :] = shortened(1, chunk, 0, HALO) * shortened(2, chunk, 0, HALO)
        block = mixed[chunk]
        top = jnp.maximum(jnp.max(jnp.abs(block), axis=0, keepdims=True), FAINT)
        mix_top[chunk] = top * (1.0 / REACH)
        spread(chunk, encoded(block * (REACH / top)), [mix_out.at[half] for half in range(halves)])
    send_all(1, mix_top, mix_tops, lambda target: target // per_chunk)
    across = [a for a in range(devices - 1, 0, -1) if a & (shards // 2)]
    within = [a for a in range(devices - 1, 0, -1) if not a & (shards // 2)]
    for half in range(halves):
        send_all(MIX + half, mix_out.at[half], mix_in.at[half], aparts=across)
        if half == 0:
            send_all(0, filt_out, filt_in, aparts=within)
        send_all(MIX + half, mix_out.at[half], mix_in.at[half], aparts=within)

    for chunk in range(chunks):
        query[chunk] = shortened(0, chunk, 0, positions)

    @pl.when(me < EARLY)
    def _():
        for chunk in range(chunks):
            lanes = slice(chunk * LANES, (chunk + 1) * LANES)
            own_filt[lanes, :] = filt_ref[:, lanes].T
            own_mix[lanes, :] = mixed[chunk].T

    first_copies = [
        pltpu.make_async_remote_copy(
            src_ref=source,
            dst_ref=landing,
            send_sem=first_sems.at[0, which],
            recv_sem=first_sems.at[1, which],
            device_id=place(jnp.bitwise_xor(me, 1)),
            device_id_type=MESH,
        )
        for which, (source, landing) in enumerate(((own_filt, first_filt), (own_mix, first_mix)))
    ]

    @pl.when(me == 0)
    def _():
        for copy in first_copies:
            copy.start()

    for chunk in range(chunks):
        lanes = slice(chunk * LANES, (chunk + 1) * LANES)
        mixed[chunk] = mixed[chunk] * gain_ref[:, lanes]

    def transform(half, level):
        def load(block):
            def get():
                value = blocks[half, block]
                angle = 2.0 * math.pi * block / (4 * devices)
                return (value * (level * math.cos(angle)), value * (level * math.sin(angle)))

            return get

        for k, (real, imag) in enumerate(fft([load(b) for b in range(devices)], 1)):
            cos, sin = (twist_cos[k : k + 1, :], twist_sin[k : k + 1, :])
            rows = slice(k * SUB, (k + 1) * SUB)
            spec_a[rows, :LANES] = real * cos - imag * sin
            spec_a[rows, LANES:] = real * sin + imag * cos
        return dot3(spec_a[...], fwd_hi, fwd_lo)

    wait_all(0, filt_in, recv_sems)
    for block in range(devices):
        value = decoded(filt_in[block])
        for half in range(halves):
            blocks[half, block] = value[half * SUB : (half + 1) * SUB, :]
    for half in range(halves):
        spec_held[half] = transform(half, bound / REACH)

    wait_all(1, mix_tops, recv_sems)
    columns[...] = jnp.zeros_like(columns)
    columns[:devices, :] = mix_tops[:, 0, :]
    columns[...] = columns[...].T
    own_tops = columns[pl.ds(pl.multiple_of(first_lane, owned), owned), :]
    row = lax.broadcasted_iota(jnp.int32, (SUB, LANES), 0) + first_lane
    lane = lax.broadcasted_iota(jnp.int32, (SUB, LANES), 1)
    top_row = None
    for half in range(halves):
        wait_all(MIX + half, mix_in.at[half], recv_sems)
        for block in range(devices):
            top = own_tops[half * SUB : (half + 1) * SUB, block : block + 1]
            blocks[half, block] = decoded(mix_in[half, block]) * top
        far_spec = transform(half, 1.0)
        far_re, far_im = (far_spec[:, :LANES], far_spec[:, LANES:])
        held_re, held_im = (spec_held[half, :, :LANES], spec_held[half, :, LANES:])
        spec_a[:, :LANES] = far_re * held_re - far_im * held_im
        spec_a[:, LANES:] = far_re * held_im + far_im * held_re
        spec_g[...] = dot3(spec_a[...], inv_hi, inv_lo)

        def load(k):
            def get():
                rows = slice(k * SUB, (k + 1) * SUB)
                real, imag = (spec_g[rows, :LANES], spec_g[rows, LANES:])
                cos, sin = (twist_cos[k : k + 1, :], twist_sin[k : k + 1, :])
                return (real * cos + imag * sin, imag * cos - real * sin)

            return get

        top = None
        for block, (real, imag) in enumerate(fft([load(k) for k in range(devices)], -1)):
            angle = 2.0 * math.pi * block / (4 * devices)
            value = real * math.cos(angle) + imag * math.sin(angle)
            blocks[half, block] = value
            top = jnp.abs(value) if top is None else jnp.maximum(top, jnp.abs(value))
        top = jnp.maximum(jnp.max(top, axis=1, keepdims=True), FAINT)
        ratio = REACH / top
        for block in range(devices):
            conv_out[half, block] = encoded(blocks[half, block] * ratio).astype(jnp.bfloat16)
        here = jnp.where(row + half * SUB == lane, top * (1.0 / REACH), 0.0)
        here = jnp.sum(here, axis=0, keepdims=True)
        top_row = here if top_row is None else top_row + here
        if half == halves - 1:
            conv_top[0] = top_row
            send_all(2, conv_top, conv_tops, lambda target: 0, EARLY)
        send_all(MIX + halves + half, conv_out.at[half], conv_in.at[half], first=EARLY)

    def store(chunk, conv):
        lanes = slice(chunk * LANES, (chunk + 1) * LANES)
        out_ref[:, lanes] = (query[chunk] * (conv + mixed[chunk])).astype(out_ref.dtype)

    @pl.when(me >= EARLY)
    def _():
        wait_all(2, conv_tops, recv_sems)
        for half in range(halves):
            wait_all(MIX + halves + half, conv_in.at[half], recv_sems)
            for block in range(devices):
                blocks[half, block] = decoded(conv_in[half, block])
        for chunk in range(chunks):
            owners = slice(chunk * per_chunk, (chunk + 1) * per_chunk)
            top = jnp.sum(conv_tops[owners, 0, :], axis=0, keepdims=True)
            pieces = [
                blocks[half, chunk * per_chunk + part]
                for part in range(per_chunk)
                for half in range(halves)
            ]
            store(chunk, jnp.concatenate(pieces, axis=0).T * top)
        wait_all(2, conv_tops, send_sems, devices - 1 - EARLY)
        for half in range(halves):
            wait_all(MIX + halves + half, conv_in.at[half], send_sems, devices - 1 - EARLY)

    @pl.when(me == 0)
    def _():
        for copy in first_copies:
            copy.wait_send()
        first_filt[...] = own_filt[...]
        first_mix[...] = jnp.zeros_like(first_mix)

    @pl.when(me == 1)
    def _():
        for copy in first_copies:
            copy.wait_recv()

    @pl.when(me < EARLY)
    def _():
        cos, sin = (twist_cos[devices : devices + 1, :], twist_sin[devices : devices + 1, :])

        def spectrum(source, rows):
            value = source[rows, :]
            return dot3(jnp.concatenate([value * cos, value * sin], axis=1), fwd_hi, fwd_lo)

        def product(left, right):
            left_re, left_im = (left[:, :LANES], left[:, LANES:])
            right_re, right_im = (right[:, :LANES], right[:, LANES:])
            return (left_re * right_re - left_im * right_im, left_re * right_im + left_im * right_re)

        for chunk in range(chunks):
            rows = slice(chunk * LANES, (chunk + 1) * LANES)
            filt_here, mix_here = (spectrum(own_filt, rows), spectrum(own_mix, rows))
            filt_first, mix_first = (spectrum(first_filt, rows), spectrum(first_mix, rows))
            near_re, near_im = product(mix_here, filt_first)
            cross_re, cross_im = product(mix_first, filt_here)
            over_re, over_im = product(mix_first, filt_first)
            total = jnp.concatenate(
                [near_re + cross_re + over_im, near_im + cross_im - over_re], axis=1
            )
            back = dot3(total, inv_hi, inv_lo) * float(devices)
            store(chunk, (back[:, :LANES] * cos + back[:, LANES:] * sin).T)
        wait_all(2, conv_tops, send_sems, devices - EARLY)
        for half in range(halves):
            wait_all(MIX + halves + half, conv_in.at[half], send_sems, devices - EARLY)

    wait_all(0, filt_out, send_sems)
    wait_all(1, mix_tops, send_sems)
    for half in range(halves):
        wait_all(MIX + half, mix_out.at[half], send_sems)


def split_table(table):
    hi = table.astype(jnp.bfloat16)
    lo = (table - hi.astype(np.float64)).astype(jnp.bfloat16)
    return hi, lo


def tables(devices, positions):
    p = np.arange(positions, dtype=np.float64)
    angle = 2.0 * np.pi * ((p[:, None] * p[None, :]) % positions) / positions
    cos, sin = (np.cos(angle), np.sin(angle))
    forward = np.block([[cos, sin], [-sin, cos]])
    backward = np.block([[cos, -sin], [sin, cos]]) / (devices * positions)
    k = np.arange(devices, dtype=np.float64)
    turns = np.append(k + 0.25, 0.25 * devices)
    twist = 2.0 * np.pi * turns[:, None] * p[None, :] / (devices * positions)
    return (
        *split_table(forward),
        *split_table(backward),
        np.cos(twist).astype(np.float32),
        np.sin(twist).astype(np.float32),
    )


def owned_channels(consts, groups, shards, projections, short_taps, long_filter, skip_gain):
    _, positions, channels = projections.shape
    devices = groups * shards
    owned = channels // devices
    halves = owned // SUB
    chunks = channels // LANES
    sizes = (groups, shards, positions, channels, short_taps.shape[1])
    f32, bf16 = (jnp.float32, jnp.bfloat16)
    operands = (projections, short_taps, long_filter, skip_gain.reshape(1, channels), *consts)
    slabs = pltpu.VMEM((devices, owned, LANES), bf16)
    halved = pltpu.VMEM((halves, devices, SUB, LANES), bf16)
    vmem = pl.BlockSpec(memory_space=pltpu.VMEM)
    return pl.pallas_call(
        functools.partial(owner_kernel, sizes),
        out_shape=jax.ShapeDtypeStruct((positions, channels), bf16),
        in_specs=[pl.BlockSpec(memory_space=pl.ANY)] * (4 + len(consts)),
        out_specs=vmem,
        scratch_shapes=[
            *(pltpu.VMEM(operand.shape, operand.dtype) for operand in operands),
            pltpu.VMEM((2, 16, channels), bf16),
            pltpu.VMEM((2, 16, channels), bf16),
            pltpu.VMEM((3, chunks, HALO + positions, LANES), f32),
            pltpu.VMEM((chunks, positions, LANES), f32),
            pltpu.VMEM((chunks, positions, LANES), f32),
            slabs,
            halved,
            halved,
            slabs,
            halved,
            halved,
            pltpu.VMEM((chunks, 1, LANES), f32),
            pltpu.VMEM((devices, 1, LANES), f32),
            pltpu.VMEM((1, 1, LANES), f32),
            pltpu.VMEM((devices, 1, LANES), f32),
            pltpu.VMEM((LANES, LANES), f32),
            pltpu.VMEM((halves, devices, SUB, LANES), f32),
            pltpu.VMEM((devices * SUB, 2 * LANES), f32),
            pltpu.VMEM((halves, devices * SUB, 2 * LANES), f32),
            pltpu.VMEM((devices * SUB, 2 * LANES), f32),
            *(pltpu.VMEM((channels, LANES), f32) for _ in range(4)),
            pltpu.SemaphoreType.DMA((len(operands),)),
            pltpu.SemaphoreType.DMA((2, 2)),
            pltpu.SemaphoreType.DMA((MIX + 2 * halves,)),
            pltpu.SemaphoreType.DMA((MIX + 2 * halves,)),
            pltpu.SemaphoreType.DMA((2, 2)),
        ],
        compiler_params=pltpu.CompilerParams(collective_id=0, has_side_effects=True, vmem_limit_bytes=16*1024*1024),
    )(*(pltpu.with_memory_space_constraint(o, pltpu.HBM) for o in operands))


def on_device(groups, shards, projections, short_taps, long_filter, skip_gain):
    _, positions, channels = projections.shape
    devices = groups * shards
    fits = (
        positions == LANES
        and channels % LANES == 0
        and channels % (SUB * devices) == 0
        and LANES % (channels // devices) == 0
        and devices & (devices - 1) == 0
        and (channels // devices) % 16 == 0
        and EARLY < devices <= LANES
        and short_taps.shape[1] <= HALO + 1
    )
    if not fits:
        return per_device(projections, short_taps, long_filter, skip_gain)
    consts = tables(devices, positions)
    return owned_channels(consts, groups, shards, projections, short_taps, long_filter, skip_gain)


def solution(mesh):
    placed = (P(None, ("grp", "shard"), None), P(), P(("grp", "shard"), None), P())
    body = functools.partial(on_device, mesh.shape["grp"], mesh.shape["shard"])
    return jax.shard_map(
        body, mesh=mesh, in_specs=placed, out_specs=P(("grp", "shard"), None), check_vma=False
    )
```

```python
import functools
import math

import jax
import jax.numpy as jnp
import numpy as np
from jax import lax
from jax.experimental import pallas as pl
from jax.experimental.pallas import tpu as pltpu
from jax.sharding import PartitionSpec as P

precise = lax.Precision.HIGHEST


def from_behind(block, axis, distance):
    devices = range(lax.axis_size(axis))
    route = [(i - distance, i) for i in devices if i - distance in devices]
    return lax.ppermute(block, axis, route)


def angles_of(first, second, modulus):
    return (first * second % modulus).astype(jnp.float32) * (2.0 * math.pi / modulus)


def per_device(projections, short_taps, long_filter, skip_gain):
    positions = projections.shape[1]
    channels = projections.shape[2]
    taps_count = short_taps.shape[1]
    groups = lax.axis_size("grp")
    shards = lax.axis_size("shard")
    devices = groups * shards
    span_len = 2 * devices
    length = span_len * positions
    slice_len = positions * channels // devices
    device_id = lax.axis_index("grp") * shards + lax.axis_index("shard")
    rim_rows = from_behind(projections[:, positions - (taps_count - 1) :, :], ("grp", "shard"), 1)
    extended = jnp.concatenate([rim_rows, projections], axis=1)
    shortened = short_taps[:, 0, None, :] * extended[
        :, taps_count - 1 : taps_count - 1 + positions, :
    ].astype(jnp.float32)
    for tap_index in range(1, taps_count):
        shortened = shortened + short_taps[:, tap_index, None, :] * extended[
            :, taps_count - 1 - tap_index : taps_count - 1 - tap_index + positions, :
        ].astype(jnp.float32)
    query = shortened[0]
    mixed = shortened[1] * shortened[2]
    mixed_rows = mixed.reshape(groups, shards, slice_len)
    filt_rows = long_filter.reshape(groups, shards, slice_len)
    got_mixed, got_filt = (
        lax.all_to_all(
            lax.all_to_all(mixed_rows, "grp", split_axis=0, concat_axis=0, tiled=True),
            "shard",
            split_axis=1,
            concat_axis=1,
            tiled=True,
        ),
        lax.all_to_all(
            lax.all_to_all(filt_rows, "grp", split_axis=0, concat_axis=0, tiled=True),
            "shard",
            split_axis=1,
            concat_axis=1,
            tiled=True,
        ),
    )
    dev_ids = jnp.arange(devices, dtype=jnp.int32)
    freq_ids = jnp.arange(span_len, dtype=jnp.int32)
    outer = angles_of(freq_ids[:, None], dev_ids[None, :], span_len)
    outer_cos, outer_sin = (jnp.cos(outer), jnp.sin(outer))
    flat_ids = device_id * slice_len + jnp.arange(slice_len, dtype=jnp.int32)
    row_of = flat_ids // channels
    twist = angles_of(freq_ids[:, None], row_of[None, :], length)
    twist_cos, twist_sin = (jnp.cos(twist), jnp.sin(twist))

    def forward_outer(values):
        flat_values = values.reshape(devices, slice_len)
        real = jnp.dot(outer_cos, flat_values, precision=precise)
        imag = -jnp.dot(outer_sin, flat_values, precision=precise)
        turned_re = real * twist_cos + imag * twist_sin
        turned_im = imag * twist_cos - real * twist_sin
        return (
            turned_re.reshape(2, groups, shards, slice_len),
            turned_im.reshape(2, groups, shards, slice_len),
        )

    mixed_re, mixed_im = forward_outer(got_mixed)
    filt_re, filt_im = forward_outer(got_filt)
    mixed_re, mixed_im, filt_re, filt_im = (
        lax.all_to_all(
            lax.all_to_all(mixed_re, "grp", split_axis=1, concat_axis=1, tiled=True),
            "shard",
            split_axis=2,
            concat_axis=2,
            tiled=True,
        ),
        lax.all_to_all(
            lax.all_to_all(mixed_im, "grp", split_axis=1, concat_axis=1, tiled=True),
            "shard",
            split_axis=2,
            concat_axis=2,
            tiled=True,
        ),
        lax.all_to_all(
            lax.all_to_all(filt_re, "grp", split_axis=1, concat_axis=1, tiled=True),
            "shard",
            split_axis=2,
            concat_axis=2,
            tiled=True,
        ),
        lax.all_to_all(
            lax.all_to_all(filt_im, "grp", split_axis=1, concat_axis=1, tiled=True),
            "shard",
            split_axis=2,
            concat_axis=2,
            tiled=True,
        ),
    )
    row_ids = jnp.arange(positions, dtype=jnp.int32)
    inner = angles_of(row_ids[:, None], row_ids[None, :], positions)
    inner_cos, inner_sin = (jnp.cos(inner), jnp.sin(inner))

    def forward_inner(real, imag):
        real = real.reshape(2, positions, channels)
        imag = imag.reshape(2, positions, channels)
        out_re = jnp.einsum("kp,rpc->rkc", inner_cos, real, precision=precise) + jnp.einsum(
            "kp,rpc->rkc", inner_sin, imag, precision=precise
        )
        out_im = jnp.einsum("kp,rpc->rkc", inner_cos, imag, precision=precise) - jnp.einsum(
            "kp,rpc->rkc", inner_sin, real, precision=precise
        )
        return (out_re, out_im)

    spec_mixed_re, spec_mixed_im = forward_inner(mixed_re, mixed_im)
    spec_filt_re, spec_filt_im = forward_inner(filt_re, filt_im)
    prod_re = spec_mixed_re * spec_filt_re - spec_mixed_im * spec_filt_im
    prod_im = spec_mixed_re * spec_filt_im + spec_mixed_im * spec_filt_re
    back_re = jnp.einsum("kp,rkc->rpc", inner_cos, prod_re, precision=precise) - jnp.einsum(
        "kp,rkc->rpc", inner_sin, prod_im, precision=precise
    )
    back_im = jnp.einsum("kp,rkc->rpc", inner_cos, prod_im, precision=precise) + jnp.einsum(
        "kp,rkc->rpc", inner_sin, prod_re, precision=precise
    )
    own_freqs = jnp.arange(2, dtype=jnp.int32) * devices + device_id
    back_twist = angles_of(own_freqs[:, None], row_ids[None, :], length)
    back_cos, back_sin = (jnp.cos(back_twist)[:, :, None], jnp.sin(back_twist)[:, :, None])
    rot_re = (back_re * back_cos - back_im * back_sin).reshape(2, groups, shards, slice_len)
    rot_im = (back_re * back_sin + back_im * back_cos).reshape(2, groups, shards, slice_len)
    rot_re, rot_im = (
        lax.all_to_all(
            lax.all_to_all(rot_re, "grp", split_axis=1, concat_axis=1, tiled=True),
            "shard",
            split_axis=2,
            concat_axis=2,
            tiled=True,
        ),
        lax.all_to_all(
            lax.all_to_all(rot_im, "grp", split_axis=1, concat_axis=1, tiled=True),
            "shard",
            split_axis=2,
            concat_axis=2,
            tiled=True,
        ),
    )
    rot_re = rot_re.reshape(span_len, slice_len)
    rot_im = rot_im.reshape(span_len, slice_len)
    values = (
        jnp.einsum("kd,kf->df", outer_cos, rot_re, precision=precise)
        - jnp.einsum("kd,kf->df", outer_sin, rot_im, precision=precise)
    ) / length
    values = values.reshape(groups, shards, slice_len)
    conv_rows = lax.all_to_all(
        lax.all_to_all(values, "grp", split_axis=0, concat_axis=0, tiled=True),
        "shard",
        split_axis=1,
        concat_axis=1,
        tiled=True,
    )
    conv = conv_rows.reshape(positions, channels)
    return (query * (conv + skip_gain * mixed)).astype(jnp.bfloat16)


MESH = pl.DeviceIdType.MESH
LANES = 128
SUB = 8
HALO = 8
REACH = 250.0
FAINT = 1e-30
MIX = 3
EARLY = 2
RIMS = ((1, 2), (0, 0))


def turned(value, numerator, denominator):
    numerator %= denominator
    real, imag = value
    eighths, rest = divmod(8 * numerator, denominator)
    if rest == 0:
        half = math.sqrt(0.5)
        if eighths == 0:
            return (real, imag)
        if eighths == 2:
            return (-imag, real)
        if eighths == 4:
            return (-real, -imag)
        if eighths == 6:
            return (imag, -real)
        if eighths == 1:
            return ((real - imag) * half, (real + imag) * half)
        if eighths == 3:
            return ((real + imag) * -half, (real - imag) * half)
        if eighths == 5:
            return ((imag - real) * half, (real + imag) * -half)
        return ((real + imag) * half, (imag - real) * half)
    angle = 2.0 * math.pi * numerator / denominator
    cos, sin = (math.cos(angle), math.sin(angle))
    return (real * cos - imag * sin, real * sin + imag * cos)


def fft(loads, sign):
    count = len(loads)
    if count == 1:
        return [loads[0]()]
    even, odd = (fft(loads[::2], sign), fft(loads[1::2], sign))
    low, high = ([], [])
    for k in range(count // 2):
        moved = turned(odd[k], sign * k, count)
        low.append((even[k][0] + moved[0], even[k][1] + moved[1]))
        high.append((even[k][0] - moved[0], even[k][1] - moved[1]))
    return low + high


def dot3(values, table_hi, table_lo):
    hi = values.astype(jnp.bfloat16)
    lo = (values - hi.astype(jnp.float32)).astype(jnp.bfloat16)
    dot = functools.partial(jnp.dot, preferred_element_type=jnp.float32)
    return dot(hi, table_hi[...]) + (dot(lo, table_hi[...]) + dot(hi, table_lo[...]))


def encoded(scaled):
    magnitude = jnp.exp2(jnp.abs(scaled) - REACH / 2)
    return jnp.where(scaled < 0, -magnitude, magnitude)


def decoded(code):
    wide = code.astype(jnp.float32)
    magnitude = jnp.log2(jnp.abs(wide)) + REACH / 2
    return jnp.where(wide < 0, -magnitude, magnitude)


def owner_kernel(
    sizes,
    proj_ref_far,
    taps_ref_far,
    filt_ref_far,
    gain_ref_far,
    fwd_hi_far,
    fwd_lo_far,
    inv_hi_far,
    inv_lo_far,
    twist_cos_far,
    twist_sin_far,
    out_ref,
    proj_ref,
    taps_ref,
    filt_ref,
    gain_ref,
    fwd_hi,
    fwd_lo,
    inv_hi,
    inv_lo,
    twist_cos,
    twist_sin,
    rim_out,
    rim_in,
    ext,
    query,
    mixed,
    filt_out,
    mix_out,
    conv_out,
    filt_in,
    mix_in,
    conv_in,
    mix_top,
    mix_tops,
    conv_top,
    conv_tops,
    columns,
    blocks,
    spec_a,
    spec_held,
    spec_g,
    own_filt,
    own_mix,
    first_filt,
    first_mix,
    load_sems,
    rim_sems,
    send_sems,
    recv_sems,
    first_sems,
):
    groups, shards, positions, channels, taps = sizes
    devices = groups * shards
    owned = channels // devices
    halves = owned // SUB
    per_chunk = LANES // owned
    chunks = channels // LANES
    bound = 6.0 / math.sqrt(devices * positions)
    my_group, my_shard = (lax.axis_index("grp"), lax.axis_index("shard"))
    me = my_group * shards + my_shard
    first_lane = lax.rem(me, per_chunk) * owned

    def partners(act, aparts=()):
        for apart in aparts or range(devices - 1, 0, -1):
            group = jnp.bitwise_xor(my_group, apart // shards)
            shard = jnp.bitwise_xor(my_shard, apart % shards)
            act((group, shard), group * shards + shard)

    def place(target):
        return (target // shards, target % shards)

    barrier = pltpu.get_barrier_semaphore()
    partners(
        lambda there, target: pl.semaphore_signal(
            barrier, inc=1, device_id=there, device_id_type=MESH
        )
    )

    far = (filt_ref_far, proj_ref_far, taps_ref_far, gain_ref_far, fwd_hi_far, fwd_lo_far)
    far += (inv_hi_far, inv_lo_far, twist_cos_far, twist_sin_far)
    near = (filt_ref, proj_ref, taps_ref, gain_ref, fwd_hi, fwd_lo)
    near += (inv_hi, inv_lo, twist_cos, twist_sin)
    loads = [
        pltpu.make_async_copy(source_ref, here_ref, load_sems.at[which])
        for which, (source_ref, here_ref) in enumerate(zip(far, near))
    ]
    for load in loads:
        load.start()

    def spread(chunk, block, stores):
        turned_block = block.T
        rows = owned // len(stores)
        for part in range(per_chunk):
            for which, store in enumerate(stores):
                first = part * owned + which * rows
                piece = turned_block[first : first + rows, :]
                store[chunk * per_chunk + part] = piece.astype(jnp.bfloat16)

    loads[0].wait()
    for chunk in range(chunks):
        lanes = slice(chunk * LANES, (chunk + 1) * LANES)
        spread(chunk, encoded(filt_ref[:, lanes] * (REACH / bound)), [filt_out])
    loads[1].wait()
    last = slice(positions - 16, positions)
    for pair in range(2):
        tails = [
            proj_ref[which, last, :].astype(jnp.float32)[8:]
            for which in RIMS[pair]
        ]
        rim_out[pair] = jnp.concatenate(tails, axis=0).astype(jnp.bfloat16)
    pl.semaphore_wait(barrier, devices - 1)

    rim_copies = [
        pltpu.make_async_remote_copy(
            src_ref=rim_out.at[pair],
            dst_ref=rim_in.at[pair],
            send_sem=rim_sems.at[0, pair],
            recv_sem=rim_sems.at[1, pair],
            device_id=place(lax.rem(me + 1, devices)),
            device_id_type=MESH,
        )
        for pair in range(2)
    ]

    def send_all(kind, source, landing, index=lambda target: target, first=0, aparts=()):
        def send(there, target):
            copy = pltpu.make_async_remote_copy(
                src_ref=source.at[index(target)],
                dst_ref=landing.at[me],
                send_sem=send_sems.at[kind],
                recv_sem=recv_sems.at[kind],
                device_id=there,
                device_id_type=MESH,
            )
            if first:
                pl.when(target >= first)(copy.start)
            else:
                copy.start()

        partners(send, aparts)
        landing[me] = source[index(me)]

    def wait_all(kind, landing, sems, count=devices - 1):
        others = landing.at[pl.ds(0, count)]
        pltpu.make_async_copy(others, others, sems.at[kind]).wait()

    for rim_copy in rim_copies:
        rim_copy.start()
    send_all(0, filt_out, filt_in, aparts=[a for a in range(devices - 1, 0, -1) if a & (shards // 2)])

    for load in loads[2:]:
        load.wait()

    def shortened(which, chunk, begin, end):
        lanes = slice(chunk * LANES, (chunk + 1) * LANES)
        total = None
        for tap in range(taps):
            term = taps_ref[which, tap : tap + 1, lanes] * ext[
                which, chunk, HALO + begin - tap : HALO + end - tap, :
            ]
            total = term if total is None else total + term
        return total

    for chunk in range(chunks):
        lanes = slice(chunk * LANES, (chunk + 1) * LANES)
        for which in range(3):
            ext[which, chunk, HALO:, :] = proj_ref[which, :, lanes].astype(jnp.float32)
        mixed[chunk, HALO:, :] = shortened(1, chunk, HALO, positions) * shortened(
            2, chunk, HALO, positions
        )
    for rim_copy in rim_copies:
        rim_copy.wait()
    keep = jnp.where(me > 0, 1.0, 0.0).astype(jnp.float32)
    for chunk in range(chunks):
        lanes = slice(chunk * LANES, (chunk + 1) * LANES)
        for which in range(3):
            pair = 0 if which in RIMS[0] else 1
            part = RIMS[pair].index(which)
            tail = rim_in[pair, :, lanes].astype(jnp.float32)[part * 8 : part * 8 + 8]
            ext[which, chunk, HALO - 8 : HALO, :] = tail * keep
        mixed[chunk, :HALO, :] = shortened(1, chunk, 0, HALO) * shortened(2, chunk, 0, HALO)
        block = mixed[chunk]
        top = jnp.maximum(jnp.max(jnp.abs(block), axis=0, keepdims=True), FAINT)
        mix_top[chunk] = top * (1.0 / REACH)
        spread(chunk, encoded(block * (REACH / top)), [mix_out.at[half] for half in range(halves)])
    send_all(1, mix_top, mix_tops, lambda target: target // per_chunk)
    for half in range(halves):
        send_all(MIX + half, mix_out.at[half], mix_in.at[half])
        if half == 0:
            send_all(0, filt_out, filt_in, aparts=[a for a in range(devices - 1, 0, -1) if not a & (shards // 2)])

    for chunk in range(chunks):
        query[chunk] = shortened(0, chunk, 0, positions)

    @pl.when(me < EARLY)
    def _():
        for chunk in range(chunks):
            lanes = slice(chunk * LANES, (chunk + 1) * LANES)
            own_filt[lanes, :] = filt_ref[:, lanes].T
            own_mix[lanes, :] = mixed[chunk].T

    first_copies = [
        pltpu.make_async_remote_copy(
            src_ref=source,
            dst_ref=landing,
            send_sem=first_sems.at[0, which],
            recv_sem=first_sems.at[1, which],
            device_id=place(jnp.bitwise_xor(me, 1)),
            device_id_type=MESH,
        )
        for which, (source, landing) in enumerate(((own_filt, first_filt), (own_mix, first_mix)))
    ]

    @pl.when(me == 0)
    def _():
        for copy in first_copies:
            copy.start()

    for chunk in range(chunks):
        lanes = slice(chunk * LANES, (chunk + 1) * LANES)
        mixed[chunk] = mixed[chunk] * gain_ref[:, lanes]

    def transform(half, level):
        def load(block):
            def get():
                value = blocks[half, block]
                angle = 2.0 * math.pi * block / (4 * devices)
                return (value * (level * math.cos(angle)), value * (level * math.sin(angle)))

            return get

        for k, (real, imag) in enumerate(fft([load(b) for b in range(devices)], 1)):
            cos, sin = (twist_cos[k : k + 1, :], twist_sin[k : k + 1, :])
            rows = slice(k * SUB, (k + 1) * SUB)
            spec_a[rows, :LANES] = real * cos - imag * sin
            spec_a[rows, LANES:] = real * sin + imag * cos
        return dot3(spec_a[...], fwd_hi, fwd_lo)

    wait_all(0, filt_in, recv_sems)
    for block in range(devices):
        value = decoded(filt_in[block])
        for half in range(halves):
            blocks[half, block] = value[half * SUB : (half + 1) * SUB, :]
    for half in range(halves):
        spec_held[half] = transform(half, bound / REACH)

    wait_all(1, mix_tops, recv_sems)
    columns[...] = jnp.zeros_like(columns)
    columns[:devices, :] = mix_tops[:, 0, :]
    columns[...] = columns[...].T
    own_tops = columns[pl.ds(pl.multiple_of(first_lane, owned), owned), :]
    row = lax.broadcasted_iota(jnp.int32, (SUB, LANES), 0) + first_lane
    lane = lax.broadcasted_iota(jnp.int32, (SUB, LANES), 1)
    top_row = None
    for half in range(halves):
        wait_all(MIX + half, mix_in.at[half], recv_sems)
        for block in range(devices):
            top = own_tops[half * SUB : (half + 1) * SUB, block : block + 1]
            blocks[half, block] = decoded(mix_in[half, block]) * top
        far_spec = transform(half, 1.0)
        far_re, far_im = (far_spec[:, :LANES], far_spec[:, LANES:])
        held_re, held_im = (spec_held[half, :, :LANES], spec_held[half, :, LANES:])
        spec_a[:, :LANES] = far_re * held_re - far_im * held_im
        spec_a[:, LANES:] = far_re * held_im + far_im * held_re
        spec_g[...] = dot3(spec_a[...], inv_hi, inv_lo)

        def load(k):
            def get():
                rows = slice(k * SUB, (k + 1) * SUB)
                real, imag = (spec_g[rows, :LANES], spec_g[rows, LANES:])
                cos, sin = (twist_cos[k : k + 1, :], twist_sin[k : k + 1, :])
                return (real * cos + imag * sin, imag * cos - real * sin)

            return get

        top = None
        for block, (real, imag) in enumerate(fft([load(k) for k in range(devices)], -1)):
            angle = 2.0 * math.pi * block / (4 * devices)
            value = real * math.cos(angle) + imag * math.sin(angle)
            blocks[half, block] = value
            top = jnp.abs(value) if top is None else jnp.maximum(top, jnp.abs(value))
        top = jnp.maximum(jnp.max(top, axis=1, keepdims=True), FAINT)
        ratio = REACH / top
        for block in range(devices):
            conv_out[half, block] = encoded(blocks[half, block] * ratio).astype(jnp.bfloat16)
        here = jnp.where(row + half * SUB == lane, top * (1.0 / REACH), 0.0)
        here = jnp.sum(here, axis=0, keepdims=True)
        top_row = here if top_row is None else top_row + here
        if half == halves - 1:
            conv_top[0] = top_row
            send_all(2, conv_top, conv_tops, lambda target: 0, EARLY)
        send_all(MIX + halves + half, conv_out.at[half], conv_in.at[half], first=EARLY)

    def store(chunk, conv):
        lanes = slice(chunk * LANES, (chunk + 1) * LANES)
        out_ref[:, lanes] = (query[chunk] * (conv + mixed[chunk])).astype(out_ref.dtype)

    @pl.when(me >= EARLY)
    def _():
        for half in range(halves):
            wait_all(MIX + halves + half, conv_in.at[half], recv_sems)
            for block in range(devices):
                blocks[half, block] = decoded(conv_in[half, block])
        wait_all(2, conv_tops, recv_sems)
        for chunk in range(chunks):
            owners = slice(chunk * per_chunk, (chunk + 1) * per_chunk)
            top = jnp.sum(conv_tops[owners, 0, :], axis=0, keepdims=True)
            pieces = [
                blocks[half, chunk * per_chunk + part]
                for part in range(per_chunk)
                for half in range(halves)
            ]
            store(chunk, jnp.concatenate(pieces, axis=0).T * top)
        wait_all(2, conv_tops, send_sems, devices - 1 - EARLY)
        for half in range(halves):
            wait_all(MIX + halves + half, conv_in.at[half], send_sems, devices - 1 - EARLY)

    @pl.when(me == 0)
    def _():
        for copy in first_copies:
            copy.wait_send()
        first_filt[...] = own_filt[...]
        first_mix[...] = jnp.zeros_like(first_mix)

    @pl.when(me == 1)
    def _():
        for copy in first_copies:
            copy.wait_recv()

    @pl.when(me < EARLY)
    def _():
        cos, sin = (twist_cos[devices : devices + 1, :], twist_sin[devices : devices + 1, :])

        def spectrum(source, rows):
            value = source[rows, :]
            return dot3(jnp.concatenate([value * cos, value * sin], axis=1), fwd_hi, fwd_lo)

        def product(left, right):
            left_re, left_im = (left[:, :LANES], left[:, LANES:])
            right_re, right_im = (right[:, :LANES], right[:, LANES:])
            return (left_re * right_re - left_im * right_im, left_re * right_im + left_im * right_re)

        for chunk in range(chunks):
            rows = slice(chunk * LANES, (chunk + 1) * LANES)
            filt_here, mix_here = (spectrum(own_filt, rows), spectrum(own_mix, rows))
            filt_first, mix_first = (spectrum(first_filt, rows), spectrum(first_mix, rows))
            near_re, near_im = product(mix_here, filt_first)
            cross_re, cross_im = product(mix_first, filt_here)
            over_re, over_im = product(mix_first, filt_first)
            total = jnp.concatenate(
                [near_re + cross_re + over_im, near_im + cross_im - over_re], axis=1
            )
            back = dot3(total, inv_hi, inv_lo) * float(devices)
            store(chunk, (back[:, :LANES] * cos + back[:, LANES:] * sin).T)
        wait_all(2, conv_tops, send_sems, devices - EARLY)
        for half in range(halves):
            wait_all(MIX + halves + half, conv_in.at[half], send_sems, devices - EARLY)

    wait_all(0, filt_out, send_sems)
    wait_all(1, mix_tops, send_sems)
    for half in range(halves):
        wait_all(MIX + half, mix_out.at[half], send_sems)


def split_table(table):
    hi = table.astype(jnp.bfloat16)
    lo = (table - hi.astype(np.float64)).astype(jnp.bfloat16)
    return hi, lo


def tables(devices, positions):
    p = np.arange(positions, dtype=np.float64)
    angle = 2.0 * np.pi * ((p[:, None] * p[None, :]) % positions) / positions
    cos, sin = (np.cos(angle), np.sin(angle))
    forward = np.block([[cos, sin], [-sin, cos]])
    backward = np.block([[cos, -sin], [sin, cos]]) / (devices * positions)
    k = np.arange(devices, dtype=np.float64)
    turns = np.append(k + 0.25, 0.25 * devices)
    twist = 2.0 * np.pi * turns[:, None] * p[None, :] / (devices * positions)
    return (
        *split_table(forward),
        *split_table(backward),
        np.cos(twist).astype(np.float32),
        np.sin(twist).astype(np.float32),
    )


def owned_channels(consts, groups, shards, projections, short_taps, long_filter, skip_gain):
    _, positions, channels = projections.shape
    devices = groups * shards
    owned = channels // devices
    halves = owned // SUB
    chunks = channels // LANES
    sizes = (groups, shards, positions, channels, short_taps.shape[1])
    f32, bf16 = (jnp.float32, jnp.bfloat16)
    operands = (projections, short_taps, long_filter, skip_gain.reshape(1, channels), *consts)
    slabs = pltpu.VMEM((devices, owned, LANES), bf16)
    halved = pltpu.VMEM((halves, devices, SUB, LANES), bf16)
    vmem = pl.BlockSpec(memory_space=pltpu.VMEM)
    return pl.pallas_call(
        functools.partial(owner_kernel, sizes),
        out_shape=jax.ShapeDtypeStruct((positions, channels), bf16),
        in_specs=[pl.BlockSpec(memory_space=pl.ANY)] * (4 + len(consts)),
        out_specs=vmem,
        scratch_shapes=[
            *(pltpu.VMEM(operand.shape, operand.dtype) for operand in operands),
            pltpu.VMEM((2, 16, channels), bf16),
            pltpu.VMEM((2, 16, channels), bf16),
            pltpu.VMEM((3, chunks, HALO + positions, LANES), f32),
            pltpu.VMEM((chunks, positions, LANES), f32),
            pltpu.VMEM((chunks, positions, LANES), f32),
            slabs,
            halved,
            halved,
            slabs,
            halved,
            halved,
            pltpu.VMEM((chunks, 1, LANES), f32),
            pltpu.VMEM((devices, 1, LANES), f32),
            pltpu.VMEM((1, 1, LANES), f32),
            pltpu.VMEM((devices, 1, LANES), f32),
            pltpu.VMEM((LANES, LANES), f32),
            pltpu.VMEM((halves, devices, SUB, LANES), f32),
            pltpu.VMEM((devices * SUB, 2 * LANES), f32),
            pltpu.VMEM((halves, devices * SUB, 2 * LANES), f32),
            pltpu.VMEM((devices * SUB, 2 * LANES), f32),
            *(pltpu.VMEM((channels, LANES), f32) for _ in range(4)),
            pltpu.SemaphoreType.DMA((len(operands),)),
            pltpu.SemaphoreType.DMA((2, 2)),
            pltpu.SemaphoreType.DMA((MIX + 2 * halves,)),
            pltpu.SemaphoreType.DMA((MIX + 2 * halves,)),
            pltpu.SemaphoreType.DMA((2, 2)),
        ],
        compiler_params=pltpu.CompilerParams(collective_id=0, has_side_effects=True, vmem_limit_bytes=16*1024*1024),
    )(*(pltpu.with_memory_space_constraint(o, pltpu.HBM) for o in operands))


def on_device(groups, shards, projections, short_taps, long_filter, skip_gain):
    _, positions, channels = projections.shape
    devices = groups * shards
    fits = (
        positions == LANES
        and channels % LANES == 0
        and channels % (SUB * devices) == 0
        and LANES % (channels // devices) == 0
        and devices & (devices - 1) == 0
        and (channels // devices) % 16 == 0
        and EARLY < devices <= LANES
        and short_taps.shape[1] <= HALO + 1
    )
    if not fits:
        return per_device(projections, short_taps, long_filter, skip_gain)
    consts = tables(devices, positions)
    return owned_channels(consts, groups, shards, projections, short_taps, long_filter, skip_gain)


def solution(mesh):
    placed = (P(None, ("grp", "shard"), None), P(), P(("grp", "shard"), None), P())
    body = functools.partial(on_device, mesh.shape["grp"], mesh.shape["shard"])
    return jax.shard_map(
        body, mesh=mesh, in_specs=placed, out_specs=P(("grp", "shard"), None), check_vma=False
    )
```
